32 devices in a mesh: dp: 8 (over z, x), expert: 4 (over y, core).
Axes of the slice: x: 2, y: 2, z: 4, core: 2. Of those that a mesh axis runs over, the one named last changes fastest.
Arguments:
- tokens: bfloat16 [20480, 1024], P(('dp', 'expert')), may hold values from -6 to 6
- cotangent: bfloat16 [20480, 1024], P(('dp', 'expert')), may hold values from -6 to 6
- expert_ids: int32 [20480, 8], P(('dp', 'expert')), may hold values from 0 to 31, all different within a row; in each aligned block of 320 rows (0 to 319, 320 to 639, ...) at most 100 rows name the same one
- norm_attn: float32 [1024], replicated, may hold values from 0.5 to 1.5
- w_qkv: bfloat16 [1024, 2048], replicated, may hold values from -0.75 to 0.75
- w_out: bfloat16 [1024, 1024], replicated, may hold values from -0.8984375 to 0.8984375
- norm_moe: float32 [1024], replicated, may hold values from 0.5 to 1.5
- w_router: bfloat16 [1024, 32], replicated, may hold values from -0.095703125 to 0.095703125
- w_gate_up: bfloat16 [32, 1024, 1024], P('expert'), may hold values from -0.1875 to 0.1875
- w_down: bfloat16 [32, 512, 1024], P('expert'), may hold values from -5.375 to 5.375
Outputs:
- output: bfloat16 [20480, 1024], P(('dp', 'expert'))
- grad_tokens: bfloat16 [20480, 1024], P(('dp', 'expert'))
- grad_norm_attn: float32 [1024], replicated
- grad_qkv: float32 [1024, 2048], replicated
- grad_out: float32 [1024, 1024], replicated
- grad_norm_moe: float32 [1024], replicated
- grad_router: float32 [1024, 32], replicated
- grad_gate_up: float32 [32, 1024, 1024], P('expert', 'dp')
- grad_down: float32 [32, 512, 1024], P('expert', 'dp')
The draws below stay inside these ranges and needn't reach their ends.
Inputs may be any that keep to these rules, and one draw needn't show every extreme that they name: `expert_ids`: each row names 8 different experts. In each aligned block of 320 rows no expert is named by more than 100 rows, a bound that some block reaches.
All inputs are finite; a program needn't handle non-finite values.
Results may differ from the reference program's by a relative error of at most 0.018.
The reference program's roundings to bfloat16 on the way count: a program that leaves them out, or rounds other values in their place, can miss the bound.
Values may be sent and summed in bfloat16 or wider, within the bound.
No kernel may reach another device: no remote copies, remote signals or barrier semaphores. Data moves between devices by JAX's collectives and lax.ppermute only.
A program may use at most 320 MiB of HBM per device.

```python
import math
import jax
import jax.numpy as jnp
import numpy as np
from jax import lax

D = 1024
HEADS = 16
KV_HEADS = 8
HEAD_DIM = 64
FF = 512
EXPERTS = 32
TOP = 8
PROMPT_DEV = 64
MICRO = 2
TOK_DEV = 320
ROWS = 20480
CAP = 100
QKV = 2048
N_DP = 8
N_EXPERT = 4


def strengthened(values, stream_key, source, target, blocks, factor):
    owner, partner = [(jnp.arange(values.shape[position]) // (values.shape[position] // blocks)).reshape([-1 if axis == position else 1 for axis in range(values.ndim)]) for position in (source, target)]
    chosen = jax.random.permutation(stream_key, blocks)[partner]
    strong = (owner == chosen) | (owner == (partner + blocks // 2) % blocks)
    return jnp.where(strong, factor * values, values)


def block_levels(own_key, dims, cuts, low, top_value):
    def one(position, parts):
        heights = jax.random.uniform(jax.random.fold_in(jax.random.fold_in(own_key, 6), position), (parts,), jnp.float32, low / len(cuts), top_value / len(cuts))
        return jnp.repeat(jnp.exp(heights), dims[position] // parts).reshape((-1,) + (1,) * (len(dims) - position - 1))

    factor_of = one(*cuts[0])
    for cut in cuts[1:]:
        factor_of = factor_of * one(*cut)
    return factor_of


def deal_out(own_key, own, number, rows, count, top, bound, skew):
    order = jax.random.permutation(own_key, count)
    heavy_load, ordinary = portions_of(count, rows * top, bound, skew, True), portions_of(count, rows * top, bound, skew, False)
    places = jnp.arange(count)

    def named(tallies, turn):
        used = int((tallies > 0).sum())
        fixed = max(1, used // 4)
        shifted = fixed + (places - fixed + turn * (used - fixed)) % max(1, count - fixed)
        return jnp.zeros((count,), jnp.int32).at[order[jnp.where(places < fixed, places, shifted)]].set(jnp.asarray(tallies, jnp.int32))

    tallies = jnp.where(number % 4 == 0, named(heavy_load, number // 4), named(ordinary, number - number // 4 - 1))
    mixed = jax.random.permutation(jax.random.fold_in(own, 3), count)
    donor, sink = mixed[0:count // 2 * 2:2], mixed[1:count // 2 * 2:2]
    margin = jnp.minimum(tallies[donor] - 1, bound - tallies[sink]) // 2
    margin = jnp.where((donor == order[0]) | (sink == order[0]) | (tallies[sink] == 0), 0, jnp.maximum(margin, 0))
    shifted = jax.random.randint(jax.random.fold_in(own, 4), (count // 2,), 0, 1 << 20) % (margin + 1)
    tallies = tallies.at[donor].add(-shifted).at[sink].add(shifted)
    members = jnp.searchsorted(jnp.cumsum(tallies), jnp.arange(rows * top), side="right").astype(jnp.int32)
    table = members.reshape(top, rows).T
    table = table[jax.random.permutation(jax.random.fold_in(own, 1), rows)]
    turn = jax.random.randint(jax.random.fold_in(own, 2), (rows, 1), 0, top)
    return jnp.take_along_axis(table, (jnp.arange(top)[None, :] + turn) % top, axis=1)


def portions_of(count, total, limit, skew, full):
    loads = [(1 << 20) // math.isqrt(standing ** skew) + 1 for standing in range(1, count + 1)]
    largest = limit if full else min(limit, max(-(-total // count), total * loads[0] // sum(loads)))
    least = 1 if total - largest >= count - 1 else 0
    holding, rest = [largest] + [least] * (count - 1), total - largest - least * (count - 1)
    while rest > 0:
        movable = [i for i in range(1, count) if holding[i] < largest] or [i for i in range(1, count) if holding[i] < limit]
        mass, budget = sum([loads[i] for i in movable]), rest
        for i in movable:
            extra = min(limit - holding[i], max(1, budget * loads[i] // mass), rest)
            holding[i] = holding[i] + extra
            rest = rest - extra
    return np.array(holding)


def gaussian(rng, shape, scale, bound, cuts=(), held_as=jnp.bfloat16):
    level = block_levels(rng, shape, cuts, -0.22, 0.18) if cuts else 1.0
    values = jax.random.normal(rng, shape, jnp.float32) * scale * level
    return jnp.minimum(jnp.maximum(values, -bound), bound).astype(held_as)


def bell_draw_with(stream_key, shape, spread, reach, cuts, heavy, held_as=jnp.bfloat16):
    values = spread * jax.random.normal(stream_key, shape, jnp.float32)
    if cuts:
        values = values * block_levels(stream_key, shape, cuts, -0.22, 0.18)
    return jnp.clip(strengthened(values, jax.random.fold_in(stream_key, 3), *heavy), -reach, reach).astype(held_as)


def setup_inputs(seed: int = 0) -> dict:
    arg_keys = jax.random.split(jax.random.key(seed), 11)
    tokens = bell_draw_with(arg_keys[0], (ROWS, D), 1.0, 6.0, ((0, 32),), (0, 1, 32, 2.75))
    cotangent = gaussian(arg_keys[1], (ROWS, D), 1.0, 6.0, ((0, 32),))
    expert_ids_keys = jax.random.split(jax.random.fold_in(arg_keys[2], 1), ROWS // TOK_DEV)
    expert_ids_turns = jax.random.permutation(jax.random.fold_in(arg_keys[2], 3), ROWS // TOK_DEV)
    expert_ids = jax.vmap(lambda own, number: deal_out(jax.random.fold_in(arg_keys[2], 2), own, number, TOK_DEV, EXPERTS, TOP, CAP, 1))(expert_ids_keys, expert_ids_turns).reshape((ROWS, TOP))
    norm_attn = jnp.clip(1.0 + 0.1 * jax.random.normal(arg_keys[3], (D,), jnp.float32), 0.5, 1.5)
    w_qkv = gaussian(arg_keys[4], (D, QKV), 0.125, 0.75)
    w_out = gaussian(arg_keys[5], (D, D), 0.15, 0.8984375)
    norm_moe = jnp.clip(1.0 + 0.1 * jax.random.normal(arg_keys[6], (D,), jnp.float32), 0.5, 1.5)
    w_router = gaussian(arg_keys[7], (D, EXPERTS), 0.016, 0.095703125)
    w_gate_up = gaussian(arg_keys[8], (EXPERTS, D, 2 * FF), D ** -0.5, 0.1875, ((0, 4),))
    w_down = gaussian(arg_keys[9], (EXPERTS, FF, D), 0.9, 5.375, ((0, 4),))
    return {"tokens": tokens, "cotangent": cotangent, "expert_ids": expert_ids, "norm_attn": norm_attn, "w_qkv": w_qkv, "w_out": w_out, "norm_moe": norm_moe, "w_router": w_router, "w_gate_up": w_gate_up, "w_down": w_down}


@jax.custom_vjp
def low(v):
    return lax.optimization_barrier(v.astype(jnp.bfloat16)).astype(jnp.float32)

@jax.custom_vjp
def low_back(v):
    return v

def low_keep(v):
    return (low(v), None)

def low_pass(kept, grad):
    return (grad,)

def back_keep(v):
    return (v, None)

def back_low(kept, grad):
    return (low(grad),)
low.defvjp(low_keep, low_pass)
low_back.defvjp(back_keep, back_low)
epsilon = 1e-06
score_scale = 1.0 / 64.0
branch_scale = 0.22
highest = lax.Precision.HIGHEST

def product(left, right):
    return jnp.dot(left, right, precision=highest)

def normalize(values, gain_vec):
    return values * lax.rsqrt(lax.optimization_barrier(jnp.mean(values * values, axis=-1, keepdims=True)) + epsilon) * gain_vec

def rotary_tables(positions):
    half_dim = HEAD_DIM // 2
    inverse = 10000.0 ** (-2.0 * jnp.arange(half_dim, dtype=jnp.float32) / HEAD_DIM)
    angles = positions[:, None] * inverse[None, :]
    cosine = jnp.concatenate([jnp.cos(angles), jnp.cos(angles)], axis=-1)
    sine_table = jnp.concatenate([jnp.sin(angles), jnp.sin(angles)], axis=-1)
    return (cosine, sine_table)

def rotate(vectors, cosine, sine_table):
    half_dim = HEAD_DIM // 2
    turned = jnp.concatenate([-vectors[..., half_dim:], vectors[..., :half_dim]], axis=-1)
    return vectors * cosine[:, None, :] + turned * sine_table[:, None, :]

def slot_places(block_ids, member):
    flat_ids = block_ids.reshape(-1)
    one_hot = (flat_ids[:, None] == jnp.arange(EXPERTS, dtype=jnp.int32)[None, :]).astype(jnp.int32)
    slot_rank = lax.optimization_barrier(jnp.sum(jnp.cumsum(one_hot, axis=0) * one_hot, axis=1)) - 1
    return (flat_ids * N_EXPERT + member) * CAP + slot_rank

def device_attention(queries, prompt_keys, prompt_values, own_keys, own_values, positions):
    all_keys = jnp.concatenate([prompt_keys, own_keys], axis=0)
    all_values = jnp.concatenate([prompt_values, own_values], axis=0)
    key_count = all_keys.shape[0]
    allowed = jnp.arange(key_count, dtype=jnp.int32)[None, :] <= positions[:, None]
    grouped = queries.reshape(TOK_DEV, KV_HEADS, HEADS // KV_HEADS, HEAD_DIM)
    scores = jnp.einsum('qhgd,khd->hgqk', grouped, all_keys, precision=highest) * score_scale
    scores = low_back(scores)
    scores = jnp.where(allowed[None, None], scores, -1e+30)
    weights = low(jax.nn.softmax(scores, axis=-1))
    mixed_rows = jnp.einsum('hgqk,khd->qhgd', weights, all_values, precision=highest)
    return mixed_rows.reshape(TOK_DEV, HEADS * HEAD_DIM)

def group_forward(params, group_tokens, group_ids):
    norm_attn, w_qkv, w_out, norm_moe, w_router, w_gate_up, w_down = params
    member = jnp.arange(N_EXPERT, dtype=jnp.int32)
    local_index = jnp.arange(TOK_DEV, dtype=jnp.int32)
    prompt_len = PROMPT_DEV * N_EXPERT
    positions = jnp.where(local_index[None, :] < PROMPT_DEV, member[:, None] * PROMPT_DEV + local_index[None, :], prompt_len + local_index[None, :] - PROMPT_DEV)
    flat_tokens = group_tokens.reshape(N_EXPERT * TOK_DEV, D)
    normed = low(normalize(flat_tokens, norm_attn))
    projected = low_back(product(normed, w_qkv))
    query_width = HEADS * HEAD_DIM
    key_width = KV_HEADS * HEAD_DIM
    cosine, sine_table = rotary_tables(positions.reshape(-1).astype(jnp.float32))
    queries = low(rotate(projected[:, :query_width].reshape(-1, HEADS, HEAD_DIM), cosine, sine_table))
    key_rows = low(rotate(projected[:, query_width:query_width + key_width].reshape(-1, KV_HEADS, HEAD_DIM), cosine, sine_table))
    value_rows = low(projected[:, query_width + key_width:]).reshape(-1, KV_HEADS, HEAD_DIM)
    queries = queries.reshape(N_EXPERT, TOK_DEV, HEADS, HEAD_DIM)
    key_rows = key_rows.reshape(N_EXPERT, TOK_DEV, KV_HEADS, HEAD_DIM)
    value_rows = value_rows.reshape(N_EXPERT, TOK_DEV, KV_HEADS, HEAD_DIM)
    prompt_keys = key_rows[:, :PROMPT_DEV].reshape(prompt_len, KV_HEADS, HEAD_DIM)
    prompt_values = value_rows[:, :PROMPT_DEV].reshape(prompt_len, KV_HEADS, HEAD_DIM)

    def attend(pieces):
        return device_attention(pieces[0], prompt_keys, prompt_values, pieces[1], pieces[2], pieces[3])
    attended = lax.map(jax.checkpoint(attend), (queries, key_rows[:, PROMPT_DEV:], value_rows[:, PROMPT_DEV:], positions))
    attended = low(low_back(attended.reshape(-1, D)))
    hidden = flat_tokens + branch_scale * low_back(product(attended, w_out))
    normed_moe = low(normalize(hidden, norm_moe))
    logits = low_back(product(normed_moe, w_router))
    places = jax.vmap(slot_places)(group_ids, member).reshape(-1)
    routed = places.shape[0]
    slot_table = jnp.full((EXPERTS * N_EXPERT * CAP,), routed, dtype=jnp.int32).at[places].set(jnp.arange(routed, dtype=jnp.int32))
    padded = jnp.concatenate([normed_moe, jnp.zeros((1, D), jnp.float32)], axis=0)
    routed_rows = low_back(padded[slot_table // TOP]).reshape(EXPERTS, N_EXPERT * CAP, D)

    def expert_apply(pieces):
        rows_in, gate_up_w, down_w = pieces
        gate_up = low_back(product(rows_in, gate_up_w))
        middle = low(jax.nn.silu(gate_up[:, :FF]) * gate_up[:, FF:])
        return low(low_back(product(middle, down_w)))
    outputs = lax.map(jax.checkpoint(expert_apply), (routed_rows, w_gate_up, w_down)).reshape(-1, D)
    picked = outputs[places].reshape(N_EXPERT * TOK_DEV, TOP, D)
    chosen = jnp.take_along_axis(logits, group_ids.reshape(-1, TOP), axis=1)
    gate_weights = jax.nn.softmax(chosen, axis=-1)
    mixture = lax.optimization_barrier(jnp.sum(gate_weights[:, :, None] * picked, axis=1))
    return hidden + branch_scale * mixture

def to_groups(array):
    width = array.shape[-1]
    grouped = array.reshape(N_DP, N_EXPERT, MICRO, TOK_DEV, width).transpose(0, 2, 1, 3, 4)
    return grouped.reshape(N_DP * MICRO, N_EXPERT, TOK_DEV, width)

def from_groups(array):
    width = array.shape[-1]
    ungrouped = array.reshape(N_DP, MICRO, N_EXPERT, TOK_DEV, width).transpose(0, 2, 1, 3, 4)
    return ungrouped.reshape(ROWS, width)

def reference(tokens, cotangent, expert_ids, norm_attn, w_qkv, w_out, norm_moe, w_router, w_gate_up, w_down):
    params = (norm_attn.astype(jnp.float32), w_qkv.astype(jnp.float32), w_out.astype(jnp.float32), norm_moe.astype(jnp.float32), w_router.astype(jnp.float32), w_gate_up.astype(jnp.float32), w_down.astype(jnp.float32))
    group_tokens = to_groups(tokens.astype(jnp.float32))
    group_ids = to_groups(expert_ids)
    group_cot = to_groups(cotangent.astype(jnp.float32)).reshape(N_DP * MICRO, N_EXPERT * TOK_DEV, D)

    def forward(params_in, tokens_in):

        def group_step(pieces):
            return group_forward(params_in, pieces[0], pieces[1])
        return lax.map(jax.checkpoint(group_step), (tokens_in, group_ids))
    result, pullback = jax.vjp(forward, params, group_tokens)
    gradients, grad_inputs = pullback(group_cot)
    output = from_groups(result).astype(jnp.bfloat16)
    grad_tokens = from_groups(grad_inputs).astype(jnp.bfloat16)
    return (output, grad_tokens, gradients[0], gradients[1], gradients[2], gradients[3], gradients[4], gradients[5], gradients[6])
```

```python
import functools

import jax
import jax.numpy as jnp
from jax import lax
from jax.experimental import pallas as pl
from jax.experimental.pallas import tpu as pltpu
from jax.sharding import PartitionSpec as P

D = 1024
HEADS = 16
KV_HEADS = 8
HEAD_DIM = 64
FF = 512
EXPERTS = 32
TOP = 8
PROMPT_DEV = 64
MICRO = 2
CAP = 100
SLOTS = 112
CHUNKS = (2, 2, 2, 1, 1)


epsilon = 1e-06
score_scale = 1.0 / 64.0
branch_scale = 0.22
masked_score = -1e30

f32 = jnp.float32
bf16 = jnp.bfloat16
vmem_limit = 60 * 1024 * 1024


def params():
    return pltpu.CompilerParams(
        vmem_limit_bytes=vmem_limit, dimension_semantics=("arbitrary",)
    )


def mm(left, right, dims):
    return lax.dot_general(left, right, (dims, ((), ())), preferred_element_type=f32)


def fill_one_hot(slot_rows, onehot_ref):
    experts, rows = slot_rows.shape
    place = lax.broadcasted_iota(jnp.int32, (SLOTS, rows), 0)
    for e in range(experts):
        hit = place == slot_rows[e : e + 1, :]
        onehot_ref[e * SLOTS : (e + 1) * SLOTS, :] = jnp.where(hit, 1.0, 0.0).astype(bf16)


def chosen_of(ids, count):
    rows = ids.shape[1]
    label = lax.broadcasted_iota(jnp.int32, (count, rows), 0)
    hit = ids[0:1, :] == label
    for k in range(1, ids.shape[0]):
        hit = hit | (ids[k : k + 1, :] == label)
    return hit


def select_block(row_refs, rows_ref):
    b = pl.program_id(0)
    at = 0
    for ref in row_refs:
        for i in range(ref.shape[0]):

            @pl.when(b == at)
            def _(ref=ref, i=i):
                rows_ref[...] = ref[i]

            at += 1


def store_picked(onehot_ref, rows_ref, out_ref):
    picked = mm(onehot_ref[...], rows_ref[...], ((1,), (0,))).astype(bf16)
    for e in range(out_ref.shape[0]):
        out_ref[e, 0] = picked[e * SLOTS : (e + 1) * SLOTS]


def pick_grad_body(*refs, pieces):
    ids_ref = refs[0]
    row_refs = refs[1 : 1 + pieces]
    out_ref, slot_ref, onehot_ref, rows_ref, earlier_ref = refs[1 + pieces :]
    experts, rows = slot_ref.shape[1], slot_ref.shape[2]

    @pl.when(pl.program_id(0) == 0)
    def _():
        first = lax.broadcasted_iota(jnp.int32, (rows, rows), 0)
        second = lax.broadcasted_iota(jnp.int32, (rows, rows), 1)
        earlier_ref[...] = jnp.where(first < second, 1.0, 0.0).astype(bf16)

    select_block(row_refs, rows_ref)
    hit = chosen_of(ids_ref[0], 8)
    rank = mm(jnp.where(hit, 1.0, 0.0).astype(bf16), earlier_ref[...], ((1,), (0,)))
    slots = jnp.where(hit, rank, -1.0).astype(jnp.int32)[:experts]
    slot_ref[0] = slots
    fill_one_hot(slots, onehot_ref)
    store_picked(onehot_ref, rows_ref, out_ref)


def full_spec(array):
    zeros = (0,) * array.ndim
    return pl.BlockSpec(array.shape, lambda *_: zeros)


def pick_grads(ids, pieces, experts):
    blocks, top, tok = ids.shape
    return pl.pallas_call(
        functools.partial(pick_grad_body, pieces=len(pieces)),
        grid=(blocks,),
        in_specs=[pl.BlockSpec((1, top, tok), lambda b: (b, 0, 0))]
        + [full_spec(piece) for piece in pieces],
        out_specs=[
            pl.BlockSpec((experts, 1, SLOTS, D), lambda b: (0, b, 0, 0)),
            pl.BlockSpec((1, experts, tok), lambda b: (b, 0, 0)),
        ],
        out_shape=[
            jax.ShapeDtypeStruct((experts, blocks, SLOTS, D), bf16),
            jax.ShapeDtypeStruct((blocks, experts, tok), jnp.int32),
        ],
        scratch_shapes=[
            pltpu.VMEM((experts * SLOTS, tok), bf16),
            pltpu.VMEM((tok, D), bf16),
            pltpu.VMEM((tok, tok), bf16),
        ],
        compiler_params=params(),
    )(ids, *pieces)


def pick_token_body(*refs, pieces):
    ids_ref, slot_ref, router_ref = refs[:3]
    row_refs = refs[3 : 3 + pieces]
    out_ref, slot_gate_ref, gate_ref, onehot_ref, rows_ref = refs[3 + pieces :]
    experts, rows = slot_ref.shape[1], slot_ref.shape[2]
    select_block(row_refs, rows_ref)
    logits = mm(router_ref[...], rows_ref[...], ((0,), (1,)))
    hit = chosen_of(ids_ref[0], EXPERTS)
    masked = jnp.where(hit, logits, masked_score)
    raised = jnp.where(hit, jnp.exp(masked - jnp.max(masked, axis=0, keepdims=True)), 0.0)
    gates = raised / jnp.sum(raised, axis=0, keepdims=True)
    gate_ref[0] = gates
    fill_one_hot(slot_ref[0], onehot_ref)
    store_picked(onehot_ref, rows_ref, out_ref)
    place = lax.broadcasted_iota(jnp.int32, (SLOTS, rows), 0)
    for e in range(experts):
        here = place == slot_ref[0, e : e + 1, :]
        gate = jnp.sum(jnp.where(here, gates[e : e + 1, :], 0.0), axis=1, keepdims=True)
        slot_gate_ref[e, 0] = jnp.broadcast_to(gate, (SLOTS, 128))


def pick_tokens(ids, slots, w_router, pieces):
    blocks, experts, tok = slots.shape
    return pl.pallas_call(
        functools.partial(pick_token_body, pieces=len(pieces)),
        grid=(blocks,),
        in_specs=[
            pl.BlockSpec((1, ids.shape[1], tok), lambda b: (b, 0, 0)),
            pl.BlockSpec((1, experts, tok), lambda b: (b, 0, 0)),
            full_spec(w_router),
        ]
        + [full_spec(piece) for piece in pieces],
        out_specs=[
            pl.BlockSpec((experts, 1, SLOTS, D), lambda b: (0, b, 0, 0)),
            pl.BlockSpec((experts, 1, SLOTS, 128), lambda b: (0, b, 0, 0)),
            pl.BlockSpec((1, EXPERTS, tok), lambda b: (b, 0, 0)),
        ],
        out_shape=[
            jax.ShapeDtypeStruct((experts, blocks, SLOTS, D), bf16),
            jax.ShapeDtypeStruct((experts, blocks, SLOTS, 128), f32),
            jax.ShapeDtypeStruct((blocks, EXPERTS, tok), f32),
        ],
        scratch_shapes=[pltpu.VMEM((experts * SLOTS, tok), bf16), pltpu.VMEM((tok, D), bf16)],
        compiler_params=params(),
    )(ids, slots, w_router, *pieces)


def sum_rows_body(*refs, chunks, with_dots):
    slot_ref = refs[0]
    row_refs = refs[1 : 1 + chunks]
    refs = refs[1 + chunks :]
    if with_dots:
        dot_refs, refs = refs[:chunks], refs[chunks:]
        out_ref, back_ref, onehot_ref, flat_ref = refs
    else:
        out_ref, onehot_ref, flat_ref = refs
    fill_one_hot(slot_ref[0], onehot_ref)
    e = 0
    for ref in row_refs:
        for i in range(ref.shape[0]):
            flat_ref[e * SLOTS : (e + 1) * SLOTS, :] = ref[i, 0]
            e += 1
    out_ref[0] = mm(onehot_ref[...], flat_ref[...], ((0,), (0,))).astype(bf16)
    if with_dots:
        place = lax.broadcasted_iota(jnp.int32, (SLOTS, slot_ref.shape[2]), 0)
        e = 0
        for ref in dot_refs:
            for i in range(ref.shape[0]):
                hit = place == slot_ref[0, e : e + 1, :]
                back_ref[0, e : e + 1, :] = jnp.sum(
                    jnp.where(hit, ref[i, 0, :, 0:1], 0.0), axis=0, keepdims=True
                )
                e += 1


def sum_rows(slots, rows, dots=None):
    blocks, experts, tok = slots.shape

    def chunk_spec(chunk):
        return pl.BlockSpec((chunk.shape[0], 1) + chunk.shape[2:], lambda b: (0, b, 0, 0))

    in_specs = [pl.BlockSpec((1, experts, tok), lambda b: (b, 0, 0))]
    in_specs += [chunk_spec(chunk) for chunk in rows]
    args = [slots] + rows
    out_shape = [jax.ShapeDtypeStruct((blocks, tok, D), bf16)]
    out_specs = [pl.BlockSpec((1, tok, D), lambda b: (b, 0, 0))]
    if dots is not None:
        in_specs += [chunk_spec(chunk) for chunk in dots]
        args += dots
        out_shape.append(jax.ShapeDtypeStruct((blocks, experts, tok), f32))
        out_specs.append(pl.BlockSpec((1, experts, tok), lambda b: (b, 0, 0)))
    return pl.pallas_call(
        functools.partial(sum_rows_body, chunks=len(rows), with_dots=dots is not None),
        grid=(blocks,),
        in_specs=in_specs,
        out_specs=out_specs,
        out_shape=out_shape,
        scratch_shapes=[
            pltpu.VMEM((experts * SLOTS, tok), bf16),
            pltpu.VMEM((experts * SLOTS, D), bf16),
        ],
        compiler_params=params(),
    )(*args)


def expert_body(
    parity_ref,
    x_ref,
    d_ref,
    gate_ref,
    wgu_ref,
    wd_ref,
    out_ref,
    back_ref,
    dots_ref,
    *part_refs,
    tile,
):
    mid_ref, grad_ref, act_ref, gu_ref, down_ref = part_refs[-5:]
    part_refs = part_refs[:-5]
    rows = x_ref.shape[1]

    def step(i, carry):
        span = pl.ds(pl.multiple_of(i * tile, tile), tile)
        hidden = mm(x_ref[0, span, :], wgu_ref[0], ((1,), (0,)))
        gate, up = hidden[:, :FF], hidden[:, FF:]
        sig = 1.0 / (1.0 + jnp.exp(-gate))
        silu = gate * sig
        middle = (silu * up).astype(bf16)
        mid_ref[span, :] = middle
        out = mm(middle, wd_ref[0], ((1,), (0,))).astype(bf16).astype(f32)
        weight = gate_ref[0, span, 0:1]
        scaled = branch_scale * d_ref[0, span, :].astype(f32)
        dots_ref[0, span, :] = jnp.broadcast_to(
            jnp.sum(scaled * out, axis=1, keepdims=True), (tile, 128)
        )
        out_ref[0, span, :] = (weight * out).astype(bf16)
        grad = (weight * scaled).astype(bf16)
        grad_ref[span, :] = grad
        grad_mid = mm(grad, wd_ref[0], ((1,), (1,)))
        act_ref[span, :FF] = (grad_mid * up * sig * (1.0 + gate * (1.0 - sig))).astype(bf16)
        act_ref[span, FF:] = (grad_mid * silu).astype(bf16)
        back_ref[0, span, :] = mm(act_ref[span, :], wgu_ref[0], ((1,), (1,))).astype(bf16)
        return carry

    lax.fori_loop(0, rows // tile, step, 0)
    gu_ref[...] = mm(x_ref[0], act_ref[...], ((0,), (0,))).astype(bf16)
    down_ref[...] = mm(mid_ref[...], grad_ref[...], ((0,), (0,))).astype(bf16)
    parity = parity_ref[0]
    pairs = part_refs[0].shape[1]
    half = (gu_ref.shape[0] + down_ref.shape[0]) // (2 * pairs)
    keep_ref, send_ref = part_refs[0], part_refs[-1]
    shift = half if len(part_refs) == 1 else 0
    start = 0
    for full in (gu_ref, down_ref):
        piece = full.shape[0] // (2 * pairs)
        for j in range(pairs):
            mine = pl.multiple_of((2 * j + parity) * piece, piece)
            other = pl.multiple_of((2 * j + 1 - parity) * piece, piece)
            keep_ref[0, j, start : start + piece, :] = full[pl.ds(mine, piece), :]
            send_ref[0, j, shift + start : shift + start + piece, :] = full[pl.ds(other, piece), :]
        start += piece


def expert_chunk(parity, first, count, pairs, split, x_rows, d_rows, slot_gate, w_gate_up, w_down):
    rows = x_rows.shape[1]
    tile = 2 * SLOTS
    mode = pl.Buffered(1 if rows > 1024 else 2)
    row_spec = pl.BlockSpec((1, rows, D), lambda e, p: (e + first, 0, 0), pipeline_mode=mode)
    col_spec = pl.BlockSpec((1, rows, 128), lambda e, p: (e + first, 0, 0))
    parts = 2 if split else 1
    piece = (D + FF) // (parts * pairs)
    part_spec = pl.BlockSpec((1, pairs, piece, D), lambda e, p: (e, 0, 0, 0))
    part_shape = jax.ShapeDtypeStruct((count, pairs, piece, D), bf16)
    out_row = pl.BlockSpec((1, rows, D), lambda e, p: (e, 0, 0))
    grid_spec = pltpu.PrefetchScalarGridSpec(
        num_scalar_prefetch=1,
        grid=(count,),
        in_specs=[
            row_spec,
            row_spec,
            col_spec,
            pl.BlockSpec((1, D, 2 * FF), lambda e, p: (e + first, 0, 0)),
            pl.BlockSpec((1, FF, D), lambda e, p: (e + first, 0, 0)),
        ],
        out_specs=[
            out_row,
            out_row,
            pl.BlockSpec((1, rows, 128), lambda e, p: (e, 0, 0)),
        ]
        + [part_spec] * parts,
        scratch_shapes=[
            pltpu.VMEM((rows, FF), bf16),
            pltpu.VMEM((rows, D), bf16),
            pltpu.VMEM((rows, 2 * FF), bf16),
            pltpu.VMEM((D, 2 * FF), bf16),
            pltpu.VMEM((FF, D), bf16),
        ],
    )
    return pl.pallas_call(
        functools.partial(expert_body, tile=tile),
        grid_spec=grid_spec,
        out_shape=[
            jax.ShapeDtypeStruct((count, rows, D), bf16),
            jax.ShapeDtypeStruct((count, rows, D), bf16),
            jax.ShapeDtypeStruct((count, rows, 128), f32),
        ]
        + [part_shape] * parts,
        compiler_params=params(),
    )(parity, x_rows, d_rows, slot_gate, w_gate_up, w_down)


def core_swap(value, groups):
    return lax.ppermute(value, "expert", [(m, m ^ 1) for m in range(groups)])


def from_row(value, groups, shift):
    count = groups // 2
    pairs = [((((y + shift) % count) * 2 + c), y * 2 + c) for y in range(count) for c in range(2)]
    return lax.ppermute(value, "expert", pairs)


def to_row(value, groups, shift):
    count = groups // 2
    pairs = [(y * 2 + c, ((y + shift) % count) * 2 + c) for y in range(count) for c in range(2)]
    return lax.ppermute(value, "expert", pairs)


def gather_members(value, groups):
    column = [value] + [from_row(value, groups, s) for s in range(1, groups // 2)]
    result = []
    for piece in column:
        result += [piece, core_swap(piece, groups)]
    return result


def return_members(pieces, groups):
    swapped = [core_swap(pieces[2 * s + 1], groups) for s in range(groups // 2)]
    terms = [pieces[0], swapped[0]]
    for s in range(1, groups // 2):
        both = (pieces[2 * s].astype(f32) + swapped[s].astype(f32)).astype(bf16)
        terms.append(to_row(both, groups, s))
    return terms


def exchange_members(pieces, groups):
    count = groups // 2
    result = []
    for s in range(count):
        for c in range(2):
            if s == 0 and c == 0:
                result.append(pieces[0])
                continue
            pairs = [
                (((y - s) % count) * 2 + (core ^ c), y * 2 + core)
                for y in range(count)
                for core in range(2)
            ]
            result.append(lax.ppermute(pieces[2 * s + c], "expert", pairs))
    return result


def lane(shape):
    return lax.broadcasted_iota(jnp.int32, shape, len(shape) - 1)


def turn(value, cosine, sine, sign):
    first = lax.rem(lane(value.shape), HEAD_DIM) < HEAD_DIM // 2
    other = jnp.where(
        first, pltpu.roll(value, 128 - HEAD_DIM // 2, 1), pltpu.roll(value, HEAD_DIM // 2, 1)
    )
    return value * cosine + sign * other * sine


def project_body(x_ref, gain_ref, w_ref, cos_ref, sin_ref, normed_ref, q_ref, kv_ref):
    x = x_ref[0].astype(f32)
    scale = lax.rsqrt(jnp.mean(x * x, axis=1, keepdims=True) + epsilon)
    normed = (x * scale * gain_ref[...]).astype(bf16)
    normed_ref[0] = normed
    cosine, sine = cos_ref[...], sin_ref[...]
    q_width, k_width = HEADS * HEAD_DIM, KV_HEADS * HEAD_DIM
    for start in range(0, q_width + 2 * k_width, 512):
        part = mm(normed, w_ref[:, start : start + 512], ((1,), (0,)))
        for inner in range(0, 512, 128):
            at = start + inner
            value = part[:, inner : inner + 128]
            if at < q_width:
                q_ref[0, :, at : at + 128] = turn(value, cosine, sine, 1.0).astype(bf16)
            elif at < q_width + k_width:
                at -= q_width
                kv_ref[0, :, at : at + 128] = turn(value, cosine, sine, 1.0).astype(bf16)
            else:
                at -= q_width
                kv_ref[0, :, at : at + 128] = value.astype(bf16)


def project(tokens, gain, w_qkv, cosine, sine):
    micro, rows, _ = tokens.shape
    block = pl.BlockSpec((1, rows, D), lambda m: (m, 0, 0))
    table = pl.BlockSpec((rows, 128), lambda m: (0, 0))
    shape = jax.ShapeDtypeStruct((micro, rows, D), bf16)
    return pl.pallas_call(
        project_body,
        grid=(micro,),
        in_specs=[
            block,
            pl.BlockSpec((1, D), lambda m: (0, 0)),
            pl.BlockSpec(w_qkv.shape, lambda m: (0, 0)),
            table,
            table,
        ],
        out_specs=[block, block, block],
        out_shape=[shape, shape, shape],
        compiler_params=params(),
    )(tokens, gain, w_qkv, cosine, sine)


def stack_heads(block, scale):
    wide = block.astype(f32) * scale
    result = []
    for p in range(2):
        part = wide[:, p * 128 : (p + 1) * 128]
        half = (lane(part.shape) >= HEAD_DIM) == (p == 1)
        for h in range(2):
            moved = part if h == p else pltpu.roll(part, HEAD_DIM, 1)
            result.append(jnp.where(half, moved, 0.0).astype(bf16))
    return jnp.concatenate(result, axis=0)


def unstack_heads(stacked, rows):
    result = []
    for p in range(2):
        pieces = []
        for h in range(2):
            i = 2 * p + h
            part = stacked[i * rows : (i + 1) * rows]
            pieces.append(part if h == p else pltpu.roll(part, HEAD_DIM, 1))
        result.append(jnp.where(lane(pieces[0].shape) < HEAD_DIM, pieces[0], pieces[1]))
    return result


def attend_body(
    q_ref, pk_ref, pv_ref, ok_ref, ov_ref, bias_ref, x_ref, w_ref, gain_ref,
    att_ref, lse_ref, hidden_ref, low_ref, all_ref,
):
    j = pl.program_id(0)
    rows = q_ref.shape[1]
    q = stack_heads(q_ref[0], score_scale)
    k = jnp.concatenate([pk_ref[0], ok_ref[0, PROMPT_DEV:, :]], axis=0)
    v = jnp.concatenate([pv_ref[0], ov_ref[0, PROMPT_DEV:, :]], axis=0)
    scores = mm(k, q, ((1,), (1,))) + bias_ref[...]
    largest = jnp.max(scores, axis=0, keepdims=True)
    raised = jnp.exp(scores - largest)
    total = jnp.sum(raised, axis=0, keepdims=True)
    weights = (raised * (1.0 / total)).astype(bf16)
    lse_ref[0] = largest + jnp.log(total)
    mixed = mm(v, weights, ((0,), (0,))).T
    for p, part in enumerate(unstack_heads(mixed, rows)):
        at = pl.multiple_of(j * 256 + p * 128, 128)
        att_ref[0, :, p * 128 : (p + 1) * 128] = part.astype(bf16)
        all_ref[:, pl.ds(at, 128)] = part.astype(bf16)

    @pl.when(j == pl.num_programs(0) - 1)
    def _():
        branch = mm(all_ref[...], w_ref[...], ((1,), (0,)))
        hidden = x_ref[0].astype(f32) + branch_scale * branch
        hidden_ref[0] = hidden
        scale = lax.rsqrt(jnp.mean(hidden * hidden, axis=1, keepdims=True) + epsilon)
        low_ref[0] = (hidden * scale * gain_ref[...]).astype(bf16)


def attend(micro, q, kv, prompt, bias, tokens, w_out, gain):
    rows, prompt_rows = q.shape[1], prompt.shape[1]
    steps = KV_HEADS // 2
    full = pl.BlockSpec((1, rows, D), lambda j: (micro, 0, 0))
    one = pl.BlockSpec((1, rows, D), lambda j: (0, 0, 0))
    return pl.pallas_call(
        attend_body,
        grid=(steps,),
        in_specs=[
            pl.BlockSpec((1, rows, 256), lambda j: (micro, 0, j)),
            pl.BlockSpec((1, prompt_rows, 128), lambda j: (micro, 0, j)),
            pl.BlockSpec((1, prompt_rows, 128), lambda j: (micro, 0, j + steps)),
            pl.BlockSpec((1, rows, 128), lambda j: (micro, 0, j)),
            pl.BlockSpec((1, rows, 128), lambda j: (micro, 0, j + steps)),
            pl.BlockSpec(bias.shape, lambda j: (0, 0)),
            full,
            pl.BlockSpec(w_out.shape, lambda j: (0, 0)),
            pl.BlockSpec((1, D), lambda j: (0, 0)),
        ],
        out_specs=[
            pl.BlockSpec((1, rows, 256), lambda j: (0, 0, j)),
            pl.BlockSpec((1, 1, 4 * rows), lambda j: (j, 0, 0)),
            one,
            one,
        ],
        out_shape=[
            jax.ShapeDtypeStruct((1, rows, D), bf16),
            jax.ShapeDtypeStruct((steps, 1, 4 * rows), f32),
            jax.ShapeDtypeStruct((1, rows, D), f32),
            jax.ShapeDtypeStruct((1, rows, D), bf16),
        ],
        scratch_shapes=[pltpu.VMEM((rows, D), bf16)],
        compiler_params=params(),
    )(q, prompt, prompt, kv, kv, bias, tokens, w_out, gain)


def norm_back(value, gain, grad):
    scale = lax.rsqrt(jnp.mean(value * value, axis=1, keepdims=True) + epsilon)
    scaled = grad * gain
    inner = jnp.mean(scaled * value, axis=1, keepdims=True)
    back = scale * scaled - value * (scale * scale * scale * inner)
    return back, jnp.sum(grad * value * scale, axis=0, keepdims=True)


def middle_body(*refs, terms):
    term_refs = refs[:terms]
    (logit_ref, router_ref, hidden_ref, gain_ref, cot_ref, w_ref) = refs[terms : terms + 6]
    grad_hidden_ref, branch_ref, att_ref, gain_out_ref = refs[terms + 6 :]
    total = mm(logit_ref[0], router_ref[...], ((0,), (1,)))
    for ref in term_refs:
        total = total + ref[0].astype(f32)
    back, gain_grad = norm_back(hidden_ref[0], gain_ref[...], total)
    grad_hidden = cot_ref[0].astype(f32) + back
    grad_hidden_ref[0] = grad_hidden
    branch = (branch_scale * grad_hidden).astype(bf16)
    branch_ref[0] = branch
    att_ref[0] = mm(branch, w_ref[...], ((1,), (1,))).astype(bf16)

    @pl.when(pl.program_id(0) == 0)
    def _():
        gain_out_ref[...] = gain_grad

    @pl.when(pl.program_id(0) != 0)
    def _():
        gain_out_ref[...] += gain_grad


def middle_back(terms, grad_logits, w_router, hidden, gain, cotangent, w_out):
    micro, rows, _ = hidden.shape
    block = pl.BlockSpec((1, rows, D), lambda m: (m, 0, 0))
    row = pl.BlockSpec((1, D), lambda m: (0, 0))
    return pl.pallas_call(
        functools.partial(middle_body, terms=len(terms)),
        grid=(micro,),
        in_specs=[block] * len(terms)
        + [
            pl.BlockSpec((1, EXPERTS, rows), lambda m: (m, 0, 0)),
            pl.BlockSpec(w_router.shape, lambda m: (0, 0)),
            block,
            row,
            block,
            pl.BlockSpec(w_out.shape, lambda m: (0, 0)),
        ],
        out_specs=[block, block, block, row],
        out_shape=[
            jax.ShapeDtypeStruct((micro, rows, D), f32),
            jax.ShapeDtypeStruct((micro, rows, D), bf16),
            jax.ShapeDtypeStruct((micro, rows, D), bf16),
            jax.ShapeDtypeStruct((1, D), f32),
        ],
        compiler_params=params(),
    )(*terms, grad_logits, w_router, hidden, gain, cotangent, w_out)


def attend_back_body(
    q_ref, pk_ref, pv_ref, ok_ref, ov_ref, bias_ref, lse_ref, grad_ref, cos_ref, sin_ref,
    gq_ref, gpk_ref, gpv_ref, gok_ref, gov_ref,
):
    rows, prompt_rows = q_ref.shape[1], pk_ref.shape[1]
    q = stack_heads(q_ref[0], score_scale)
    grad = stack_heads(grad_ref[0], 1.0)
    k = jnp.concatenate([pk_ref[0], ok_ref[0, PROMPT_DEV:, :]], axis=0)
    v = jnp.concatenate([pv_ref[0], ov_ref[0, PROMPT_DEV:, :]], axis=0)
    probs = jnp.exp(mm(k, q, ((1,), (1,))) + bias_ref[...] - lse_ref[0, 0])
    grad_probs = mm(v, grad, ((1,), (1,)))
    centre = jnp.sum(probs * grad_probs, axis=0, keepdims=True)
    grad_scores = (probs * (grad_probs - centre)).astype(bf16)
    grad_v = mm(probs.astype(bf16), grad, ((1,), (0,)))
    grad_k = mm(grad_scores, q, ((1,), (0,)))
    grad_q = mm(k, grad_scores, ((0,), (0,))).T * score_scale
    cosine, sine = cos_ref[...], sin_ref[...]
    for p, part in enumerate(unstack_heads(grad_q, rows)):
        gq_ref[0, :, p * 128 : (p + 1) * 128] = turn(part, cosine, sine, -1.0).astype(bf16)
    gpk_ref[0] = grad_k[:prompt_rows].astype(bf16)
    gpv_ref[0] = grad_v[:prompt_rows].astype(bf16)
    gok_ref[0] = turn(
        grad_k[prompt_rows:], cosine[PROMPT_DEV:], sine[PROMPT_DEV:], -1.0
    ).astype(bf16)
    gov_ref[0] = grad_v[prompt_rows:].astype(bf16)


def attend_back(q, kv, prompt, bias, lse, grad, cosine, sine):
    micro, rows, _ = q.shape
    prompt_rows = prompt.shape[1]
    own_rows = rows - PROMPT_DEV
    steps = KV_HEADS // 2
    wide = pl.BlockSpec((1, rows, 256), lambda m, j: (m, 0, j))
    table = pl.BlockSpec((rows, 128), lambda m, j: (0, 0))
    prompt_spec = pl.BlockSpec((1, prompt_rows, 128), lambda m, j: (m, 0, j))
    own_spec = pl.BlockSpec((1, own_rows, 128), lambda m, j: (m, 0, j))
    k_width = KV_HEADS * HEAD_DIM
    return pl.pallas_call(
        attend_back_body,
        grid=(micro, steps),
        in_specs=[
            wide,
            prompt_spec,
            pl.BlockSpec((1, prompt_rows, 128), lambda m, j: (m, 0, j + steps)),
            pl.BlockSpec((1, rows, 128), lambda m, j: (m, 0, j)),
            pl.BlockSpec((1, rows, 128), lambda m, j: (m, 0, j + steps)),
            pl.BlockSpec(bias.shape, lambda m, j: (0, 0)),
            pl.BlockSpec((1, 1, 1, 4 * rows), lambda m, j: (m, j, 0, 0)),
            wide,
            table,
            table,
        ],
        out_specs=[wide, prompt_spec, prompt_spec, own_spec, own_spec],
        out_shape=[
            jax.ShapeDtypeStruct((micro, rows, D), bf16),
            jax.ShapeDtypeStruct((micro, prompt_rows, k_width), bf16),
            jax.ShapeDtypeStruct((micro, prompt_rows, k_width), bf16),
            jax.ShapeDtypeStruct((micro, own_rows, k_width), bf16),
            jax.ShapeDtypeStruct((micro, own_rows, k_width), bf16),
        ],
        compiler_params=pltpu.CompilerParams(
            vmem_limit_bytes=vmem_limit, dimension_semantics=("arbitrary", "arbitrary")
        ),
    )(q, prompt, prompt, kv, kv, bias, lse, grad, cosine, sine)


def weight_body(*refs, terms):
    normed_ref, gq_ref, gok_ref, gov_ref = refs[:4]
    k_terms, v_terms = refs[4 : 4 + terms], refs[4 + terms : 4 + 2 * terms]
    cos_ref, sin_ref, gp_ref, out_ref, acc_ref = refs[4 + 2 * terms :]
    q_width, k_width = HEADS * HEAD_DIM, KV_HEADS * HEAD_DIM
    gp_ref[0, :, :q_width] = gq_ref[0]
    gp_ref[0, PROMPT_DEV:, q_width : q_width + k_width] = gok_ref[0]
    gp_ref[0, PROMPT_DEV:, q_width + k_width :] = gov_ref[0]
    prompt_k, prompt_v = [sum(ref[0].astype(f32) for ref in group) for group in (k_terms, v_terms)]
    cosine, sine = cos_ref[:PROMPT_DEV, :], sin_ref[:PROMPT_DEV, :]
    for at in range(0, k_width, 128):
        turned = turn(prompt_k[:, at : at + 128], cosine, sine, -1.0)
        gp_ref[0, :PROMPT_DEV, q_width + at : q_width + at + 128] = turned.astype(bf16)
    gp_ref[0, :PROMPT_DEV, q_width + k_width :] = prompt_v.astype(bf16)
    part = mm(normed_ref[0], gp_ref[0], ((0,), (0,)))
    m = pl.program_id(0)

    @pl.when(m == 0)
    def _():
        acc_ref[...] = part

    @pl.when(m != 0)
    def _():
        acc_ref[...] += part

    @pl.when(m == pl.num_programs(0) - 1)
    def _():
        out_ref[...] = acc_ref[...].astype(bf16)


def weight_back(normed, gq, gok, gov, k_terms, v_terms, cosine, sine):
    micro, rows, _ = normed.shape
    k_width = KV_HEADS * HEAD_DIM
    wide = pl.BlockSpec((1, rows, D), lambda m: (m, 0, 0))
    own = pl.BlockSpec((1, rows - PROMPT_DEV, k_width), lambda m: (m, 0, 0))
    term = pl.BlockSpec((1, PROMPT_DEV, k_width), lambda m: (m, 0, 0))
    table = pl.BlockSpec((rows, 128), lambda m: (0, 0))
    return pl.pallas_call(
        functools.partial(weight_body, terms=len(k_terms)),
        grid=(micro,),
        in_specs=[wide, wide, own, own] + [term] * (2 * len(k_terms)) + [table, table],
        out_specs=[
            pl.BlockSpec((1, rows, 2 * D), lambda m: (m, 0, 0)),
            pl.BlockSpec((D, 2 * D), lambda m: (0, 0)),
        ],
        out_shape=[
            jax.ShapeDtypeStruct((micro, rows, 2 * D), bf16),
            jax.ShapeDtypeStruct((D, 2 * D), bf16),
        ],
        scratch_shapes=[pltpu.VMEM((D, 2 * D), f32)],
        compiler_params=params(),
    )(normed, gq, gok, gov, *k_terms, *v_terms, cosine, sine)


def token_body(gp_ref, w_ref, x_ref, gain_ref, hidden_ref, out_ref, gain_out_ref):
    grad = mm(gp_ref[0], w_ref[...], ((1,), (1,)))
    back, gain_grad = norm_back(x_ref[0].astype(f32), gain_ref[...], grad)
    out_ref[0] = (hidden_ref[0] + back).astype(bf16)

    @pl.when(pl.program_id(0) == 0)
    def _():
        gain_out_ref[...] = gain_grad

    @pl.when(pl.program_id(0) != 0)
    def _():
        gain_out_ref[...] += gain_grad


def token_back(gp, w_qkv, tokens, gain, grad_hidden):
    micro, rows, _ = tokens.shape
    block = pl.BlockSpec((1, rows, D), lambda m: (m, 0, 0))
    row = pl.BlockSpec((1, D), lambda m: (0, 0))
    return pl.pallas_call(
        token_body,
        grid=(micro,),
        in_specs=[
            pl.BlockSpec((1, rows, 2 * D), lambda m: (m, 0, 0)),
            pl.BlockSpec(w_qkv.shape, lambda m: (0, 0)),
            block,
            row,
            block,
        ],
        out_specs=[block, row],
        out_shape=[
            jax.ShapeDtypeStruct((micro, rows, D), bf16),
            jax.ShapeDtypeStruct((1, D), f32),
        ],
        compiler_params=params(),
    )(gp, w_qkv, tokens, gain, grad_hidden)


def after(value, *others):
    return lax.optimization_barrier((value,) + others)[0]


def local(
    tokens, cotangent, expert_ids, norm_attn, w_qkv, w_out, norm_moe, w_router, w_gate_up, w_down
):
    groups = lax.axis_size("expert")
    dp_size = lax.axis_size("dp")
    member = lax.axis_index("expert")
    dp_index = lax.axis_index("dp")
    rows_all = tokens.shape[0]
    tok_rows = rows_all // MICRO
    local_experts = w_gate_up.shape[0]
    prompt_len = PROMPT_DEV * groups
    k_width = KV_HEADS * HEAD_DIM
    pairs = dp_size // 2
    blocks = groups * MICRO
    attn_gain = norm_attn.reshape(1, D)
    moe_gain = norm_moe.reshape(1, D)
    token_rows = tokens.reshape(MICRO, tok_rows, D)
    cot_rows = cotangent.reshape(MICRO, tok_rows, D)

    local_index = jnp.arange(tok_rows, dtype=jnp.int32)
    positions = jnp.where(
        local_index < PROMPT_DEV,
        member * PROMPT_DEV + local_index,
        prompt_len + local_index - PROMPT_DEV,
    )
    half_dim = HEAD_DIM // 2
    inverse = 10000.0 ** (-2.0 * jnp.arange(half_dim, dtype=f32) / HEAD_DIM)
    angles = positions.astype(f32)[:, None] * inverse[None, :]
    cosine = jnp.tile(jnp.cos(angles), (1, 128 // half_dim))
    sine = jnp.tile(jnp.sin(angles), (1, 128 // half_dim))
    sine = jnp.where(jnp.arange(128)[None, :] % HEAD_DIM < half_dim, -sine, sine)
    rows_of = []
    for s in range(groups // 2):
        for c in range(2):
            place = lax.rem(member // 2 + s, groups // 2) * 2 + lax.rem(member + c, 2)
            rows_of.append(place * PROMPT_DEV + jnp.arange(PROMPT_DEV, dtype=jnp.int32))
    key_positions = jnp.concatenate(
        rows_of + [prompt_len + jnp.arange(tok_rows - PROMPT_DEV, dtype=jnp.int32)]
    )
    bias = jnp.where(
        key_positions[:, None] <= jnp.tile(positions, HEADS // (KV_HEADS // 2))[None, :],
        0.0,
        masked_score,
    )

    normed, queries, key_value = project(token_rows, attn_gain, w_qkv, cosine, sine)
    prompt = jnp.concatenate(gather_members(key_value[:, :PROMPT_DEV], groups), axis=1)

    first_expert = member * local_experts
    ids_t = gather_members(expert_ids.reshape(MICRO, tok_rows, TOP).transpose(0, 2, 1), groups)
    ids_all = lax.rem(jnp.concatenate(ids_t, axis=0) + (EXPERTS - first_expert), EXPERTS)
    cot_pieces = gather_members(cot_rows, groups)
    router = lax.dynamic_slice_in_dim(
        jnp.concatenate([w_router, w_router], axis=1), first_expert, EXPERTS, 1
    )

    attended, lse, hidden, moe_pieces, moe_low = [], [], [], [], []
    for m in range(MICRO):
        mask = bias if m == 0 else after(bias, *cot_pieces)
        att, log_total, hid, low = attend(
            m, queries, key_value, prompt, mask, token_rows, w_out, moe_gain
        )
        attended.append(att)
        lse.append(log_total[None])
        hidden.append(hid)
        moe_low.append(low)
        moe_pieces.append(gather_members(low, groups))
    d_rows, slots = pick_grads(ids_all, cot_pieces, local_experts)
    attended = jnp.concatenate(attended, axis=0)
    lse = jnp.concatenate(lse, axis=0)
    hidden = jnp.concatenate(hidden, axis=0)
    moe_low = jnp.concatenate(moe_low, axis=0)

    x_rows, slot_gate, gates = pick_tokens(
        ids_all, slots, router, [moe_pieces[m][g] for g in range(groups) for m in range(MICRO)]
    )
    slot_rows = blocks * SLOTS
    x_rows = x_rows.reshape(local_experts, slot_rows, D)
    d_rows = d_rows.reshape(local_experts, slot_rows, D)
    slot_gate = slot_gate.reshape(local_experts, slot_rows, 128)
    parity = lax.rem(dp_index, 2).astype(jnp.int32).reshape(1)
    swap_x = [(d, d ^ 1) for d in range(dp_size)]
    z_groups = [[d for d in range(dp_size) if d % 2 == r] for r in range(2)]
    piece = (D + FF) // (2 * pairs)

    def sum_z(value):
        count, _, height, _ = value.shape
        return lax.psum_scatter(
            value.reshape(count, pairs * height, D),
            "dp",
            scatter_dimension=1,
            axis_index_groups=z_groups,
            tiled=True,
        )

    outs, backs, dots, parts, pending = [], [], [], [], []
    first = 0
    for count in CHUNKS if sum(CHUNKS) == local_experts else (1,) * local_experts:
        split = first > 0
        out, back, dot, *sums = expert_chunk(
            parity, first, count, pairs, split, x_rows, d_rows, slot_gate, w_gate_up, w_down
        )
        shape = (count, blocks, SLOTS)
        outs.append(out.reshape(shape + (D,)))
        backs.append(back.reshape(shape + (D,)))
        dots.append(dot.reshape(shape + (128,)))
        if split:
            pending.append((sums[0], lax.ppermute(sums[1], "dp", swap_x)))
        else:
            whole = sum_z(sums[0])
        first += count

    def reduce_next():
        keep, got = pending.pop(0)
        half = (keep.astype(f32) + got.astype(f32)).astype(bf16)
        parts.append(sum_z(half))
        return half

    back_sum, back_dots = sum_rows(after(slots, reduce_next()), backs, dots)

    def pieces_of(value):
        return [value[j * MICRO : (j + 1) * MICRO] for j in range(groups)]

    back_terms = return_members(pieces_of(back_sum), groups)
    dot_pieces = exchange_members(pieces_of(back_dots), groups)
    token_dots = jnp.zeros((MICRO, EXPERTS, tok_rows), f32)
    for s in range(groups // 2):
        for c in range(2):
            place = lax.rem(member // 2 + groups // 2 - s, groups // 2) * 2 + lax.rem(
                member + c, 2
            )
            label = lax.rem(place + groups - member, groups) * local_experts
            token_dots = lax.dynamic_update_slice_in_dim(
                token_dots, dot_pieces[2 * s + c], label, 1
            )
    own_gates = gates[:MICRO]
    centre = jnp.sum(own_gates * token_dots, axis=1, keepdims=True)
    grad_logits = (own_gates * (token_dots - centre)).astype(bf16)
    (mixed,) = sum_rows(after(slots, back_sum), outs)
    mix_terms = return_members(pieces_of(mixed), groups)

    grad_hidden, grad_branch, grad_attended, grad_norm_moe = middle_back(
        back_terms, grad_logits, router, hidden, moe_gain, after(cot_rows, mixed), w_out
    )
    grad_router = jnp.einsum("btd,bet->de", moe_low, grad_logits, preferred_element_type=f32)
    grad_out = jnp.einsum("brd,bre->de", attended, grad_branch, preferred_element_type=f32)
    gq, gpk, gpv, gok, gov = attend_back(
        queries, key_value, prompt, bias, lse, grad_attended, cosine, sine
    )
    def prompt_terms(value):
        return return_members(
            [value[:, j * PROMPT_DEV : (j + 1) * PROMPT_DEV] for j in range(groups)], groups
        )

    gp, grad_qkv = weight_back(
        after(normed, reduce_next()), gq, gok, gov, prompt_terms(gpk), prompt_terms(gpv), cosine, sine
    )
    grad_tokens, grad_norm_attn = token_back(gp, w_qkv, token_rows, attn_gain, grad_hidden)
    while pending:
        reduce_next()
    swapped = lax.ppermute(whole[:, piece:], "dp", swap_x)
    whole = (whole[:, :piece].astype(f32) + swapped.astype(f32)).astype(bf16)
    parts.insert(0, whole)
    grad_router = lax.dynamic_slice_in_dim(
        jnp.concatenate([grad_router, grad_router], axis=1), EXPERTS - first_expert, EXPERTS, 1
    )
    mixture = sum(term.astype(f32) for term in mix_terms)
    output = (hidden + branch_scale * mixture).astype(bf16)

    small = jnp.concatenate(
        [
            grad_router,
            grad_norm_attn.reshape(D, 1),
            grad_norm_moe.reshape(D, 1),
            jnp.zeros((D, 128 - EXPERTS - 2), f32),
        ],
        axis=1,
    )
    wide = jnp.concatenate([grad_qkv, grad_out.astype(bf16), small.astype(bf16)], axis=1)
    wide = lax.psum(wide, ("dp", "expert")).astype(f32)
    experts_sum = jnp.concatenate(parts, axis=0).astype(f32)
    gu_piece = D // (2 * pairs)
    return (
        output.reshape(rows_all, D),
        grad_tokens.reshape(rows_all, D),
        wide[:, 3 * D + EXPERTS],
        wide[:, : 2 * D],
        wide[:, 2 * D : 3 * D],
        wide[:, 3 * D + EXPERTS + 1],
        wide[:, 3 * D : 3 * D + EXPERTS],
        experts_sum[:, :gu_piece],
        experts_sum[:, gu_piece:],
    )


def solution(mesh):
    in_specs = (
        P(("dp", "expert"), None),
        P(("dp", "expert"), None),
        P(("dp", "expert"), None),
        P(),
        P(),
        P(),
        P(),
        P(),
        P("expert", None, None),
        P("expert", None, None),
    )
    out_specs = (
        P(("dp", "expert"), None),
        P(("dp", "expert"), None),
        P(),
        P(),
        P(),
        P(),
        P(),
        P("expert", "dp", None),
        P("expert", "dp", None),
    )
    return jax.shard_map(local, mesh=mesh, in_specs=in_specs, out_specs=out_specs, check_vma=False)
```

```python
import functools

import jax
import jax.numpy as jnp
from jax import lax
from jax.experimental import pallas as pl
from jax.experimental.pallas import tpu as pltpu
from jax.sharding import PartitionSpec as P

D = 1024
HEADS = 16
KV_HEADS = 8
HEAD_DIM = 64
FF = 512
EXPERTS = 32
TOP = 8
PROMPT_DEV = 64
MICRO = 2
CAP = 100
SLOTS = 112
CHUNKS = ((1, True), (1, False), (2, False), (2, False), (1, True), (1, False))


epsilon = 1e-06
score_scale = 1.0 / 64.0
branch_scale = 0.22
masked_score = -1e30

f32 = jnp.float32
bf16 = jnp.bfloat16
vmem_limit = 60 * 1024 * 1024


def params():
    return pltpu.CompilerParams(
        vmem_limit_bytes=vmem_limit, dimension_semantics=("arbitrary",)
    )


def cost(micros):
    return pl.CostEstimate(flops=int(micros * 1.15e9), bytes_accessed=0, transcendentals=0)


def mm(left, right, dims):
    return lax.dot_general(left, right, (dims, ((), ())), preferred_element_type=f32)


def fill_one_hot(slot_rows, onehot_ref):
    experts, rows = slot_rows.shape
    place = lax.broadcasted_iota(jnp.int32, (SLOTS, rows), 0)
    for e in range(experts):
        hit = place == slot_rows[e : e + 1, :]
        onehot_ref[e * SLOTS : (e + 1) * SLOTS, :] = jnp.where(hit, 1.0, 0.0).astype(bf16)


def chosen_of(ids, count):
    rows = ids.shape[1]
    label = lax.broadcasted_iota(jnp.int32, (count, rows), 0)
    hit = ids[0:1, :] == label
    for k in range(1, ids.shape[0]):
        hit = hit | (ids[k : k + 1, :] == label)
    return hit


def select_block(row_refs, rows_ref):
    b = pl.program_id(0)
    at = 0
    for ref in row_refs:
        for i in range(ref.shape[0]):

            @pl.when(b == at)
            def _(ref=ref, i=i):
                rows_ref[...] = ref[i]

            at += 1


def store_picked(onehot_ref, rows_ref, out_ref):
    picked = mm(onehot_ref[...], rows_ref[...], ((1,), (0,))).astype(bf16)
    for e in range(out_ref.shape[0]):
        out_ref[e, 0] = picked[e * SLOTS : (e + 1) * SLOTS]


def pick_grad_body(*refs, pieces):
    ids_ref = refs[0]
    row_refs = refs[1 : 1 + pieces]
    out_ref, slot_ref, onehot_ref, rows_ref, earlier_ref = refs[1 + pieces :]
    experts, rows = slot_ref.shape[1], slot_ref.shape[2]

    @pl.when(pl.program_id(0) == 0)
    def _():
        first = lax.broadcasted_iota(jnp.int32, (rows, rows), 0)
        second = lax.broadcasted_iota(jnp.int32, (rows, rows), 1)
        earlier_ref[...] = jnp.where(first < second, 1.0, 0.0).astype(bf16)

    select_block(row_refs, rows_ref)
    hit = chosen_of(ids_ref[0], 8)
    rank = mm(jnp.where(hit, 1.0, 0.0).astype(bf16), earlier_ref[...], ((1,), (0,)))
    slots = jnp.where(hit, rank, -1.0).astype(jnp.int32)[:experts]
    slot_ref[0] = slots
    fill_one_hot(slots, onehot_ref)
    store_picked(onehot_ref, rows_ref, out_ref)


def full_spec(array):
    zeros = (0,) * array.ndim
    return pl.BlockSpec(array.shape, lambda *_: zeros)


def pick_grads(ids, pieces, experts):
    blocks, top, tok = ids.shape
    return pl.pallas_call(
        functools.partial(pick_grad_body, pieces=len(pieces)),
        grid=(blocks,),
        in_specs=[pl.BlockSpec((1, top, tok), lambda b: (b, 0, 0))]
        + [full_spec(piece) for piece in pieces],
        out_specs=[
            pl.BlockSpec((experts, 1, SLOTS, D), lambda b: (0, b, 0, 0)),
            pl.BlockSpec((1, experts, tok), lambda b: (b, 0, 0)),
        ],
        out_shape=[
            jax.ShapeDtypeStruct((experts, blocks, SLOTS, D), bf16),
            jax.ShapeDtypeStruct((blocks, experts, tok), jnp.int32),
        ],
        scratch_shapes=[
            pltpu.VMEM((experts * SLOTS, tok), bf16),
            pltpu.VMEM((tok, D), bf16),
            pltpu.VMEM((tok, tok), bf16),
        ],
        cost_estimate=cost(15),
        compiler_params=params(),
    )(ids, *pieces)


def pick_token_body(*refs, pieces):
    ids_ref, slot_ref, router_ref = refs[:3]
    row_refs = refs[3 : 3 + pieces]
    out_ref, slot_gate_ref, gate_ref, onehot_ref, rows_ref = refs[3 + pieces :]
    experts, rows = slot_ref.shape[1], slot_ref.shape[2]
    select_block(row_refs, rows_ref)
    logits = mm(router_ref[...], rows_ref[...], ((0,), (1,)))
    hit = chosen_of(ids_ref[0], EXPERTS)
    masked = jnp.where(hit, logits, masked_score)
    raised = jnp.where(hit, jnp.exp(masked - jnp.max(masked, axis=0, keepdims=True)), 0.0)
    gates = raised / jnp.sum(raised, axis=0, keepdims=True)
    gate_ref[0] = gates
    fill_one_hot(slot_ref[0], onehot_ref)
    store_picked(onehot_ref, rows_ref, out_ref)
    place = lax.broadcasted_iota(jnp.int32, (SLOTS, rows), 0)
    for e in range(experts):
        here = place == slot_ref[0, e : e + 1, :]
        gate = jnp.sum(jnp.where(here, gates[e : e + 1, :], 0.0), axis=1, keepdims=True)
        slot_gate_ref[e, 0] = jnp.broadcast_to(gate, (SLOTS, 128))


def pick_tokens(ids, slots, w_router, pieces):
    blocks, experts, tok = slots.shape
    return pl.pallas_call(
        functools.partial(pick_token_body, pieces=len(pieces)),
        grid=(blocks,),
        in_specs=[
            pl.BlockSpec((1, ids.shape[1], tok), lambda b: (b, 0, 0)),
            pl.BlockSpec((1, experts, tok), lambda b: (b, 0, 0)),
            full_spec(w_router),
        ]
        + [full_spec(piece) for piece in pieces],
        out_specs=[
            pl.BlockSpec((experts, 1, SLOTS, D), lambda b: (0, b, 0, 0)),
            pl.BlockSpec((experts, 1, SLOTS, 128), lambda b: (0, b, 0, 0)),
            pl.BlockSpec((1, EXPERTS, tok), lambda b: (b, 0, 0)),
        ],
        out_shape=[
            jax.ShapeDtypeStruct((experts, blocks, SLOTS, D), bf16),
            jax.ShapeDtypeStruct((experts, blocks, SLOTS, 128), f32),
            jax.ShapeDtypeStruct((blocks, EXPERTS, tok), f32),
        ],
        scratch_shapes=[pltpu.VMEM((experts * SLOTS, tok), bf16), pltpu.VMEM((tok, D), bf16)],
        cost_estimate=cost(17),
        compiler_params=params(),
    )(ids, slots, w_router, *pieces)


def sum_rows_body(*refs, chunks, with_dots):
    slot_ref = refs[0]
    row_refs = refs[1 : 1 + chunks]
    refs = refs[1 + chunks :]
    if with_dots:
        dot_refs, refs = refs[:chunks], refs[chunks:]
        out_ref, back_ref, onehot_ref, flat_ref = refs
    else:
        out_ref, onehot_ref, flat_ref = refs
    fill_one_hot(slot_ref[0], onehot_ref)
    e = 0
    for ref in row_refs:
        for i in range(ref.shape[0]):
            flat_ref[e * SLOTS : (e + 1) * SLOTS, :] = ref[i, 0]
            e += 1
    out_ref[0] = mm(onehot_ref[...], flat_ref[...], ((0,), (0,))).astype(bf16)
    if with_dots:
        place = lax.broadcasted_iota(jnp.int32, (SLOTS, slot_ref.shape[2]), 0)
        e = 0
        for ref in dot_refs:
            for i in range(ref.shape[0]):
                hit = place == slot_ref[0, e : e + 1, :]
                back_ref[0, e : e + 1, :] = jnp.sum(
                    jnp.where(hit, ref[i, 0, :, 0:1], 0.0), axis=0, keepdims=True
                )
                e += 1


def sum_rows(slots, rows, dots=None):
    blocks, experts, tok = slots.shape

    def chunk_spec(chunk):
        return pl.BlockSpec((chunk.shape[0], 1) + chunk.shape[2:], lambda b: (0, b, 0, 0))

    in_specs = [pl.BlockSpec((1, experts, tok), lambda b: (b, 0, 0))]
    in_specs += [chunk_spec(chunk) for chunk in rows]
    args = [slots] + rows
    out_shape = [jax.ShapeDtypeStruct((blocks, tok, D), bf16)]
    out_specs = [pl.BlockSpec((1, tok, D), lambda b: (b, 0, 0))]
    if dots is not None:
        in_specs += [chunk_spec(chunk) for chunk in dots]
        args += dots
        out_shape.append(jax.ShapeDtypeStruct((blocks, experts, tok), f32))
        out_specs.append(pl.BlockSpec((1, experts, tok), lambda b: (b, 0, 0)))
    return pl.pallas_call(
        functools.partial(sum_rows_body, chunks=len(rows), with_dots=dots is not None),
        grid=(blocks,),
        in_specs=in_specs,
        out_specs=out_specs,
        out_shape=out_shape,
        scratch_shapes=[
            pltpu.VMEM((experts * SLOTS, tok), bf16),
            pltpu.VMEM((experts * SLOTS, D), bf16),
        ],
        cost_estimate=cost(15),
        compiler_params=params(),
    )(*args)


def expert_body(
    parity_ref,
    x_ref,
    d_ref,
    gate_ref,
    wgu_ref,
    wd_ref,
    out_ref,
    back_ref,
    dots_ref,
    *part_refs,
    tile,
):
    mid_ref, grad_ref, act_ref, gu_ref, down_ref = part_refs[-5:]
    part_refs = part_refs[:-5]
    rows = x_ref.shape[1]

    def step(i, carry):
        span = pl.ds(pl.multiple_of(i * tile, tile), tile)
        hidden = mm(x_ref[0, span, :], wgu_ref[0], ((1,), (0,)))
        gate, up = hidden[:, :FF], hidden[:, FF:]
        sig = 1.0 / (1.0 + jnp.exp(-gate))
        silu = gate * sig
        middle = (silu * up).astype(bf16)
        mid_ref[span, :] = middle
        out = mm(middle, wd_ref[0], ((1,), (0,))).astype(bf16).astype(f32)
        weight = gate_ref[0, span, 0:1]
        scaled = branch_scale * d_ref[0, span, :].astype(f32)
        dots_ref[0, span, :] = jnp.broadcast_to(
            jnp.sum(scaled * out, axis=1, keepdims=True), (tile, 128)
        )
        out_ref[0, span, :] = (weight * out).astype(bf16)
        grad = (weight * scaled).astype(bf16)
        grad_ref[span, :] = grad
        grad_mid = mm(grad, wd_ref[0], ((1,), (1,)))
        act_ref[span, :FF] = (grad_mid * up * sig * (1.0 + gate * (1.0 - sig))).astype(bf16)
        act_ref[span, FF:] = (grad_mid * silu).astype(bf16)
        back_ref[0, span, :] = mm(act_ref[span, :], wgu_ref[0], ((1,), (1,))).astype(bf16)
        return carry

    lax.fori_loop(0, rows // tile, step, 0)
    gu_ref[...] = mm(x_ref[0], act_ref[...], ((0,), (0,))).astype(bf16)
    down_ref[...] = mm(mid_ref[...], grad_ref[...], ((0,), (0,))).astype(bf16)
    parity = parity_ref[0]
    pairs = part_refs[0].shape[1]
    half = (gu_ref.shape[0] + down_ref.shape[0]) // (2 * pairs)
    keep_ref, send_ref = part_refs[0], part_refs[-1]
    shift = half if len(part_refs) == 1 else 0
    start = 0
    for full in (gu_ref, down_ref):
        piece = full.shape[0] // (2 * pairs)
        for j in range(pairs):
            mine = pl.multiple_of((2 * j + parity) * piece, piece)
            other = pl.multiple_of((2 * j + 1 - parity) * piece, piece)
            keep_ref[0, j, start : start + piece, :] = full[pl.ds(mine, piece), :]
            send_ref[0, j, shift + start : shift + start + piece, :] = full[pl.ds(other, piece), :]
        start += piece


def expert_chunk(parity, first, count, pairs, split, x_rows, d_rows, slot_gate, w_gate_up, w_down):
    rows = x_rows.shape[1]
    tile = 2 * SLOTS
    mode = pl.Buffered(1 if rows > 1024 else 2)
    row_spec = pl.BlockSpec((1, rows, D), lambda e, p: (e + first, 0, 0), pipeline_mode=mode)
    col_spec = pl.BlockSpec((1, rows, 128), lambda e, p: (e + first, 0, 0))
    parts = 2 if split else 1
    piece = (D + FF) // (parts * pairs)
    part_spec = pl.BlockSpec((1, pairs, piece, D), lambda e, p: (e, 0, 0, 0))
    part_shape = jax.ShapeDtypeStruct((count, pairs, piece, D), bf16)
    out_row = pl.BlockSpec((1, rows, D), lambda e, p: (e, 0, 0))
    grid_spec = pltpu.PrefetchScalarGridSpec(
        num_scalar_prefetch=1,
        grid=(count,),
        in_specs=[
            row_spec,
            row_spec,
            col_spec,
            pl.BlockSpec((1, D, 2 * FF), lambda e, p: (e + first, 0, 0)),
            pl.BlockSpec((1, FF, D), lambda e, p: (e + first, 0, 0)),
        ],
        out_specs=[
            out_row,
            out_row,
            pl.BlockSpec((1, rows, 128), lambda e, p: (e, 0, 0)),
        ]
        + [part_spec] * parts,
        scratch_shapes=[
            pltpu.VMEM((rows, FF), bf16),
            pltpu.VMEM((rows, D), bf16),
            pltpu.VMEM((rows, 2 * FF), bf16),
            pltpu.VMEM((D, 2 * FF), bf16),
            pltpu.VMEM((FF, D), bf16),
        ],
    )
    return pl.pallas_call(
        functools.partial(expert_body, tile=tile),
        grid_spec=grid_spec,
        out_shape=[
            jax.ShapeDtypeStruct((count, rows, D), bf16),
            jax.ShapeDtypeStruct((count, rows, D), bf16),
            jax.ShapeDtypeStruct((count, rows, 128), f32),
        ]
        + [part_shape] * parts,
        cost_estimate=cost(15 * count),
        compiler_params=params(),
    )(parity, x_rows, d_rows, slot_gate, w_gate_up, w_down)


def core_swap(value, groups):
    return lax.ppermute(value, "expert", [(m, m ^ 1) for m in range(groups)])


def from_row(value, groups, shift):
    count = groups // 2
    pairs = [((((y + shift) % count) * 2 + c), y * 2 + c) for y in range(count) for c in range(2)]
    return lax.ppermute(value, "expert", pairs)


def to_row(value, groups, shift):
    count = groups // 2
    pairs = [(y * 2 + c, ((y + shift) % count) * 2 + c) for y in range(count) for c in range(2)]
    return lax.ppermute(value, "expert", pairs)


def gather_members(value, groups):
    column = [value] + [from_row(value, groups, s) for s in range(1, groups // 2)]
    result = []
    for piece in column:
        result += [piece, core_swap(piece, groups)]
    return result


def return_members(pieces, groups):
    swapped = [core_swap(pieces[2 * s + 1], groups) for s in range(groups // 2)]
    terms = [pieces[0], swapped[0]]
    for s in range(1, groups // 2):
        both = (pieces[2 * s].astype(f32) + swapped[s].astype(f32)).astype(bf16)
        terms.append(to_row(both, groups, s))
    return terms


def exchange_members(pieces, groups):
    count = groups // 2
    result = []
    for s in range(count):
        for c in range(2):
            if s == 0 and c == 0:
                result.append(pieces[0])
                continue
            pairs = [
                (((y - s) % count) * 2 + (core ^ c), y * 2 + core)
                for y in range(count)
                for core in range(2)
            ]
            result.append(lax.ppermute(pieces[2 * s + c], "expert", pairs))
    return result


def lane(shape):
    return lax.broadcasted_iota(jnp.int32, shape, len(shape) - 1)


def turn(value, cosine, sine, sign):
    first = lax.rem(lane(value.shape), HEAD_DIM) < HEAD_DIM // 2
    other = jnp.where(
        first, pltpu.roll(value, 128 - HEAD_DIM // 2, 1), pltpu.roll(value, HEAD_DIM // 2, 1)
    )
    return value * cosine + sign * other * sine


def project_body(x_ref, gain_ref, w_ref, cos_ref, sin_ref, normed_ref, q_ref, kv_ref):
    x = x_ref[0].astype(f32)
    scale = lax.rsqrt(jnp.mean(x * x, axis=1, keepdims=True) + epsilon)
    normed = (x * scale * gain_ref[...]).astype(bf16)
    normed_ref[0] = normed
    cosine, sine = cos_ref[...], sin_ref[...]
    q_width, k_width = HEADS * HEAD_DIM, KV_HEADS * HEAD_DIM
    for start in range(0, q_width + 2 * k_width, 512):
        part = mm(normed, w_ref[:, start : start + 512], ((1,), (0,)))
        for inner in range(0, 512, 128):
            at = start + inner
            value = part[:, inner : inner + 128]
            if at < q_width:
                q_ref[0, :, at : at + 128] = turn(value, cosine, sine, 1.0).astype(bf16)
            elif at < q_width + k_width:
                at -= q_width
                kv_ref[0, :, at : at + 128] = turn(value, cosine, sine, 1.0).astype(bf16)
            else:
                at -= q_width
                kv_ref[0, :, at : at + 128] = value.astype(bf16)


def project(tokens, gain, w_qkv, cosine, sine):
    micro, rows, _ = tokens.shape
    block = pl.BlockSpec((1, rows, D), lambda m: (m, 0, 0))
    table = pl.BlockSpec((rows, 128), lambda m: (0, 0))
    shape = jax.ShapeDtypeStruct((micro, rows, D), bf16)
    return pl.pallas_call(
        project_body,
        grid=(micro,),
        in_specs=[
            block,
            pl.BlockSpec((1, D), lambda m: (0, 0)),
            pl.BlockSpec(w_qkv.shape, lambda m: (0, 0)),
            table,
            table,
        ],
        out_specs=[block, block, block],
        out_shape=[shape, shape, shape],
        cost_estimate=cost(7),
        compiler_params=params(),
    )(tokens, gain, w_qkv, cosine, sine)


def stack_heads(block, scale):
    wide = block.astype(f32) * scale
    result = []
    for p in range(2):
        part = wide[:, p * 128 : (p + 1) * 128]
        half = (lane(part.shape) >= HEAD_DIM) == (p == 1)
        for h in range(2):
            moved = part if h == p else pltpu.roll(part, HEAD_DIM, 1)
            result.append(jnp.where(half, moved, 0.0).astype(bf16))
    return jnp.concatenate(result, axis=0)


def unstack_heads(stacked, rows):
    result = []
    for p in range(2):
        pieces = []
        for h in range(2):
            i = 2 * p + h
            part = stacked[i * rows : (i + 1) * rows]
            pieces.append(part if h == p else pltpu.roll(part, HEAD_DIM, 1))
        result.append(jnp.where(lane(pieces[0].shape) < HEAD_DIM, pieces[0], pieces[1]))
    return result


def attend_body(
    q_ref, pk_ref, pv_ref, ok_ref, ov_ref, bias_ref, x_ref, w_ref, gain_ref,
    att_ref, lse_ref, hidden_ref, low_ref, all_ref,
):
    j = pl.program_id(0)
    rows = q_ref.shape[1]
    q = stack_heads(q_ref[0], score_scale)
    k = jnp.concatenate([pk_ref[0], ok_ref[0, PROMPT_DEV:, :]], axis=0)
    v = jnp.concatenate([pv_ref[0], ov_ref[0, PROMPT_DEV:, :]], axis=0)
    scores = mm(k, q, ((1,), (1,))) + bias_ref[...]
    largest = jnp.max(scores, axis=0, keepdims=True)
    raised = jnp.exp(scores - largest)
    total = jnp.sum(raised, axis=0, keepdims=True)
    weights = (raised * (1.0 / total)).astype(bf16)
    lse_ref[0] = largest + jnp.log(total)
    mixed = mm(v, weights, ((0,), (0,))).T
    for p, part in enumerate(unstack_heads(mixed, rows)):
        at = pl.multiple_of(j * 256 + p * 128, 128)
        att_ref[0, :, p * 128 : (p + 1) * 128] = part.astype(bf16)
        all_ref[:, pl.ds(at, 128)] = part.astype(bf16)

    @pl.when(j == pl.num_programs(0) - 1)
    def _():
        branch = mm(all_ref[...], w_ref[...], ((1,), (0,)))
        hidden = x_ref[0].astype(f32) + branch_scale * branch
        hidden_ref[0] = hidden
        scale = lax.rsqrt(jnp.mean(hidden * hidden, axis=1, keepdims=True) + epsilon)
        low_ref[0] = (hidden * scale * gain_ref[...]).astype(bf16)


def attend(micro, q, kv, prompt, bias, tokens, w_out, gain):
    rows, prompt_rows = q.shape[1], prompt.shape[1]
    steps = KV_HEADS // 2
    full = pl.BlockSpec((1, rows, D), lambda j: (micro, 0, 0))
    one = pl.BlockSpec((1, rows, D), lambda j: (0, 0, 0))
    return pl.pallas_call(
        attend_body,
        grid=(steps,),
        in_specs=[
            pl.BlockSpec((1, rows, 256), lambda j: (micro, 0, j)),
            pl.BlockSpec((1, prompt_rows, 128), lambda j: (micro, 0, j)),
            pl.BlockSpec((1, prompt_rows, 128), lambda j: (micro, 0, j + steps)),
            pl.BlockSpec((1, rows, 128), lambda j: (micro, 0, j)),
            pl.BlockSpec((1, rows, 128), lambda j: (micro, 0, j + steps)),
            pl.BlockSpec(bias.shape, lambda j: (0, 0)),
            full,
            pl.BlockSpec(w_out.shape, lambda j: (0, 0)),
            pl.BlockSpec((1, D), lambda j: (0, 0)),
        ],
        out_specs=[
            pl.BlockSpec((1, rows, 256), lambda j: (0, 0, j)),
            pl.BlockSpec((1, 1, 4 * rows), lambda j: (j, 0, 0)),
            one,
            one,
        ],
        out_shape=[
            jax.ShapeDtypeStruct((1, rows, D), bf16),
            jax.ShapeDtypeStruct((steps, 1, 4 * rows), f32),
            jax.ShapeDtypeStruct((1, rows, D), f32),
            jax.ShapeDtypeStruct((1, rows, D), bf16),
        ],
        scratch_shapes=[pltpu.VMEM((rows, D), bf16)],
        cost_estimate=cost(12),
        compiler_params=params(),
    )(q, prompt, prompt, kv, kv, bias, tokens, w_out, gain)


def norm_back(value, gain, grad):
    scale = lax.rsqrt(jnp.mean(value * value, axis=1, keepdims=True) + epsilon)
    scaled = grad * gain
    inner = jnp.mean(scaled * value, axis=1, keepdims=True)
    back = scale * scaled - value * (scale * scale * scale * inner)
    return back, jnp.sum(grad * value * scale, axis=0, keepdims=True)


def middle_body(*refs, terms):
    term_refs = refs[:terms]
    (logit_ref, router_ref, hidden_ref, gain_ref, cot_ref, w_ref) = refs[terms : terms + 6]
    grad_hidden_ref, branch_ref, att_ref, gain_out_ref = refs[terms + 6 :]
    total = mm(logit_ref[0], router_ref[...], ((0,), (1,)))
    for ref in term_refs:
        total = total + ref[0].astype(f32)
    back, gain_grad = norm_back(hidden_ref[0], gain_ref[...], total)
    grad_hidden = cot_ref[0].astype(f32) + back
    grad_hidden_ref[0] = grad_hidden
    branch = (branch_scale * grad_hidden).astype(bf16)
    branch_ref[0] = branch
    att_ref[0] = mm(branch, w_ref[...], ((1,), (1,))).astype(bf16)

    @pl.when(pl.program_id(0) == 0)
    def _():
        gain_out_ref[...] = gain_grad

    @pl.when(pl.program_id(0) != 0)
    def _():
        gain_out_ref[...] += gain_grad


def middle_back(terms, grad_logits, w_router, hidden, gain, cotangent, w_out):
    micro, rows, _ = hidden.shape
    block = pl.BlockSpec((1, rows, D), lambda m: (m, 0, 0))
    row = pl.BlockSpec((1, D), lambda m: (0, 0))
    return pl.pallas_call(
        functools.partial(middle_body, terms=len(terms)),
        grid=(micro,),
        in_specs=[block] * len(terms)
        + [
            pl.BlockSpec((1, EXPERTS, rows), lambda m: (m, 0, 0)),
            pl.BlockSpec(w_router.shape, lambda m: (0, 0)),
            block,
            row,
            block,
            pl.BlockSpec(w_out.shape, lambda m: (0, 0)),
        ],
        out_specs=[block, block, block, row],
        out_shape=[
            jax.ShapeDtypeStruct((micro, rows, D), f32),
            jax.ShapeDtypeStruct((micro, rows, D), bf16),
            jax.ShapeDtypeStruct((micro, rows, D), bf16),
            jax.ShapeDtypeStruct((1, D), f32),
        ],
        cost_estimate=cost(8),
        compiler_params=params(),
    )(*terms, grad_logits, w_router, hidden, gain, cotangent, w_out)


def attend_back_body(
    q_ref, pk_ref, pv_ref, ok_ref, ov_ref, bias_ref, lse_ref, grad_ref, cos_ref, sin_ref,
    gq_ref, gpk_ref, gpv_ref, gok_ref, gov_ref,
):
    rows, prompt_rows = q_ref.shape[1], pk_ref.shape[1]
    q = stack_heads(q_ref[0], score_scale)
    grad = stack_heads(grad_ref[0], 1.0)
    k = jnp.concatenate([pk_ref[0], ok_ref[0, PROMPT_DEV:, :]], axis=0)
    v = jnp.concatenate([pv_ref[0], ov_ref[0, PROMPT_DEV:, :]], axis=0)
    probs = jnp.exp(mm(k, q, ((1,), (1,))) + bias_ref[...] - lse_ref[0, 0])
    grad_probs = mm(v, grad, ((1,), (1,)))
    centre = jnp.sum(probs * grad_probs, axis=0, keepdims=True)
    grad_scores = (probs * (grad_probs - centre)).astype(bf16)
    grad_v = mm(probs.astype(bf16), grad, ((1,), (0,)))
    grad_k = mm(grad_scores, q, ((1,), (0,)))
    grad_q = mm(k, grad_scores, ((0,), (0,))).T * score_scale
    cosine, sine = cos_ref[...], sin_ref[...]
    for p, part in enumerate(unstack_heads(grad_q, rows)):
        gq_ref[0, :, p * 128 : (p + 1) * 128] = turn(part, cosine, sine, -1.0).astype(bf16)
    gpk_ref[0] = grad_k[:prompt_rows].astype(bf16)
    gpv_ref[0] = grad_v[:prompt_rows].astype(bf16)
    gok_ref[0] = turn(
        grad_k[prompt_rows:], cosine[PROMPT_DEV:], sine[PROMPT_DEV:], -1.0
    ).astype(bf16)
    gov_ref[0] = grad_v[prompt_rows:].astype(bf16)


def attend_back(q, kv, prompt, bias, lse, grad, cosine, sine):
    micro, rows, _ = q.shape
    prompt_rows = prompt.shape[1]
    own_rows = rows - PROMPT_DEV
    steps = KV_HEADS // 2
    wide = pl.BlockSpec((1, rows, 256), lambda m, j: (m, 0, j))
    table = pl.BlockSpec((rows, 128), lambda m, j: (0, 0))
    prompt_spec = pl.BlockSpec((1, prompt_rows, 128), lambda m, j: (m, 0, j))
    own_spec = pl.BlockSpec((1, own_rows, 128), lambda m, j: (m, 0, j))
    k_width = KV_HEADS * HEAD_DIM
    return pl.pallas_call(
        attend_back_body,
        grid=(micro, steps),
        in_specs=[
            wide,
            prompt_spec,
            pl.BlockSpec((1, prompt_rows, 128), lambda m, j: (m, 0, j + steps)),
            pl.BlockSpec((1, rows, 128), lambda m, j: (m, 0, j)),
            pl.BlockSpec((1, rows, 128), lambda m, j: (m, 0, j + steps)),
            pl.BlockSpec(bias.shape, lambda m, j: (0, 0)),
            pl.BlockSpec((1, 1, 1, 4 * rows), lambda m, j: (m, j, 0, 0)),
            wide,
            table,
            table,
        ],
        out_specs=[wide, prompt_spec, prompt_spec, own_spec, own_spec],
        out_shape=[
            jax.ShapeDtypeStruct((micro, rows, D), bf16),
            jax.ShapeDtypeStruct((micro, prompt_rows, k_width), bf16),
            jax.ShapeDtypeStruct((micro, prompt_rows, k_width), bf16),
            jax.ShapeDtypeStruct((micro, own_rows, k_width), bf16),
            jax.ShapeDtypeStruct((micro, own_rows, k_width), bf16),
        ],
        cost_estimate=cost(23),
        compiler_params=pltpu.CompilerParams(
            vmem_limit_bytes=vmem_limit, dimension_semantics=("arbitrary", "arbitrary")
        ),
    )(q, prompt, prompt, kv, kv, bias, lse, grad, cosine, sine)


def weight_body(*refs, terms):
    normed_ref, gq_ref, gok_ref, gov_ref = refs[:4]
    k_terms, v_terms = refs[4 : 4 + terms], refs[4 + terms : 4 + 2 * terms]
    cos_ref, sin_ref, gp_ref, out_ref, acc_ref = refs[4 + 2 * terms :]
    q_width, k_width = HEADS * HEAD_DIM, KV_HEADS * HEAD_DIM
    gp_ref[0, :, :q_width] = gq_ref[0]
    gp_ref[0, PROMPT_DEV:, q_width : q_width + k_width] = gok_ref[0]
    gp_ref[0, PROMPT_DEV:, q_width + k_width :] = gov_ref[0]
    prompt_k, prompt_v = [sum(ref[0].astype(f32) for ref in group) for group in (k_terms, v_terms)]
    cosine, sine = cos_ref[:PROMPT_DEV, :], sin_ref[:PROMPT_DEV, :]
    for at in range(0, k_width, 128):
        turned = turn(prompt_k[:, at : at + 128], cosine, sine, -1.0)
        gp_ref[0, :PROMPT_DEV, q_width + at : q_width + at + 128] = turned.astype(bf16)
    gp_ref[0, :PROMPT_DEV, q_width + k_width :] = prompt_v.astype(bf16)
    part = mm(normed_ref[0], gp_ref[0], ((0,), (0,)))
    m = pl.program_id(0)

    @pl.when(m == 0)
    def _():
        acc_ref[...] = part

    @pl.when(m != 0)
    def _():
        acc_ref[...] += part

    @pl.when(m == pl.num_programs(0) - 1)
    def _():
        out_ref[...] = acc_ref[...].astype(bf16)


def weight_back(normed, gq, gok, gov, k_terms, v_terms, cosine, sine):
    micro, rows, _ = normed.shape
    k_width = KV_HEADS * HEAD_DIM
    wide = pl.BlockSpec((1, rows, D), lambda m: (m, 0, 0))
    own = pl.BlockSpec((1, rows - PROMPT_DEV, k_width), lambda m: (m, 0, 0))
    term = pl.BlockSpec((1, PROMPT_DEV, k_width), lambda m: (m, 0, 0))
    table = pl.BlockSpec((rows, 128), lambda m: (0, 0))
    return pl.pallas_call(
        functools.partial(weight_body, terms=len(k_terms)),
        grid=(micro,),
        in_specs=[wide, wide, own, own] + [term] * (2 * len(k_terms)) + [table, table],
        out_specs=[
            pl.BlockSpec((1, rows, 2 * D), lambda m: (m, 0, 0)),
            pl.BlockSpec((D, 2 * D), lambda m: (0, 0)),
        ],
        out_shape=[
            jax.ShapeDtypeStruct((micro, rows, 2 * D), bf16),
            jax.ShapeDtypeStruct((D, 2 * D), bf16),
        ],
        scratch_shapes=[pltpu.VMEM((D, 2 * D), f32)],
        cost_estimate=cost(11),
        compiler_params=params(),
    )(normed, gq, gok, gov, *k_terms, *v_terms, cosine, sine)


def token_body(gp_ref, w_ref, x_ref, gain_ref, hidden_ref, out_ref, gain_out_ref):
    grad = mm(gp_ref[0], w_ref[...], ((1,), (1,)))
    back, gain_grad = norm_back(x_ref[0].astype(f32), gain_ref[...], grad)
    out_ref[0] = (hidden_ref[0] + back).astype(bf16)

    @pl.when(pl.program_id(0) == 0)
    def _():
        gain_out_ref[...] = gain_grad

    @pl.when(pl.program_id(0) != 0)
    def _():
        gain_out_ref[...] += gain_grad


def token_back(gp, w_qkv, tokens, gain, grad_hidden):
    micro, rows, _ = tokens.shape
    block = pl.BlockSpec((1, rows, D), lambda m: (m, 0, 0))
    row = pl.BlockSpec((1, D), lambda m: (0, 0))
    return pl.pallas_call(
        token_body,
        grid=(micro,),
        in_specs=[
            pl.BlockSpec((1, rows, 2 * D), lambda m: (m, 0, 0)),
            pl.BlockSpec(w_qkv.shape, lambda m: (0, 0)),
            block,
            row,
            block,
        ],
        out_specs=[block, row],
        out_shape=[
            jax.ShapeDtypeStruct((micro, rows, D), bf16),
            jax.ShapeDtypeStruct((1, D), f32),
        ],
        cost_estimate=cost(8),
        compiler_params=params(),
    )(gp, w_qkv, tokens, gain, grad_hidden)


def halve(value, axis, swap, bit):
    rows = value.shape[0] // 2
    keep = lax.dynamic_slice_in_dim(value, bit * rows, rows, 0)
    send = lax.dynamic_slice_in_dim(value, (1 - bit) * rows, rows, 0)
    got = lax.ppermute(send, axis, swap)
    return (keep.astype(f32) + got.astype(f32)).astype(bf16)


def finish_dense_body(table_ref, *refs, pieces):
    first_refs, second_refs = refs[:pieces], refs[pieces : 2 * pieces]
    qkv_ref, out_ref = refs[2 * pieces :]
    width = first_refs[0].shape[1]
    rest = qkv_ref.shape[1] - width
    for i in range(pieces):

        @pl.when(pl.program_id(0) == i)
        def _(i=i):
            qkv_ref[:, :width] = first_refs[i][...].astype(f32)
            qkv_ref[:, width:] = second_refs[i][:, :rest].astype(f32)
            out_ref[...] = second_refs[i][:, rest:].astype(f32)


def finish_dense(table, first, second):
    pieces = len(first)
    height = first[0].shape[0]
    grid_spec = pltpu.PrefetchScalarGridSpec(
        num_scalar_prefetch=1,
        grid=(pieces,),
        in_specs=[full_spec(piece) for piece in first + second],
        out_specs=[
            pl.BlockSpec((height, 2 * D), lambda i, t: (t[i], 0)),
            pl.BlockSpec((height, D), lambda i, t: (t[i], 0)),
        ],
    )
    return pl.pallas_call(
        functools.partial(finish_dense_body, pieces=pieces),
        grid_spec=grid_spec,
        out_shape=[
            jax.ShapeDtypeStruct((pieces * height, 2 * D), f32),
            jax.ShapeDtypeStruct((pieces * height, D), f32),
        ],
        cost_estimate=cost(9),
        compiler_params=params(),
    )(table, *first, *second)


def after(value, *others):
    return lax.optimization_barrier((value,) + others)[0]


def local(
    tokens, cotangent, expert_ids, norm_attn, w_qkv, w_out, norm_moe, w_router, w_gate_up, w_down
):
    groups = lax.axis_size("expert")
    dp_size = lax.axis_size("dp")
    member = lax.axis_index("expert")
    dp_index = lax.axis_index("dp")
    rows_all = tokens.shape[0]
    tok_rows = rows_all // MICRO
    local_experts = w_gate_up.shape[0]
    prompt_len = PROMPT_DEV * groups
    k_width = KV_HEADS * HEAD_DIM
    pairs = dp_size // 2
    blocks = groups * MICRO
    attn_gain = norm_attn.reshape(1, D)
    moe_gain = norm_moe.reshape(1, D)
    token_rows = tokens.reshape(MICRO, tok_rows, D)
    cot_rows = cotangent.reshape(MICRO, tok_rows, D)

    local_index = jnp.arange(tok_rows, dtype=jnp.int32)
    positions = jnp.where(
        local_index < PROMPT_DEV,
        member * PROMPT_DEV + local_index,
        prompt_len + local_index - PROMPT_DEV,
    )
    half_dim = HEAD_DIM // 2
    inverse = 10000.0 ** (-2.0 * jnp.arange(half_dim, dtype=f32) / HEAD_DIM)
    angles = positions.astype(f32)[:, None] * inverse[None, :]
    cosine = jnp.tile(jnp.cos(angles), (1, 128 // half_dim))
    sine = jnp.tile(jnp.sin(angles), (1, 128 // half_dim))
    sine = jnp.where(jnp.arange(128)[None, :] % HEAD_DIM < half_dim, -sine, sine)
    rows_of = []
    for s in range(groups // 2):
        for c in range(2):
            place = lax.rem(member // 2 + s, groups // 2) * 2 + lax.rem(member + c, 2)
            rows_of.append(place * PROMPT_DEV + jnp.arange(PROMPT_DEV, dtype=jnp.int32))
    key_positions = jnp.concatenate(
        rows_of + [prompt_len + jnp.arange(tok_rows - PROMPT_DEV, dtype=jnp.int32)]
    )
    bias = jnp.where(
        key_positions[:, None] <= jnp.tile(positions, HEADS // (KV_HEADS // 2))[None, :],
        0.0,
        masked_score,
    )

    first_expert = member * local_experts
    ids_t = gather_members(expert_ids.reshape(MICRO, tok_rows, TOP).transpose(0, 2, 1), groups)
    ids_all = lax.rem(jnp.concatenate(ids_t, axis=0) + (EXPERTS - first_expert), EXPERTS)
    cot_pieces = [gather_members(cot_rows[:1], groups)]
    normed, queries, key_value = project(token_rows, attn_gain, w_qkv, cosine, sine)
    prompt_pieces = gather_members(key_value[:, :PROMPT_DEV], groups)
    prompt = jnp.concatenate(prompt_pieces, axis=1)
    cot_pieces += [
        gather_members(after(cot_rows[m : m + 1], prompt_pieces[2]), groups)
        for m in range(1, MICRO)
    ]
    router = lax.dynamic_slice_in_dim(
        jnp.concatenate([w_router, w_router], axis=1), first_expert, EXPERTS, 1
    )

    attended, lse, hidden, moe_pieces, moe_low = [], [], [], [], []
    for m in range(MICRO):
        mask = bias if m == 0 else after(bias, moe_low[-1])
        att, log_total, hid, low = attend(
            m, queries, key_value, prompt, mask, token_rows, w_out, moe_gain
        )
        attended.append(att)
        lse.append(log_total[None])
        hidden.append(hid)
        moe_low.append(low)
        moe_pieces.append(gather_members(low, groups))

    def by_block(pieces):
        return [pieces[m][g] for g in range(groups) for m in range(MICRO)]

    d_rows, slots = pick_grads(after(ids_all, moe_low[-1]), by_block(cot_pieces), local_experts)
    attended = jnp.concatenate(attended, axis=0)
    lse = jnp.concatenate(lse, axis=0)
    hidden = jnp.concatenate(hidden, axis=0)
    moe_low = jnp.concatenate(moe_low, axis=0)

    x_rows, slot_gate, gates = pick_tokens(ids_all, slots, router, by_block(moe_pieces))
    slot_rows = blocks * SLOTS
    x_rows = x_rows.reshape(local_experts, slot_rows, D)
    d_rows = d_rows.reshape(local_experts, slot_rows, D)
    slot_gate = slot_gate.reshape(local_experts, slot_rows, 128)
    parity = lax.rem(dp_index, 2).astype(jnp.int32)
    swap_x = [(d, d ^ 1) for d in range(dp_size)]
    swap_y = [(m, m ^ 2) for m in range(groups)]
    swap_core = [(m, m ^ 1) for m in range(groups)]
    z_groups = [[d for d in range(dp_size) if d % 2 == r] for r in range(2)]
    piece = (D + FF) // (2 * pairs)

    def sum_z(value):
        count, _, height, _ = value.shape
        return lax.psum_scatter(
            value.reshape(count, pairs * height, D),
            "dp",
            scatter_dimension=1,
            axis_index_groups=z_groups,
            tiled=True,
        )

    plan = CHUNKS
    if sum(count for count, _ in plan) != local_experts:
        plan = tuple((1, e == 0) for e in range(local_experts))
    outs, backs, dots, halves, parts = [], [], [], {}, {}

    def add_x(i, *before):
        keep, got = halves.pop(i)
        got = after(got, *before)
        half = (keep.astype(f32) + got.astype(f32)).astype(bf16)
        parts[i] = sum_z(half)
        return half

    first = 0
    order = parity.reshape(1)
    for i, (count, whole) in enumerate(plan):
        if i:
            order = after(order, outs[-1])
        if i == 4:
            order = after(order, add_x(1, outs[-1]), parts[0])
        out, back, dot, *sums = expert_chunk(
            order, first, count, pairs, not whole, x_rows, d_rows, slot_gate, w_gate_up, w_down
        )
        shape = (count, blocks, SLOTS)
        outs.append(out.reshape(shape + (D,)))
        backs.append(back.reshape(shape + (D,)))
        dots.append(dot.reshape(shape + (128,)))
        if whole:
            parts[i] = sum_z(sums[0])
        else:
            halves[i] = (sums[0], lax.ppermute(sums[1], "dp", swap_x))
        first += count

    def left(i, *before):
        return [add_x(i, *before)] if i in halves else []

    def sent(i):
        return [parts[i]] if i in parts else []

    back_sum, back_dots = sum_rows(slots, backs, dots)

    def pieces_of(value):
        return [value[j * MICRO : (j + 1) * MICRO] for j in range(groups)]

    back_terms = return_members(pieces_of(back_sum), groups)
    dot_pieces = exchange_members(pieces_of(back_dots), groups)
    token_dots = jnp.zeros((MICRO, EXPERTS, tok_rows), f32)
    for s in range(groups // 2):
        for c in range(2):
            place = lax.rem(member // 2 + groups // 2 - s, groups // 2) * 2 + lax.rem(
                member + c, 2
            )
            label = lax.rem(place + groups - member, groups) * local_experts
            token_dots = lax.dynamic_update_slice_in_dim(
                token_dots, dot_pieces[2 * s + c], label, 1
            )
    own_gates = gates[:MICRO]
    centre = jnp.sum(own_gates * token_dots, axis=1, keepdims=True)
    grad_logits = (own_gates * (token_dots - centre)).astype(bf16)
    (mixed,) = sum_rows(after(slots, back_sum, *sent(1)), outs)
    mix_terms = return_members(pieces_of(mixed), groups)

    grad_hidden, grad_branch, grad_attended, grad_norm_moe = middle_back(
        back_terms, grad_logits, router, hidden, moe_gain, after(cot_rows, mixed, *left(2, mixed)), w_out
    )
    grad_router = jnp.einsum("bet,btd->ed", grad_logits, moe_low, preferred_element_type=f32)
    grad_out = jnp.einsum(
        "brd,bre->de", attended, grad_branch, preferred_element_type=f32
    ).astype(bf16)
    gq, gpk, gpv, gok, gov = attend_back(
        queries,
        key_value,
        prompt,
        after(bias, grad_out, *sent(4)),
        lse,
        grad_attended,
        cosine,
        sine,
    )

    def prompt_terms(value):
        return return_members(
            [value[:, j * PROMPT_DEV : (j + 1) * PROMPT_DEV] for j in range(groups)], groups
        )

    mixture = sum(term.astype(f32) for term in mix_terms)
    output = (hidden + branch_scale * mixture).astype(bf16)
    core_bit, row_bit = lax.rem(member, 2), lax.rem(member // 2, 2)
    grad_out = halve(halve(grad_out, "expert", swap_core, core_bit), "expert", swap_y, row_bit)
    gp, grad_qkv = weight_back(
        after(normed, output, *left(3, gq)),
        gq,
        gok,
        gov,
        prompt_terms(gpk),
        prompt_terms(gpv),
        cosine,
        sine,
    )
    grad_tokens, grad_norm_attn = token_back(
        after(gp, grad_qkv, *sent(2)), w_qkv, token_rows, attn_gain, grad_hidden
    )
    grad_qkv = halve(grad_qkv, "expert", swap_core, core_bit)
    last = [add_x(i, gp) for i in list(halves)]
    grad_qkv = after(grad_qkv, *last)
    grad_qkv = halve(grad_qkv, "expert", swap_y, row_bit)

    whole_sums = [parts[i] for i, (_, whole) in enumerate(plan) if whole]
    whole_sums = jnp.concatenate(whole_sums, axis=0)
    swapped = lax.ppermute(after(whole_sums[:, piece:], *last), "dp", swap_x)
    whole_sums = (whole_sums[:, :piece].astype(f32) + swapped.astype(f32)).astype(bf16)
    pieces, at = [], 0
    for i, (count, whole) in enumerate(plan):
        pieces.append(whole_sums[at : at + count] if whole else parts[i])
        at += count if whole else 0

    small = jnp.concatenate(
        [
            lax.dynamic_slice_in_dim(
                jnp.concatenate([grad_router, grad_router], axis=0),
                EXPERTS - first_expert,
                EXPERTS,
                0,
            ),
            grad_norm_attn,
            grad_norm_moe,
            jnp.zeros((6, D), f32),
        ],
        axis=0,
    )
    small = lax.psum(small, ("dp", "expert"))
    dense = after(jnp.concatenate([grad_qkv, grad_out], axis=1), *sent(3))
    dense = halve(dense, "dp", swap_x, parity)
    dense = lax.psum(dense, "dp", axis_index_groups=z_groups)
    if groups > 4:
        rest = [[m for m in range(groups) if m % 4 == r] for r in range(4)]
        dense = lax.psum(dense, "expert", axis_index_groups=rest)
    width = dense.shape[1] // 2
    left_own, right_own = dense[:, :width], dense[:, width:]
    left_x = lax.ppermute(left_own, "dp", swap_x)
    right_y = lax.ppermute(right_own, "expert", swap_y)
    left_four = [left_own, left_x] + [
        lax.ppermute(value, "expert", swap_y) for value in (left_own, left_x)
    ]
    right_x = [lax.ppermute(value, "dp", swap_x) for value in (right_own, right_y)]
    right_four = [right_own, right_x[0], right_y, right_x[1]]
    left_all = left_four + [core_swap(value, groups) for value in left_four]
    right_all = right_four + [core_swap(value, groups) for value in right_four]
    base = core_bit * 4 + row_bit * 2 + parity
    table = jnp.bitwise_xor(base, jnp.arange(8, dtype=jnp.int32)).astype(jnp.int32)
    full_qkv, full_out = finish_dense(table, left_all, right_all)

    experts_sum = jnp.concatenate(pieces, axis=0).astype(f32)
    gu_piece = D // (2 * pairs)
    return (
        output.reshape(rows_all, D),
        grad_tokens.reshape(rows_all, D),
        small[EXPERTS],
        full_qkv,
        full_out,
        small[EXPERTS + 1],
        small[:EXPERTS].T,
        experts_sum[:, :gu_piece],
        experts_sum[:, gu_piece:],
    )


def solution(mesh):
    in_specs = (
        P(("dp", "expert"), None),
        P(("dp", "expert"), None),
        P(("dp", "expert"), None),
        P(),
        P(),
        P(),
        P(),
        P(),
        P("expert", None, None),
        P("expert", None, None),
    )
    out_specs = (
        P(("dp", "expert"), None),
        P(("dp", "expert"), None),
        P(),
        P(),
        P(),
        P(),
        P(),
        P("expert", "dp", None),
        P("expert", "dp", None),
    )
    return jax.shard_map(local, mesh=mesh, in_specs=in_specs, out_specs=out_specs, check_vma=False)
```

```python
import functools

import jax
import jax.numpy as jnp
from jax import lax
from jax.experimental import pallas as pl
from jax.experimental.pallas import tpu as pltpu
from jax.sharding import PartitionSpec as P

D = 1024
HEADS = 16
KV_HEADS = 8
HEAD_DIM = 64
FF = 512
EXPERTS = 32
TOP = 8
PROMPT_DEV = 64
MICRO = 2
CAP = 100
SLOTS = 112
CHUNKS = ((1, True), (1, False), (2, False), (2, False), (1, True), (1, False))


epsilon = 1e-06
score_scale = 1.0 / 64.0
branch_scale = 0.22
masked_score = -1e30

f32 = jnp.float32
bf16 = jnp.bfloat16
vmem_limit = 60 * 1024 * 1024


def params():
    return pltpu.CompilerParams(
        vmem_limit_bytes=vmem_limit, dimension_semantics=("arbitrary",)
    )


def cost(micros):
    return pl.CostEstimate(flops=int(micros * 1.15e9), bytes_accessed=0, transcendentals=0)


def mm(left, right, dims):
    return lax.dot_general(left, right, (dims, ((), ())), preferred_element_type=f32)


def fill_one_hot(slot_rows, onehot_ref):
    experts, rows = slot_rows.shape
    place = lax.broadcasted_iota(jnp.int32, (SLOTS, rows), 0)
    for e in range(experts):
        hit = place == slot_rows[e : e + 1, :]
        onehot_ref[e * SLOTS : (e + 1) * SLOTS, :] = jnp.where(hit, 1.0, 0.0).astype(bf16)


def chosen_of(ids, count):
    rows = ids.shape[1]
    label = lax.broadcasted_iota(jnp.int32, (count, rows), 0)
    hit = ids[0:1, :] == label
    for k in range(1, ids.shape[0]):
        hit = hit | (ids[k : k + 1, :] == label)
    return hit


def select_block(row_refs, rows_ref):
    b = pl.program_id(0)
    at = 0
    for ref in row_refs:
        for i in range(ref.shape[0]):

            @pl.when(b == at)
            def _(ref=ref, i=i):
                rows_ref[...] = ref[i]

            at += 1


def store_picked(onehot_ref, rows_ref, out_ref):
    picked = mm(onehot_ref[...], rows_ref[...], ((1,), (0,))).astype(bf16)
    for e in range(out_ref.shape[0]):
        out_ref[e, 0] = picked[e * SLOTS : (e + 1) * SLOTS]


def pick_grad_body(*refs, pieces):
    ids_ref = refs[0]
    row_refs = refs[1 : 1 + pieces]
    out_ref, slot_ref, onehot_ref, rows_ref, earlier_ref = refs[1 + pieces :]
    experts, rows = slot_ref.shape[1], slot_ref.shape[2]

    @pl.when(pl.program_id(0) == 0)
    def _():
        first = lax.broadcasted_iota(jnp.int32, (rows, rows), 0)
        second = lax.broadcasted_iota(jnp.int32, (rows, rows), 1)
        earlier_ref[...] = jnp.where(first < second, 1.0, 0.0).astype(bf16)

    select_block(row_refs, rows_ref)
    hit = chosen_of(ids_ref[0], 8)
    rank = mm(jnp.where(hit, 1.0, 0.0).astype(bf16), earlier_ref[...], ((1,), (0,)))
    slots = jnp.where(hit, rank, -1.0).astype(jnp.int32)[:experts]
    slot_ref[0] = slots
    fill_one_hot(slots, onehot_ref)
    store_picked(onehot_ref, rows_ref, out_ref)


def full_spec(array):
    zeros = (0,) * array.ndim
    return pl.BlockSpec(array.shape, lambda *_: zeros)


def pick_grads(ids, pieces, experts):
    blocks, top, tok = ids.shape
    return pl.pallas_call(
        functools.partial(pick_grad_body, pieces=len(pieces)),
        grid=(blocks,),
        in_specs=[pl.BlockSpec((1, top, tok), lambda b: (b, 0, 0))]
        + [full_spec(piece) for piece in pieces],
        out_specs=[
            pl.BlockSpec((experts, 1, SLOTS, D), lambda b: (0, b, 0, 0)),
            pl.BlockSpec((1, experts, tok), lambda b: (b, 0, 0)),
        ],
        out_shape=[
            jax.ShapeDtypeStruct((experts, blocks, SLOTS, D), bf16),
            jax.ShapeDtypeStruct((blocks, experts, tok), jnp.int32),
        ],
        scratch_shapes=[
            pltpu.VMEM((experts * SLOTS, tok), bf16),
            pltpu.VMEM((tok, D), bf16),
            pltpu.VMEM((tok, tok), bf16),
        ],
        cost_estimate=cost(15),
        compiler_params=params(),
    )(ids, *pieces)


def pick_token_body(*refs, pieces):
    ids_ref, slot_ref, router_ref = refs[:3]
    row_refs = refs[3 : 3 + pieces]
    out_ref, slot_gate_ref, gate_ref, onehot_ref, rows_ref = refs[3 + pieces :]
    experts, rows = slot_ref.shape[1], slot_ref.shape[2]
    select_block(row_refs, rows_ref)
    logits = mm(router_ref[...], rows_ref[...], ((0,), (1,)))
    hit = chosen_of(ids_ref[0], EXPERTS)
    masked = jnp.where(hit, logits, masked_score)
    raised = jnp.where(hit, jnp.exp(masked - jnp.max(masked, axis=0, keepdims=True)), 0.0)
    gates = raised / jnp.sum(raised, axis=0, keepdims=True)
    gate_ref[0] = gates
    fill_one_hot(slot_ref[0], onehot_ref)
    store_picked(onehot_ref, rows_ref, out_ref)
    place = lax.broadcasted_iota(jnp.int32, (SLOTS, rows), 0)
    for e in range(experts):
        here = place == slot_ref[0, e : e + 1, :]
        gate = jnp.sum(jnp.where(here, gates[e : e + 1, :], 0.0), axis=1, keepdims=True)
        slot_gate_ref[e, 0] = jnp.broadcast_to(gate, (SLOTS, 128))


def pick_tokens(ids, slots, w_router, pieces):
    blocks, experts, tok = slots.shape
    return pl.pallas_call(
        functools.partial(pick_token_body, pieces=len(pieces)),
        grid=(blocks,),
        in_specs=[
            pl.BlockSpec((1, ids.shape[1], tok), lambda b: (b, 0, 0)),
            pl.BlockSpec((1, experts, tok), lambda b: (b, 0, 0)),
            full_spec(w_router),
        ]
        + [full_spec(piece) for piece in pieces],
        out_specs=[
            pl.BlockSpec((experts, 1, SLOTS, D), lambda b: (0, b, 0, 0)),
            pl.BlockSpec((experts, 1, SLOTS, 128), lambda b: (0, b, 0, 0)),
            pl.BlockSpec((1, EXPERTS, tok), lambda b: (b, 0, 0)),
        ],
        out_shape=[
            jax.ShapeDtypeStruct((experts, blocks, SLOTS, D), bf16),
            jax.ShapeDtypeStruct((experts, blocks, SLOTS, 128), f32),
            jax.ShapeDtypeStruct((blocks, EXPERTS, tok), f32),
        ],
        scratch_shapes=[pltpu.VMEM((experts * SLOTS, tok), bf16), pltpu.VMEM((tok, D), bf16)],
        cost_estimate=cost(17),
        compiler_params=params(),
    )(ids, slots, w_router, *pieces)


def sum_rows_body(*refs, chunks, with_dots):
    slot_ref = refs[0]
    row_refs = refs[1 : 1 + chunks]
    refs = refs[1 + chunks :]
    if with_dots:
        dot_refs, refs = refs[:chunks], refs[chunks:]
        out_ref, back_ref, onehot_ref, flat_ref = refs
    else:
        out_ref, onehot_ref, flat_ref = refs
    fill_one_hot(slot_ref[0], onehot_ref)
    e = 0
    for ref in row_refs:
        for i in range(ref.shape[0]):
            flat_ref[e * SLOTS : (e + 1) * SLOTS, :] = ref[i, 0]
            e += 1
    out_ref[0] = mm(onehot_ref[...], flat_ref[...], ((0,), (0,))).astype(bf16)
    if with_dots:
        place = lax.broadcasted_iota(jnp.int32, (SLOTS, slot_ref.shape[2]), 0)
        e = 0
        for ref in dot_refs:
            for i in range(ref.shape[0]):
                hit = place == slot_ref[0, e : e + 1, :]
                back_ref[0, e : e + 1, :] = jnp.sum(
                    jnp.where(hit, ref[i, 0, :, 0:1], 0.0), axis=0, keepdims=True
                )
                e += 1


def sum_rows(slots, rows, dots=None):
    blocks, experts, tok = slots.shape

    def chunk_spec(chunk):
        return pl.BlockSpec((chunk.shape[0], 1) + chunk.shape[2:], lambda b: (0, b, 0, 0))

    in_specs = [pl.BlockSpec((1, experts, tok), lambda b: (b, 0, 0))]
    in_specs += [chunk_spec(chunk) for chunk in rows]
    args = [slots] + rows
    out_shape = [jax.ShapeDtypeStruct((blocks, tok, D), bf16)]
    out_specs = [pl.BlockSpec((1, tok, D), lambda b: (b, 0, 0))]
    if dots is not None:
        in_specs += [chunk_spec(chunk) for chunk in dots]
        args += dots
        out_shape.append(jax.ShapeDtypeStruct((blocks, experts, tok), f32))
        out_specs.append(pl.BlockSpec((1, experts, tok), lambda b: (b, 0, 0)))
    return pl.pallas_call(
        functools.partial(sum_rows_body, chunks=len(rows), with_dots=dots is not None),
        grid=(blocks,),
        in_specs=in_specs,
        out_specs=out_specs,
        out_shape=out_shape,
        scratch_shapes=[
            pltpu.VMEM((experts * SLOTS, tok), bf16),
            pltpu.VMEM((experts * SLOTS, D), bf16),
        ],
        cost_estimate=cost(15),
        compiler_params=params(),
    )(*args)


def expert_body(
    parity_ref,
    x_ref,
    d_ref,
    gate_ref,
    wgu_ref,
    wd_ref,
    out_ref,
    back_ref,
    dots_ref,
    *part_refs,
    tile,
):
    mid_ref, grad_ref, act_ref, gu_ref, down_ref = part_refs[-5:]
    part_refs = part_refs[:-5]
    rows = x_ref.shape[1]

    def step(i, carry):
        span = pl.ds(pl.multiple_of(i * tile, tile), tile)
        hidden = mm(x_ref[0, span, :], wgu_ref[0], ((1,), (0,)))
        gate, up = hidden[:, :FF], hidden[:, FF:]
        sig = 1.0 / (1.0 + jnp.exp(-gate))
        silu = gate * sig
        middle = (silu * up).astype(bf16)
        mid_ref[span, :] = middle
        out = mm(middle, wd_ref[0], ((1,), (0,))).astype(bf16).astype(f32)
        weight = gate_ref[0, span, 0:1]
        scaled = branch_scale * d_ref[0, span, :].astype(f32)
        dots_ref[0, span, :] = jnp.broadcast_to(
            jnp.sum(scaled * out, axis=1, keepdims=True), (tile, 128)
        )
        out_ref[0, span, :] = (weight * out).astype(bf16)
        grad = (weight * scaled).astype(bf16)
        grad_ref[span, :] = grad
        grad_mid = mm(grad, wd_ref[0], ((1,), (1,)))
        act_ref[span, :FF] = (grad_mid * up * sig * (1.0 + gate * (1.0 - sig))).astype(bf16)
        act_ref[span, FF:] = (grad_mid * silu).astype(bf16)
        back_ref[0, span, :] = mm(act_ref[span, :], wgu_ref[0], ((1,), (1,))).astype(bf16)
        return carry

    lax.fori_loop(0, rows // tile, step, 0)
    gu_ref[...] = mm(x_ref[0], act_ref[...], ((0,), (0,))).astype(bf16)
    down_ref[...] = mm(mid_ref[...], grad_ref[...], ((0,), (0,))).astype(bf16)
    parity = parity_ref[0]
    pairs = part_refs[0].shape[1]
    half = (gu_ref.shape[0] + down_ref.shape[0]) // (2 * pairs)
    keep_ref, send_ref = part_refs[0], part_refs[-1]
    shift = half if len(part_refs) == 1 else 0
    start = 0
    for full in (gu_ref, down_ref):
        piece = full.shape[0] // (2 * pairs)
        for j in range(pairs):
            mine = pl.multiple_of((2 * j + parity) * piece, piece)
            other = pl.multiple_of((2 * j + 1 - parity) * piece, piece)
            keep_ref[0, j, start : start + piece, :] = full[pl.ds(mine, piece), :]
            send_ref[0, j, shift + start : shift + start + piece, :] = full[pl.ds(other, piece), :]
        start += piece


def expert_chunk(parity, first, count, pairs, split, x_rows, d_rows, slot_gate, w_gate_up, w_down):
    rows = x_rows.shape[1]
    tile = 2 * SLOTS
    mode = pl.Buffered(1 if rows > 1024 else 2)
    row_spec = pl.BlockSpec((1, rows, D), lambda e, p: (e + first, 0, 0), pipeline_mode=mode)
    col_spec = pl.BlockSpec((1, rows, 128), lambda e, p: (e + first, 0, 0))
    parts = 2 if split else 1
    piece = (D + FF) // (parts * pairs)
    part_spec = pl.BlockSpec((1, pairs, piece, D), lambda e, p: (e, 0, 0, 0))
    part_shape = jax.ShapeDtypeStruct((count, pairs, piece, D), bf16)
    out_row = pl.BlockSpec((1, rows, D), lambda e, p: (e, 0, 0))
    grid_spec = pltpu.PrefetchScalarGridSpec(
        num_scalar_prefetch=1,
        grid=(count,),
        in_specs=[
            row_spec,
            row_spec,
            col_spec,
            pl.BlockSpec((1, D, 2 * FF), lambda e, p: (e + first, 0, 0)),
            pl.BlockSpec((1, FF, D), lambda e, p: (e + first, 0, 0)),
        ],
        out_specs=[
            out_row,
            out_row,
            pl.BlockSpec((1, rows, 128), lambda e, p: (e, 0, 0)),
        ]
        + [part_spec] * parts,
        scratch_shapes=[
            pltpu.VMEM((rows, FF), bf16),
            pltpu.VMEM((rows, D), bf16),
            pltpu.VMEM((rows, 2 * FF), bf16),
            pltpu.VMEM((D, 2 * FF), bf16),
            pltpu.VMEM((FF, D), bf16),
        ],
    )
    return pl.pallas_call(
        functools.partial(expert_body, tile=tile),
        grid_spec=grid_spec,
        out_shape=[
            jax.ShapeDtypeStruct((count, rows, D), bf16),
            jax.ShapeDtypeStruct((count, rows, D), bf16),
            jax.ShapeDtypeStruct((count, rows, 128), f32),
        ]
        + [part_shape] * parts,
        cost_estimate=cost(15 * count),
        compiler_params=params(),
    )(parity, x_rows, d_rows, slot_gate, w_gate_up, w_down)


def core_swap(value, groups):
    return lax.ppermute(value, "expert", [(m, m ^ 1) for m in range(groups)])


def from_row(value, groups, shift):
    count = groups // 2
    pairs = [((((y + shift) % count) * 2 + c), y * 2 + c) for y in range(count) for c in range(2)]
    return lax.ppermute(value, "expert", pairs)


def to_row(value, groups, shift):
    count = groups // 2
    pairs = [(y * 2 + c, ((y + shift) % count) * 2 + c) for y in range(count) for c in range(2)]
    return lax.ppermute(value, "expert", pairs)


def after(value, *others):
    return lax.optimization_barrier((value,) + others)[0]


def gather_column(value, groups):
    return [value] + [from_row(value, groups, s) for s in range(1, groups // 2)]


def gather_cores(column, groups, *before):
    result = [column[0], core_swap(column[0], groups)]
    for piece in column[1:]:
        piece = after(piece, *before)
        result += [piece, core_swap(piece, groups)]
    return result


def gather_members(value, groups):
    return gather_cores(gather_column(value, groups), groups)


def return_members(pieces, groups, *before):
    swapped = [core_swap(pieces[2 * s + 1], groups) for s in range(groups // 2)]
    terms = [pieces[0], swapped[0]]
    for s in range(1, groups // 2):
        mine = after(pieces[2 * s], *before)
        both = (mine.astype(f32) + swapped[s].astype(f32)).astype(bf16)
        terms.append(to_row(both, groups, s))
    return terms


def exchange_members(pieces, groups):
    count = groups // 2
    result = []
    for s in range(count):
        for c in range(2):
            if s == 0 and c == 0:
                result.append(pieces[0])
                continue
            pairs = [
                (((y - s) % count) * 2 + (core ^ c), y * 2 + core)
                for y in range(count)
                for core in range(2)
            ]
            result.append(lax.ppermute(pieces[2 * s + c], "expert", pairs))
    return result


def lane(shape):
    return lax.broadcasted_iota(jnp.int32, shape, len(shape) - 1)


def turn(value, cosine, sine, sign):
    first = lax.rem(lane(value.shape), HEAD_DIM) < HEAD_DIM // 2
    other = jnp.where(
        first, pltpu.roll(value, 128 - HEAD_DIM // 2, 1), pltpu.roll(value, HEAD_DIM // 2, 1)
    )
    return value * cosine + sign * other * sine


def project_body(x_ref, gain_ref, w_ref, cos_ref, sin_ref, normed_ref, q_ref, kv_ref):
    x = x_ref[0].astype(f32)
    scale = lax.rsqrt(jnp.mean(x * x, axis=1, keepdims=True) + epsilon)
    normed = (x * scale * gain_ref[...]).astype(bf16)
    normed_ref[0] = normed
    cosine, sine = cos_ref[...], sin_ref[...]
    q_width, k_width = HEADS * HEAD_DIM, KV_HEADS * HEAD_DIM
    for start in range(0, q_width + 2 * k_width, 512):
        part = mm(normed, w_ref[:, start : start + 512], ((1,), (0,)))
        for inner in range(0, 512, 128):
            at = start + inner
            value = part[:, inner : inner + 128]
            if at < q_width:
                q_ref[0, :, at : at + 128] = turn(value, cosine, sine, 1.0).astype(bf16)
            elif at < q_width + k_width:
                at -= q_width
                kv_ref[0, :, at : at + 128] = turn(value, cosine, sine, 1.0).astype(bf16)
            else:
                at -= q_width
                kv_ref[0, :, at : at + 128] = value.astype(bf16)


def project(tokens, gain, w_qkv, cosine, sine):
    micro, rows, _ = tokens.shape
    block = pl.BlockSpec((1, rows, D), lambda m: (m, 0, 0))
    table = pl.BlockSpec((rows, 128), lambda m: (0, 0))
    shape = jax.ShapeDtypeStruct((micro, rows, D), bf16)
    return pl.pallas_call(
        project_body,
        grid=(micro,),
        in_specs=[
            block,
            pl.BlockSpec((1, D), lambda m: (0, 0)),
            pl.BlockSpec(w_qkv.shape, lambda m: (0, 0)),
            table,
            table,
        ],
        out_specs=[block, block, block],
        out_shape=[shape, shape, shape],
        cost_estimate=cost(7),
        compiler_params=params(),
    )(tokens, gain, w_qkv, cosine, sine)


def stack_heads(block, scale):
    wide = block.astype(f32) * scale
    result = []
    for p in range(2):
        part = wide[:, p * 128 : (p + 1) * 128]
        half = (lane(part.shape) >= HEAD_DIM) == (p == 1)
        for h in range(2):
            moved = part if h == p else pltpu.roll(part, HEAD_DIM, 1)
            result.append(jnp.where(half, moved, 0.0).astype(bf16))
    return jnp.concatenate(result, axis=0)


def unstack_heads(stacked, rows):
    result = []
    for p in range(2):
        pieces = []
        for h in range(2):
            i = 2 * p + h
            part = stacked[i * rows : (i + 1) * rows]
            pieces.append(part if h == p else pltpu.roll(part, HEAD_DIM, 1))
        result.append(jnp.where(lane(pieces[0].shape) < HEAD_DIM, pieces[0], pieces[1]))
    return result


def attend_body(
    q_ref, pk_ref, pv_ref, ok_ref, ov_ref, bias_ref, x_ref, w_ref, gain_ref,
    att_ref, lse_ref, hidden_ref, low_ref, all_ref,
):
    j = pl.program_id(0)
    rows = q_ref.shape[1]
    q = stack_heads(q_ref[0], score_scale)
    k = jnp.concatenate([pk_ref[0], ok_ref[0, PROMPT_DEV:, :]], axis=0)
    v = jnp.concatenate([pv_ref[0], ov_ref[0, PROMPT_DEV:, :]], axis=0)
    scores = mm(k, q, ((1,), (1,))) + bias_ref[...]
    largest = jnp.max(scores, axis=0, keepdims=True)
    raised = jnp.exp(scores - largest)
    total = jnp.sum(raised, axis=0, keepdims=True)
    weights = (raised * (1.0 / total)).astype(bf16)
    lse_ref[0] = largest + jnp.log(total)
    mixed = mm(v, weights, ((0,), (0,))).T
    for p, part in enumerate(unstack_heads(mixed, rows)):
        at = pl.multiple_of(j * 256 + p * 128, 128)
        att_ref[0, :, p * 128 : (p + 1) * 128] = part.astype(bf16)
        all_ref[:, pl.ds(at, 128)] = part.astype(bf16)

    @pl.when(j == pl.num_programs(0) - 1)
    def _():
        branch = mm(all_ref[...], w_ref[...], ((1,), (0,)))
        hidden = x_ref[0].astype(f32) + branch_scale * branch
        hidden_ref[0] = hidden
        scale = lax.rsqrt(jnp.mean(hidden * hidden, axis=1, keepdims=True) + epsilon)
        low_ref[0] = (hidden * scale * gain_ref[...]).astype(bf16)


def attend(micro, q, kv, prompt, bias, tokens, w_out, gain):
    rows, prompt_rows = q.shape[1], prompt.shape[1]
    steps = KV_HEADS // 2
    full = pl.BlockSpec((1, rows, D), lambda j: (micro, 0, 0))
    one = pl.BlockSpec((1, rows, D), lambda j: (0, 0, 0))
    return pl.pallas_call(
        attend_body,
        grid=(steps,),
        in_specs=[
            pl.BlockSpec((1, rows, 256), lambda j: (micro, 0, j)),
            pl.BlockSpec((1, prompt_rows, 128), lambda j: (micro, 0, j)),
            pl.BlockSpec((1, prompt_rows, 128), lambda j: (micro, 0, j + steps)),
            pl.BlockSpec((1, rows, 128), lambda j: (micro, 0, j)),
            pl.BlockSpec((1, rows, 128), lambda j: (micro, 0, j + steps)),
            pl.BlockSpec(bias.shape, lambda j: (0, 0)),
            full,
            pl.BlockSpec(w_out.shape, lambda j: (0, 0)),
            pl.BlockSpec((1, D), lambda j: (0, 0)),
        ],
        out_specs=[
            pl.BlockSpec((1, rows, 256), lambda j: (0, 0, j)),
            pl.BlockSpec((1, 1, 4 * rows), lambda j: (j, 0, 0)),
            one,
            one,
        ],
        out_shape=[
            jax.ShapeDtypeStruct((1, rows, D), bf16),
            jax.ShapeDtypeStruct((steps, 1, 4 * rows), f32),
            jax.ShapeDtypeStruct((1, rows, D), f32),
            jax.ShapeDtypeStruct((1, rows, D), bf16),
        ],
        scratch_shapes=[pltpu.VMEM((rows, D), bf16)],
        cost_estimate=cost(12),
        compiler_params=params(),
    )(q, prompt, prompt, kv, kv, bias, tokens, w_out, gain)


def norm_back(value, gain, grad):
    scale = lax.rsqrt(jnp.mean(value * value, axis=1, keepdims=True) + epsilon)
    scaled = grad * gain
    inner = jnp.mean(scaled * value, axis=1, keepdims=True)
    back = scale * scaled - value * (scale * scale * scale * inner)
    return back, jnp.sum(grad * value * scale, axis=0, keepdims=True)


def middle_body(*refs, terms):
    term_refs = refs[:terms]
    (logit_ref, router_ref, hidden_ref, gain_ref, cot_ref, w_ref) = refs[terms : terms + 6]
    grad_hidden_ref, branch_ref, att_ref, gain_out_ref = refs[terms + 6 :]
    total = mm(logit_ref[0], router_ref[...], ((0,), (1,)))
    for ref in term_refs:
        total = total + ref[0].astype(f32)
    back, gain_grad = norm_back(hidden_ref[0], gain_ref[...], total)
    grad_hidden = cot_ref[0].astype(f32) + back
    grad_hidden_ref[0] = grad_hidden
    branch = (branch_scale * grad_hidden).astype(bf16)
    branch_ref[0] = branch
    att_ref[0] = mm(branch, w_ref[...], ((1,), (1,))).astype(bf16)

    @pl.when(pl.program_id(0) == 0)
    def _():
        gain_out_ref[...] = gain_grad

    @pl.when(pl.program_id(0) != 0)
    def _():
        gain_out_ref[...] += gain_grad


def middle_back(terms, grad_logits, w_router, hidden, gain, cotangent, w_out):
    micro, rows, _ = hidden.shape
    block = pl.BlockSpec((1, rows, D), lambda m: (m, 0, 0))
    row = pl.BlockSpec((1, D), lambda m: (0, 0))
    return pl.pallas_call(
        functools.partial(middle_body, terms=len(terms)),
        grid=(micro,),
        in_specs=[block] * len(terms)
        + [
            pl.BlockSpec((1, EXPERTS, rows), lambda m: (m, 0, 0)),
            pl.BlockSpec(w_router.shape, lambda m: (0, 0)),
            block,
            row,
            block,
            pl.BlockSpec(w_out.shape, lambda m: (0, 0)),
        ],
        out_specs=[block, block, block, row],
        out_shape=[
            jax.ShapeDtypeStruct((micro, rows, D), f32),
            jax.ShapeDtypeStruct((micro, rows, D), bf16),
            jax.ShapeDtypeStruct((micro, rows, D), bf16),
            jax.ShapeDtypeStruct((1, D), f32),
        ],
        cost_estimate=cost(8),
        compiler_params=params(),
    )(*terms, grad_logits, w_router, hidden, gain, cotangent, w_out)


def attend_back_body(
    q_ref, pk_ref, pv_ref, ok_ref, ov_ref, bias_ref, lse_ref, grad_ref, cos_ref, sin_ref,
    gq_ref, gpk_ref, gpv_ref, gok_ref, gov_ref,
):
    rows, prompt_rows = q_ref.shape[1], pk_ref.shape[1]
    q = stack_heads(q_ref[0], score_scale)
    grad = stack_heads(grad_ref[0], 1.0)
    k = jnp.concatenate([pk_ref[0], ok_ref[0, PROMPT_DEV:, :]], axis=0)
    v = jnp.concatenate([pv_ref[0], ov_ref[0, PROMPT_DEV:, :]], axis=0)
    probs = jnp.exp(mm(k, q, ((1,), (1,))) + bias_ref[...] - lse_ref[0, 0])
    grad_probs = mm(v, grad, ((1,), (1,)))
    centre = jnp.sum(probs * grad_probs, axis=0, keepdims=True)
    grad_scores = (probs * (grad_probs - centre)).astype(bf16)
    grad_v = mm(probs.astype(bf16), grad, ((1,), (0,)))
    grad_k = mm(grad_scores, q, ((1,), (0,)))
    grad_q = mm(k, grad_scores, ((0,), (0,))).T * score_scale
    cosine, sine = cos_ref[...], sin_ref[...]
    for p, part in enumerate(unstack_heads(grad_q, rows)):
        gq_ref[0, :, p * 128 : (p + 1) * 128] = turn(part, cosine, sine, -1.0).astype(bf16)
    gpk_ref[0] = grad_k[:prompt_rows].astype(bf16)
    gpv_ref[0] = grad_v[:prompt_rows].astype(bf16)
    gok_ref[0] = turn(
        grad_k[prompt_rows:], cosine[PROMPT_DEV:], sine[PROMPT_DEV:], -1.0
    ).astype(bf16)
    gov_ref[0] = grad_v[prompt_rows:].astype(bf16)


def attend_back(q, kv, prompt, bias, lse, grad, cosine, sine):
    micro, rows, _ = q.shape
    prompt_rows = prompt.shape[1]
    own_rows = rows - PROMPT_DEV
    steps = KV_HEADS // 2
    wide = pl.BlockSpec((1, rows, 256), lambda m, j: (m, 0, j))
    table = pl.BlockSpec((rows, 128), lambda m, j: (0, 0))
    prompt_spec = pl.BlockSpec((1, prompt_rows, 128), lambda m, j: (m, 0, j))
    own_spec = pl.BlockSpec((1, own_rows, 128), lambda m, j: (m, 0, j))
    k_width = KV_HEADS * HEAD_DIM
    return pl.pallas_call(
        attend_back_body,
        grid=(micro, steps),
        in_specs=[
            wide,
            prompt_spec,
            pl.BlockSpec((1, prompt_rows, 128), lambda m, j: (m, 0, j + steps)),
            pl.BlockSpec((1, rows, 128), lambda m, j: (m, 0, j)),
            pl.BlockSpec((1, rows, 128), lambda m, j: (m, 0, j + steps)),
            pl.BlockSpec(bias.shape, lambda m, j: (0, 0)),
            pl.BlockSpec((1, 1, 1, 4 * rows), lambda m, j: (m, j, 0, 0)),
            wide,
            table,
            table,
        ],
        out_specs=[wide, prompt_spec, prompt_spec, own_spec, own_spec],
        out_shape=[
            jax.ShapeDtypeStruct((micro, rows, D), bf16),
            jax.ShapeDtypeStruct((micro, prompt_rows, k_width), bf16),
            jax.ShapeDtypeStruct((micro, prompt_rows, k_width), bf16),
            jax.ShapeDtypeStruct((micro, own_rows, k_width), bf16),
            jax.ShapeDtypeStruct((micro, own_rows, k_width), bf16),
        ],
        cost_estimate=cost(23),
        compiler_params=pltpu.CompilerParams(
            vmem_limit_bytes=vmem_limit, dimension_semantics=("arbitrary", "arbitrary")
        ),
    )(q, prompt, prompt, kv, kv, bias, lse, grad, cosine, sine)


def weight_body(*refs, terms):
    normed_ref, gq_ref, gok_ref, gov_ref = refs[:4]
    k_terms, v_terms = refs[4 : 4 + terms], refs[4 + terms : 4 + 2 * terms]
    cos_ref, sin_ref, gp_ref, out_ref, acc_ref = refs[4 + 2 * terms :]
    q_width, k_width = HEADS * HEAD_DIM, KV_HEADS * HEAD_DIM
    gp_ref[0, :, :q_width] = gq_ref[0]
    gp_ref[0, PROMPT_DEV:, q_width : q_width + k_width] = gok_ref[0]
    gp_ref[0, PROMPT_DEV:, q_width + k_width :] = gov_ref[0]
    prompt_k, prompt_v = [sum(ref[0].astype(f32) for ref in group) for group in (k_terms, v_terms)]
    cosine, sine = cos_ref[:PROMPT_DEV, :], sin_ref[:PROMPT_DEV, :]
    for at in range(0, k_width, 128):
        turned = turn(prompt_k[:, at : at + 128], cosine, sine, -1.0)
        gp_ref[0, :PROMPT_DEV, q_width + at : q_width + at + 128] = turned.astype(bf16)
    gp_ref[0, :PROMPT_DEV, q_width + k_width :] = prompt_v.astype(bf16)
    part = mm(normed_ref[0], gp_ref[0], ((0,), (0,)))
    m = pl.program_id(0)

    @pl.when(m == 0)
    def _():
        acc_ref[...] = part

    @pl.when(m != 0)
    def _():
        acc_ref[...] += part

    @pl.when(m == pl.num_programs(0) - 1)
    def _():
        out_ref[...] = acc_ref[...].astype(bf16)


def weight_back(normed, gq, gok, gov, k_terms, v_terms, cosine, sine):
    micro, rows, _ = normed.shape
    k_width = KV_HEADS * HEAD_DIM
    wide = pl.BlockSpec((1, rows, D), lambda m: (m, 0, 0))
    own = pl.BlockSpec((1, rows - PROMPT_DEV, k_width), lambda m: (m, 0, 0))
    term = pl.BlockSpec((1, PROMPT_DEV, k_width), lambda m: (m, 0, 0))
    table = pl.BlockSpec((rows, 128), lambda m: (0, 0))
    return pl.pallas_call(
        functools.partial(weight_body, terms=len(k_terms)),
        grid=(micro,),
        in_specs=[wide, wide, own, own] + [term] * (2 * len(k_terms)) + [table, table],
        out_specs=[
            pl.BlockSpec((1, rows, 2 * D), lambda m: (m, 0, 0)),
            pl.BlockSpec((D, 2 * D), lambda m: (0, 0)),
        ],
        out_shape=[
            jax.ShapeDtypeStruct((micro, rows, 2 * D), bf16),
            jax.ShapeDtypeStruct((D, 2 * D), bf16),
        ],
        scratch_shapes=[pltpu.VMEM((D, 2 * D), f32)],
        cost_estimate=cost(11),
        compiler_params=params(),
    )(normed, gq, gok, gov, *k_terms, *v_terms, cosine, sine)


def token_body(gp_ref, w_ref, x_ref, gain_ref, hidden_ref, out_ref, gain_out_ref):
    grad = mm(gp_ref[0], w_ref[...], ((1,), (1,)))
    back, gain_grad = norm_back(x_ref[0].astype(f32), gain_ref[...], grad)
    out_ref[0] = (hidden_ref[0] + back).astype(bf16)

    @pl.when(pl.program_id(0) == 0)
    def _():
        gain_out_ref[...] = gain_grad

    @pl.when(pl.program_id(0) != 0)
    def _():
        gain_out_ref[...] += gain_grad


def token_back(gp, w_qkv, tokens, gain, grad_hidden):
    micro, rows, _ = tokens.shape
    block = pl.BlockSpec((1, rows, D), lambda m: (m, 0, 0))
    row = pl.BlockSpec((1, D), lambda m: (0, 0))
    return pl.pallas_call(
        token_body,
        grid=(micro,),
        in_specs=[
            pl.BlockSpec((1, rows, 2 * D), lambda m: (m, 0, 0)),
            pl.BlockSpec(w_qkv.shape, lambda m: (0, 0)),
            block,
            row,
            block,
        ],
        out_specs=[block, row],
        out_shape=[
            jax.ShapeDtypeStruct((micro, rows, D), bf16),
            jax.ShapeDtypeStruct((1, D), f32),
        ],
        cost_estimate=cost(8),
        compiler_params=params(),
    )(gp, w_qkv, tokens, gain, grad_hidden)


def halve(value, axis, swap, bit):
    rows = value.shape[0] // 2
    keep = lax.dynamic_slice_in_dim(value, bit * rows, rows, 0)
    send = lax.dynamic_slice_in_dim(value, (1 - bit) * rows, rows, 0)
    got = lax.ppermute(send, axis, swap)
    return (keep.astype(f32) + got.astype(f32)).astype(bf16)


def finish_dense_body(table_ref, *refs, pieces):
    first_refs, second_refs = refs[:pieces], refs[pieces : 2 * pieces]
    qkv_ref, out_ref = refs[2 * pieces :]
    width = first_refs[0].shape[1]
    rest = qkv_ref.shape[1] - width
    for i in range(pieces):

        @pl.when(pl.program_id(0) == i)
        def _(i=i):
            qkv_ref[:, :width] = first_refs[i][...].astype(f32)
            qkv_ref[:, width:] = second_refs[i][:, :rest].astype(f32)
            out_ref[...] = second_refs[i][:, rest:].astype(f32)


def finish_dense(table, first, second):
    pieces = len(first)
    height = first[0].shape[0]
    grid_spec = pltpu.PrefetchScalarGridSpec(
        num_scalar_prefetch=1,
        grid=(pieces,),
        in_specs=[full_spec(piece) for piece in first + second],
        out_specs=[
            pl.BlockSpec((height, 2 * D), lambda i, t: (t[i], 0)),
            pl.BlockSpec((height, D), lambda i, t: (t[i], 0)),
        ],
    )
    return pl.pallas_call(
        functools.partial(finish_dense_body, pieces=pieces),
        grid_spec=grid_spec,
        out_shape=[
            jax.ShapeDtypeStruct((pieces * height, 2 * D), f32),
            jax.ShapeDtypeStruct((pieces * height, D), f32),
        ],
        cost_estimate=cost(9),
        compiler_params=params(),
    )(table, *first, *second)


def local(
    tokens, cotangent, expert_ids, norm_attn, w_qkv, w_out, norm_moe, w_router, w_gate_up, w_down
):
    groups = lax.axis_size("expert")
    dp_size = lax.axis_size("dp")
    member = lax.axis_index("expert")
    dp_index = lax.axis_index("dp")
    rows_all = tokens.shape[0]
    tok_rows = rows_all // MICRO
    local_experts = w_gate_up.shape[0]
    prompt_len = PROMPT_DEV * groups
    k_width = KV_HEADS * HEAD_DIM
    pairs = dp_size // 2
    blocks = groups * MICRO
    attn_gain = norm_attn.reshape(1, D)
    moe_gain = norm_moe.reshape(1, D)
    token_rows = tokens.reshape(MICRO, tok_rows, D)
    cot_rows = cotangent.reshape(MICRO, tok_rows, D)

    local_index = jnp.arange(tok_rows, dtype=jnp.int32)
    positions = jnp.where(
        local_index < PROMPT_DEV,
        member * PROMPT_DEV + local_index,
        prompt_len + local_index - PROMPT_DEV,
    )
    half_dim = HEAD_DIM // 2
    inverse = 10000.0 ** (-2.0 * jnp.arange(half_dim, dtype=f32) / HEAD_DIM)
    angles = positions.astype(f32)[:, None] * inverse[None, :]
    cosine = jnp.tile(jnp.cos(angles), (1, 128 // half_dim))
    sine = jnp.tile(jnp.sin(angles), (1, 128 // half_dim))
    sine = jnp.where(jnp.arange(128)[None, :] % HEAD_DIM < half_dim, -sine, sine)
    rows_of = []
    for s in range(groups // 2):
        for c in range(2):
            place = lax.rem(member // 2 + s, groups // 2) * 2 + lax.rem(member + c, 2)
            rows_of.append(place * PROMPT_DEV + jnp.arange(PROMPT_DEV, dtype=jnp.int32))
    key_positions = jnp.concatenate(
        rows_of + [prompt_len + jnp.arange(tok_rows - PROMPT_DEV, dtype=jnp.int32)]
    )
    bias = jnp.where(
        key_positions[:, None] <= jnp.tile(positions, HEADS // (KV_HEADS // 2))[None, :],
        0.0,
        masked_score,
    )

    first_expert = member * local_experts
    ids_t = gather_members(expert_ids.reshape(MICRO, tok_rows, TOP).transpose(0, 2, 1), groups)
    ids_all = lax.rem(jnp.concatenate(ids_t, axis=0) + (EXPERTS - first_expert), EXPERTS)
    cot_pieces = [gather_members(cot_rows[:1], groups)]
    normed, queries, key_value = project(token_rows, attn_gain, w_qkv, cosine, sine)
    prompt_pieces = gather_members(key_value[:, :PROMPT_DEV], groups)
    prompt = jnp.concatenate(prompt_pieces, axis=1)
    cot_pieces += [
        gather_members(after(cot_rows[m : m + 1], prompt_pieces[2]), groups)
        for m in range(1, MICRO)
    ]
    router = lax.dynamic_slice_in_dim(
        jnp.concatenate([w_router, w_router], axis=1), first_expert, EXPERTS, 1
    )

    attended, lse, hidden, moe_pieces, moe_low = [], [], [], [], []
    for m in range(MICRO):
        mask = after(bias, cot_pieces[0][2] if m == 0 else moe_low[-1])
        att, log_total, hid, low = attend(
            m, queries, key_value, prompt, mask, token_rows, w_out, moe_gain
        )
        attended.append(att)
        lse.append(log_total[None])
        hidden.append(hid)
        moe_low.append(low)
        moe_pieces.append(gather_column(low, groups))

    def by_block(pieces):
        return [pieces[m][g] for g in range(groups) for m in range(MICRO)]

    d_rows, slots = pick_grads(after(ids_all, moe_low[-1]), by_block(cot_pieces), local_experts)
    moe_pieces = [gather_cores(column, groups, slots) for column in moe_pieces]
    attended = jnp.concatenate(attended, axis=0)
    lse = jnp.concatenate(lse, axis=0)
    hidden = jnp.concatenate(hidden, axis=0)
    moe_low = jnp.concatenate(moe_low, axis=0)

    x_rows, slot_gate, gates = pick_tokens(ids_all, slots, router, by_block(moe_pieces))
    slot_rows = blocks * SLOTS
    x_rows = x_rows.reshape(local_experts, slot_rows, D)
    d_rows = d_rows.reshape(local_experts, slot_rows, D)
    slot_gate = slot_gate.reshape(local_experts, slot_rows, 128)
    parity = lax.rem(dp_index, 2).astype(jnp.int32)
    swap_x = [(d, d ^ 1) for d in range(dp_size)]
    swap_y = [(m, m ^ 2) for m in range(groups)]
    swap_core = [(m, m ^ 1) for m in range(groups)]
    z_groups = [[d for d in range(dp_size) if d % 2 == r] for r in range(2)]
    piece = (D + FF) // (2 * pairs)

    def sum_z(value):
        count, _, height, _ = value.shape
        return lax.psum_scatter(
            value.reshape(count, pairs * height, D),
            "dp",
            scatter_dimension=1,
            axis_index_groups=z_groups,
            tiled=True,
        )

    plan = CHUNKS
    if sum(count for count, _ in plan) != local_experts:
        plan = tuple((1, e == 0) for e in range(local_experts))
    outs, backs, dots, halves, parts = [], [], [], {}, {}

    def add_x(i, *before):
        keep, got = halves.pop(i)
        got = after(got, *before)
        half = (keep.astype(f32) + got.astype(f32)).astype(bf16)
        parts[i] = sum_z(half)
        return half

    first = 0
    order = parity.reshape(1)
    for i, (count, whole) in enumerate(plan):
        if i:
            order = after(order, outs[-1])
        if i == 3:
            order = after(order, add_x(1, outs[-1]))
        if i == 4:
            order = after(order, parts[0])
        out, back, dot, *sums = expert_chunk(
            order, first, count, pairs, not whole, x_rows, d_rows, slot_gate, w_gate_up, w_down
        )
        shape = (count, blocks, SLOTS)
        outs.append(out.reshape(shape + (D,)))
        backs.append(back.reshape(shape + (D,)))
        dots.append(dot.reshape(shape + (128,)))
        if whole:
            parts[i] = sum_z(sums[0])
        else:
            halves[i] = (sums[0], lax.ppermute(sums[1], "dp", swap_x))
        first += count

    def left(i, *before):
        return [add_x(i, *before)] if i in halves else []

    def sent(i):
        return [parts[i]] if i in parts else []

    back_sum, back_dots = sum_rows(slots, backs, dots)

    def pieces_of(value):
        return [value[j * MICRO : (j + 1) * MICRO] for j in range(groups)]

    dot_pieces = exchange_members(pieces_of(back_dots), groups)
    back_terms = return_members(pieces_of(back_sum), groups, *dot_pieces)
    token_dots = jnp.zeros((MICRO, EXPERTS, tok_rows), f32)
    for s in range(groups // 2):
        for c in range(2):
            place = lax.rem(member // 2 + groups // 2 - s, groups // 2) * 2 + lax.rem(
                member + c, 2
            )
            label = lax.rem(place + groups - member, groups) * local_experts
            token_dots = lax.dynamic_update_slice_in_dim(
                token_dots, dot_pieces[2 * s + c], label, 1
            )
    own_gates = gates[:MICRO]
    centre = jnp.sum(own_gates * token_dots, axis=1, keepdims=True)
    grad_logits = (own_gates * (token_dots - centre)).astype(bf16)
    (mixed,) = sum_rows(after(slots, back_sum, *sent(1), *left(2, back_sum)), outs)
    mix_terms = return_members(pieces_of(mixed), groups)

    grad_hidden, grad_branch, grad_attended, grad_norm_moe = middle_back(
        back_terms, grad_logits, router, hidden, moe_gain, after(cot_rows, mixed, *sent(4)), w_out
    )
    grad_router = jnp.einsum("bet,btd->ed", grad_logits, moe_low, preferred_element_type=f32)
    grad_out = jnp.einsum(
        "brd,bre->de", attended, grad_branch, preferred_element_type=f32
    ).astype(bf16)
    gq, gpk, gpv, gok, gov = attend_back(
        queries,
        key_value,
        prompt,
        after(bias, grad_out),
        lse,
        grad_attended,
        cosine,
        sine,
    )

    def prompt_terms(value):
        return return_members(
            [value[:, j * PROMPT_DEV : (j + 1) * PROMPT_DEV] for j in range(groups)], groups
        )

    mixture = sum(after(term, gq).astype(f32) for term in mix_terms)
    output = (hidden + branch_scale * mixture).astype(bf16)
    core_bit, row_bit = lax.rem(member, 2), lax.rem(member // 2, 2)
    grad_out = halve(halve(grad_out, "expert", swap_core, core_bit), "expert", swap_y, row_bit)
    gp, grad_qkv = weight_back(
        after(normed, output, grad_out, *left(3, gq)),
        gq,
        gok,
        gov,
        prompt_terms(gpk),
        prompt_terms(gpv),
        cosine,
        sine,
    )
    grad_tokens, grad_norm_attn = token_back(
        after(gp, grad_qkv), w_qkv, token_rows, attn_gain, grad_hidden
    )
    last = [add_x(i, grad_norm_attn) for i in list(halves)]
    grad_qkv = halve(grad_qkv, "expert", swap_core, core_bit)
    grad_qkv = halve(grad_qkv, "expert", swap_y, row_bit)

    whole_sums = [parts[i] for i, (_, whole) in enumerate(plan) if whole]
    whole_sums = jnp.concatenate(whole_sums, axis=0)
    swapped = lax.ppermute(after(whole_sums[:, piece:], *last), "dp", swap_x)
    whole_sums = (whole_sums[:, :piece].astype(f32) + swapped.astype(f32)).astype(bf16)
    pieces, at = [], 0
    for i, (count, whole) in enumerate(plan):
        pieces.append(whole_sums[at : at + count] if whole else parts[i])
        at += count if whole else 0

    small = jnp.concatenate(
        [
            lax.dynamic_slice_in_dim(
                jnp.concatenate([grad_router, grad_router], axis=0),
                EXPERTS - first_expert,
                EXPERTS,
                0,
            ),
            grad_norm_attn,
            grad_norm_moe,
            jnp.zeros((14, D), f32),
        ],
        axis=0,
    )
    small = after(small, *last)
    for axis, swap in (("expert", swap_core), ("expert", swap_y), ("dp", swap_x)):
        small = small + lax.ppermute(small, axis, swap)
    dense = jnp.concatenate([grad_qkv, grad_out], axis=1)
    dense = after(halve(dense, "dp", swap_x, parity), *sent(2), *sent(3))
    dense_rows = dense.shape[0]
    dense = jnp.concatenate([dense, small.reshape(-1, 3 * D).astype(bf16)], axis=0)
    dense = lax.psum(dense, "dp", axis_index_groups=z_groups)
    if groups > 4:
        rest = [[m for m in range(groups) if m % 4 == r] for r in range(4)]
        dense = lax.psum(dense, "expert", axis_index_groups=rest)
    small = dense[dense_rows:].reshape(-1, D).astype(f32)
    dense = dense[:dense_rows]
    width = dense.shape[1] // 2
    left_own, right_own = dense[:, :width], dense[:, width:]
    left_x = lax.ppermute(left_own, "dp", swap_x)
    right_y = lax.ppermute(right_own, "expert", swap_y)
    left_four = [left_own, left_x] + [
        lax.ppermute(value, "expert", swap_y) for value in (left_own, left_x)
    ]
    right_x = [lax.ppermute(value, "dp", swap_x) for value in (right_own, right_y)]
    right_four = [right_own, right_x[0], right_y, right_x[1]]
    left_all = left_four + [core_swap(value, groups) for value in left_four]
    right_all = right_four + [core_swap(value, groups) for value in right_four]
    base = core_bit * 4 + row_bit * 2 + parity
    table = jnp.bitwise_xor(base, jnp.arange(8, dtype=jnp.int32)).astype(jnp.int32)
    full_qkv, full_out = finish_dense(table, left_all, right_all)

    experts_sum = jnp.concatenate(pieces, axis=0).astype(f32)
    gu_piece = D // (2 * pairs)
    return (
        output.reshape(rows_all, D),
        grad_tokens.reshape(rows_all, D),
        small[EXPERTS],
        full_qkv,
        full_out,
        small[EXPERTS + 1],
        small[:EXPERTS].T,
        experts_sum[:, :gu_piece],
        experts_sum[:, gu_piece:],
    )


def solution(mesh):
    in_specs = (
        P(("dp", "expert"), None),
        P(("dp", "expert"), None),
        P(("dp", "expert"), None),
        P(),
        P(),
        P(),
        P(),
        P(),
        P("expert", None, None),
        P("expert", None, None),
    )
    out_specs = (
        P(("dp", "expert"), None),
        P(("dp", "expert"), None),
        P(),
        P(),
        P(),
        P(),
        P(),
        P("expert", "dp", None),
        P("expert", "dp", None),
    )
    return jax.shard_map(local, mesh=mesh, in_specs=in_specs, out_specs=out_specs, check_vma=False)
```

```python
import functools

import jax
import jax.numpy as jnp
from jax import lax
from jax.experimental import pallas as pl
from jax.experimental.pallas import tpu as pltpu
from jax.sharding import PartitionSpec as P

D = 1024
HEADS = 16
KV_HEADS = 8
HEAD_DIM = 64
FF = 512
EXPERTS = 32
TOP = 8
PROMPT_DEV = 64
MICRO = 2
CAP = 100
SLOTS = 112
CHUNKS = ((1, True), (1, False), (2, False), (2, False), (1, True), (1, False))


epsilon = 1e-06
score_scale = 1.0 / 64.0
branch_scale = 0.22
masked_score = -1e30

f32 = jnp.float32
bf16 = jnp.bfloat16
vmem_limit = 60 * 1024 * 1024


def params():
    return pltpu.CompilerParams(
        vmem_limit_bytes=vmem_limit, dimension_semantics=("arbitrary",)
    )


def cost(micros):
    return pl.CostEstimate(flops=int(micros * 1.15e9), bytes_accessed=0, transcendentals=0)


def mm(left, right, dims):
    return lax.dot_general(left, right, (dims, ((), ())), preferred_element_type=f32)


def fill_one_hot(slot_rows, onehot_ref):
    experts, rows = slot_rows.shape
    place = lax.broadcasted_iota(jnp.int32, (SLOTS, rows), 0)
    for e in range(experts):
        hit = place == slot_rows[e : e + 1, :]
        onehot_ref[e * SLOTS : (e + 1) * SLOTS, :] = jnp.where(hit, 1.0, 0.0).astype(bf16)


def chosen_of(ids, count):
    rows = ids.shape[1]
    label = lax.broadcasted_iota(jnp.int32, (count, rows), 0)
    hit = ids[0:1, :] == label
    for k in range(1, ids.shape[0]):
        hit = hit | (ids[k : k + 1, :] == label)
    return hit


def select_block(row_refs, rows_ref):
    b = pl.program_id(0)
    at = 0
    for ref in row_refs:
        for i in range(ref.shape[0]):

            @pl.when(b == at)
            def _(ref=ref, i=i):
                rows_ref[...] = ref[i]

            at += 1


def store_picked(onehot_ref, rows_ref, out_ref):
    picked = mm(onehot_ref[...], rows_ref[...], ((1,), (0,))).astype(bf16)
    for e in range(out_ref.shape[0]):
        out_ref[e, 0] = picked[e * SLOTS : (e + 1) * SLOTS]


def pick_grad_body(*refs, pieces):
    ids_ref = refs[0]
    row_refs = refs[1 : 1 + pieces]
    out_ref, slot_ref, onehot_ref, rows_ref, earlier_ref = refs[1 + pieces :]
    experts, rows = slot_ref.shape[1], slot_ref.shape[2]

    @pl.when(pl.program_id(0) == 0)
    def _():
        first = lax.broadcasted_iota(jnp.int32, (rows, rows), 0)
        second = lax.broadcasted_iota(jnp.int32, (rows, rows), 1)
        earlier_ref[...] = jnp.where(first < second, 1.0, 0.0).astype(bf16)

    select_block(row_refs, rows_ref)
    hit = chosen_of(ids_ref[0], 8)
    rank = mm(jnp.where(hit, 1.0, 0.0).astype(bf16), earlier_ref[...], ((1,), (0,)))
    slots = jnp.where(hit, rank, -1.0).astype(jnp.int32)[:experts]
    slot_ref[0] = slots
    fill_one_hot(slots, onehot_ref)
    store_picked(onehot_ref, rows_ref, out_ref)


def full_spec(array):
    zeros = (0,) * array.ndim
    return pl.BlockSpec(array.shape, lambda *_: zeros)


def pick_grads(ids, pieces, experts):
    blocks, top, tok = ids.shape
    return pl.pallas_call(
        functools.partial(pick_grad_body, pieces=len(pieces)),
        grid=(blocks,),
        in_specs=[pl.BlockSpec((1, top, tok), lambda b: (b, 0, 0))]
        + [full_spec(piece) for piece in pieces],
        out_specs=[
            pl.BlockSpec((experts, 1, SLOTS, D), lambda b: (0, b, 0, 0)),
            pl.BlockSpec((1, experts, tok), lambda b: (b, 0, 0)),
        ],
        out_shape=[
            jax.ShapeDtypeStruct((experts, blocks, SLOTS, D), bf16),
            jax.ShapeDtypeStruct((blocks, experts, tok), jnp.int32),
        ],
        scratch_shapes=[
            pltpu.VMEM((experts * SLOTS, tok), bf16),
            pltpu.VMEM((tok, D), bf16),
            pltpu.VMEM((tok, tok), bf16),
        ],
        cost_estimate=cost(15),
        compiler_params=params(),
    )(ids, *pieces)


def pick_token_body(*refs, pieces):
    ids_ref, slot_ref, router_ref = refs[:3]
    row_refs = refs[3 : 3 + pieces]
    out_ref, slot_gate_ref, gate_ref, onehot_ref, rows_ref = refs[3 + pieces :]
    experts, rows = slot_ref.shape[1], slot_ref.shape[2]
    select_block(row_refs, rows_ref)
    logits = mm(router_ref[...], rows_ref[...], ((0,), (1,)))
    hit = chosen_of(ids_ref[0], EXPERTS)
    masked = jnp.where(hit, logits, masked_score)
    raised = jnp.where(hit, jnp.exp(masked - jnp.max(masked, axis=0, keepdims=True)), 0.0)
    gates = raised / jnp.sum(raised, axis=0, keepdims=True)
    gate_ref[0] = gates
    fill_one_hot(slot_ref[0], onehot_ref)
    store_picked(onehot_ref, rows_ref, out_ref)
    place = lax.broadcasted_iota(jnp.int32, (SLOTS, rows), 0)
    for e in range(experts):
        here = place == slot_ref[0, e : e + 1, :]
        gate = jnp.sum(jnp.where(here, gates[e : e + 1, :], 0.0), axis=1, keepdims=True)
        slot_gate_ref[e, 0] = jnp.broadcast_to(gate, (SLOTS, 128))


def pick_tokens(ids, slots, w_router, pieces):
    blocks, experts, tok = slots.shape
    return pl.pallas_call(
        functools.partial(pick_token_body, pieces=len(pieces)),
        grid=(blocks,),
        in_specs=[
            pl.BlockSpec((1, ids.shape[1], tok), lambda b: (b, 0, 0)),
            pl.BlockSpec((1, experts, tok), lambda b: (b, 0, 0)),
            full_spec(w_router),
        ]
        + [full_spec(piece) for piece in pieces],
        out_specs=[
            pl.BlockSpec((experts, 1, SLOTS, D), lambda b: (0, b, 0, 0)),
            pl.BlockSpec((experts, 1, SLOTS, 128), lambda b: (0, b, 0, 0)),
            pl.BlockSpec((1, EXPERTS, tok), lambda b: (b, 0, 0)),
        ],
        out_shape=[
            jax.ShapeDtypeStruct((experts, blocks, SLOTS, D), bf16),
            jax.ShapeDtypeStruct((experts, blocks, SLOTS, 128), f32),
            jax.ShapeDtypeStruct((blocks, EXPERTS, tok), f32),
        ],
        scratch_shapes=[pltpu.VMEM((experts * SLOTS, tok), bf16), pltpu.VMEM((tok, D), bf16)],
        cost_estimate=cost(17),
        compiler_params=params(),
    )(ids, slots, w_router, *pieces)


def sum_rows_body(*refs, chunks, with_dots):
    slot_ref = refs[0]
    row_refs = refs[1 : 1 + chunks]
    refs = refs[1 + chunks :]
    if with_dots:
        dot_refs, refs = refs[:chunks], refs[chunks:]
        back_ref, onehot_ref, flat_ref = refs[-3:]
        out_refs = refs[:-3]
    else:
        onehot_ref, flat_ref = refs[-2:]
        out_refs = refs[:-2]
    fill_one_hot(slot_ref[0], onehot_ref)
    e = 0
    for ref in row_refs:
        for i in range(ref.shape[0]):
            flat_ref[e * SLOTS : (e + 1) * SLOTS, :] = ref[i, 0]
            e += 1
    total = mm(onehot_ref[...], flat_ref[...], ((0,), (0,))).astype(bf16)
    for j, out_ref in enumerate(out_refs):

        @pl.when(pl.program_id(0) // MICRO == j)
        def _(out_ref=out_ref):
            out_ref[0] = total

    if with_dots:
        place = lax.broadcasted_iota(jnp.int32, (SLOTS, slot_ref.shape[2]), 0)
        e = 0
        for ref in dot_refs:
            for i in range(ref.shape[0]):
                hit = place == slot_ref[0, e : e + 1, :]
                back_ref[0, e : e + 1, :] = jnp.sum(
                    jnp.where(hit, ref[i, 0, :, 0:1], 0.0), axis=0, keepdims=True
                )
                e += 1


def sum_rows(slots, rows, dots=None):
    blocks, experts, tok = slots.shape

    def chunk_spec(chunk):
        return pl.BlockSpec((chunk.shape[0], 1) + chunk.shape[2:], lambda b: (0, b, 0, 0))

    in_specs = [pl.BlockSpec((1, experts, tok), lambda b: (b, 0, 0))]
    in_specs += [chunk_spec(chunk) for chunk in rows]
    args = [slots] + rows
    members = blocks // MICRO

    def member_spec(j):
        return pl.BlockSpec(
            (1, tok, D), lambda b: (jnp.clip(b - j * MICRO, 0, MICRO - 1), 0, 0)
        )

    out_shape = [jax.ShapeDtypeStruct((MICRO, tok, D), bf16)] * members
    out_specs = [member_spec(j) for j in range(members)]
    if dots is not None:
        in_specs += [chunk_spec(chunk) for chunk in dots]
        args += dots
        out_shape.append(jax.ShapeDtypeStruct((blocks, experts, tok), f32))
        out_specs.append(pl.BlockSpec((1, experts, tok), lambda b: (b, 0, 0)))
    return pl.pallas_call(
        functools.partial(sum_rows_body, chunks=len(rows), with_dots=dots is not None),
        grid=(blocks,),
        in_specs=in_specs,
        out_specs=out_specs,
        out_shape=out_shape,
        scratch_shapes=[
            pltpu.VMEM((experts * SLOTS, tok), bf16),
            pltpu.VMEM((experts * SLOTS, D), bf16),
        ],
        cost_estimate=cost(15),
        compiler_params=params(),
    )(*args)


def expert_body(
    parity_ref,
    x_ref,
    d_ref,
    gate_ref,
    wgu_ref,
    wd_ref,
    out_ref,
    back_ref,
    dots_ref,
    *part_refs,
    tile,
):
    mid_ref, grad_ref, act_ref, gu_ref, down_ref = part_refs[-5:]
    part_refs = part_refs[:-5]
    rows = x_ref.shape[1]

    def step(i, carry):
        span = pl.ds(pl.multiple_of(i * tile, tile), tile)
        hidden = mm(x_ref[0, span, :], wgu_ref[0], ((1,), (0,)))
        gate, up = hidden[:, :FF], hidden[:, FF:]
        sig = 1.0 / (1.0 + jnp.exp(-gate))
        silu = gate * sig
        middle = (silu * up).astype(bf16)
        mid_ref[span, :] = middle
        out = mm(middle, wd_ref[0], ((1,), (0,))).astype(bf16).astype(f32)
        weight = gate_ref[0, span, 0:1]
        scaled = branch_scale * d_ref[0, span, :].astype(f32)
        dots_ref[0, span, :] = jnp.broadcast_to(
            jnp.sum(scaled * out, axis=1, keepdims=True), (tile, 128)
        )
        out_ref[0, span, :] = (weight * out).astype(bf16)
        grad = (weight * scaled).astype(bf16)
        grad_ref[span, :] = grad
        grad_mid = mm(grad, wd_ref[0], ((1,), (1,)))
        act_ref[span, :FF] = (grad_mid * up * sig * (1.0 + gate * (1.0 - sig))).astype(bf16)
        act_ref[span, FF:] = (grad_mid * silu).astype(bf16)
        back_ref[0, span, :] = mm(act_ref[span, :], wgu_ref[0], ((1,), (1,))).astype(bf16)
        return carry

    lax.fori_loop(0, rows // tile, step, 0)
    gu_ref[...] = mm(x_ref[0], act_ref[...], ((0,), (0,))).astype(bf16)
    down_ref[...] = mm(mid_ref[...], grad_ref[...], ((0,), (0,))).astype(bf16)
    parity = parity_ref[0]
    pairs = part_refs[0].shape[1]
    half = (gu_ref.shape[0] + down_ref.shape[0]) // (2 * pairs)
    keep_ref, send_ref = part_refs[0], part_refs[-1]
    shift = half if len(part_refs) == 1 else 0
    start = 0
    for full in (gu_ref, down_ref):
        piece = full.shape[0] // (2 * pairs)
        for j in range(pairs):
            mine = pl.multiple_of((2 * j + parity) * piece, piece)
            other = pl.multiple_of((2 * j + 1 - parity) * piece, piece)
            keep_ref[0, j, start : start + piece, :] = full[pl.ds(mine, piece), :]
            send_ref[0, j, shift + start : shift + start + piece, :] = full[pl.ds(other, piece), :]
        start += piece


def expert_chunk(parity, first, count, pairs, split, x_rows, d_rows, slot_gate, w_gate_up, w_down):
    rows = x_rows.shape[1]
    tile = 2 * SLOTS
    mode = pl.Buffered(1 if rows > 1024 else 2)
    row_spec = pl.BlockSpec((1, rows, D), lambda e, p: (e + first, 0, 0), pipeline_mode=mode)
    col_spec = pl.BlockSpec((1, rows, 128), lambda e, p: (e + first, 0, 0))
    parts = 2 if split else 1
    piece = (D + FF) // (parts * pairs)
    part_spec = pl.BlockSpec((1, pairs, piece, D), lambda e, p: (e, 0, 0, 0))
    part_shape = jax.ShapeDtypeStruct((count, pairs, piece, D), bf16)
    out_row = pl.BlockSpec((1, rows, D), lambda e, p: (e, 0, 0))
    grid_spec = pltpu.PrefetchScalarGridSpec(
        num_scalar_prefetch=1,
        grid=(count,),
        in_specs=[
            row_spec,
            row_spec,
            col_spec,
            pl.BlockSpec((1, D, 2 * FF), lambda e, p: (e + first, 0, 0)),
            pl.BlockSpec((1, FF, D), lambda e, p: (e + first, 0, 0)),
        ],
        out_specs=[
            out_row,
            out_row,
            pl.BlockSpec((1, rows, 128), lambda e, p: (e, 0, 0)),
        ]
        + [part_spec] * parts,
        scratch_shapes=[
            pltpu.VMEM((rows, FF), bf16),
            pltpu.VMEM((rows, D), bf16),
            pltpu.VMEM((rows, 2 * FF), bf16),
            pltpu.VMEM((D, 2 * FF), bf16),
            pltpu.VMEM((FF, D), bf16),
        ],
    )
    return pl.pallas_call(
        functools.partial(expert_body, tile=tile),
        grid_spec=grid_spec,
        out_shape=[
            jax.ShapeDtypeStruct((count, rows, D), bf16),
            jax.ShapeDtypeStruct((count, rows, D), bf16),
            jax.ShapeDtypeStruct((count, rows, 128), f32),
        ]
        + [part_shape] * parts,
        cost_estimate=cost(15 * count),
        compiler_params=params(),
    )(parity, x_rows, d_rows, slot_gate, w_gate_up, w_down)


def core_swap(value, groups):
    return lax.ppermute(value, "expert", [(m, m ^ 1) for m in range(groups)])


def from_row(value, groups, shift):
    count = groups // 2
    pairs = [((((y + shift) % count) * 2 + c), y * 2 + c) for y in range(count) for c in range(2)]
    return lax.ppermute(value, "expert", pairs)


def to_row(value, groups, shift):
    count = groups // 2
    pairs = [(y * 2 + c, ((y + shift) % count) * 2 + c) for y in range(count) for c in range(2)]
    return lax.ppermute(value, "expert", pairs)


def after(value, *others):
    return lax.optimization_barrier((value,) + others)[0]


def gather_column(value, groups):
    return [value] + [from_row(value, groups, s) for s in range(1, groups // 2)]


def gather_cores(column, groups, *before):
    result = [column[0], core_swap(column[0], groups)]
    for piece in column[1:]:
        piece = after(piece, *before)
        result += [piece, core_swap(piece, groups)]
    return result


def gather_members(value, groups):
    return gather_cores(gather_column(value, groups), groups)


def return_members(pieces, groups, *before):
    swapped = [core_swap(pieces[2 * s + 1], groups) for s in range(groups // 2)]
    terms, sent = [pieces[0], swapped[0]], []
    for s in range(1, groups // 2):
        mine = after(pieces[2 * s], *before)
        both = (mine.astype(f32) + swapped[s].astype(f32)).astype(bf16)
        sent.append(both)
        terms.append(to_row(both, groups, s))
    return terms, sent


def exchange_members(pieces, groups):
    count = groups // 2
    result = []
    for s in range(count):
        for c in range(2):
            if s == 0 and c == 0:
                result.append(pieces[0])
                continue
            pairs = [
                (((y - s) % count) * 2 + (core ^ c), y * 2 + core)
                for y in range(count)
                for core in range(2)
            ]
            result.append(lax.ppermute(pieces[2 * s + c], "expert", pairs))
    return result


def lane(shape):
    return lax.broadcasted_iota(jnp.int32, shape, len(shape) - 1)


def turn(value, cosine, sine, sign):
    first = lax.rem(lane(value.shape), HEAD_DIM) < HEAD_DIM // 2
    other = jnp.where(
        first, pltpu.roll(value, 128 - HEAD_DIM // 2, 1), pltpu.roll(value, HEAD_DIM // 2, 1)
    )
    return value * cosine + sign * other * sine


def project_body(x_ref, gain_ref, w_ref, cos_ref, sin_ref, normed_ref, q_ref, kv_ref):
    x = x_ref[0].astype(f32)
    scale = lax.rsqrt(jnp.mean(x * x, axis=1, keepdims=True) + epsilon)
    normed = (x * scale * gain_ref[...]).astype(bf16)
    normed_ref[0] = normed
    cosine, sine = cos_ref[...], sin_ref[...]
    q_width, k_width = HEADS * HEAD_DIM, KV_HEADS * HEAD_DIM
    for start in range(0, q_width + 2 * k_width, 512):
        part = mm(normed, w_ref[:, start : start + 512], ((1,), (0,)))
        for inner in range(0, 512, 128):
            at = start + inner
            value = part[:, inner : inner + 128]
            if at < q_width:
                q_ref[0, :, at : at + 128] = turn(value, cosine, sine, 1.0).astype(bf16)
            elif at < q_width + k_width:
                at -= q_width
                kv_ref[0, :, at : at + 128] = turn(value, cosine, sine, 1.0).astype(bf16)
            else:
                at -= q_width
                kv_ref[0, :, at : at + 128] = value.astype(bf16)


def project(tokens, gain, w_qkv, cosine, sine):
    micro, rows, _ = tokens.shape
    block = pl.BlockSpec((1, rows, D), lambda m: (m, 0, 0))
    table = pl.BlockSpec((rows, 128), lambda m: (0, 0))
    shape = jax.ShapeDtypeStruct((micro, rows, D), bf16)
    return pl.pallas_call(
        project_body,
        grid=(micro,),
        in_specs=[
            block,
            pl.BlockSpec((1, D), lambda m: (0, 0)),
            pl.BlockSpec(w_qkv.shape, lambda m: (0, 0)),
            table,
            table,
        ],
        out_specs=[block, block, block],
        out_shape=[shape, shape, shape],
        cost_estimate=cost(7),
        compiler_params=params(),
    )(tokens, gain, w_qkv, cosine, sine)


def stack_heads(block, scale):
    wide = block.astype(f32) * scale
    result = []
    for p in range(2):
        part = wide[:, p * 128 : (p + 1) * 128]
        half = (lane(part.shape) >= HEAD_DIM) == (p == 1)
        for h in range(2):
            moved = part if h == p else pltpu.roll(part, HEAD_DIM, 1)
            result.append(jnp.where(half, moved, 0.0).astype(bf16))
    return jnp.concatenate(result, axis=0)


def unstack_heads(stacked, rows):
    result = []
    for p in range(2):
        pieces = []
        for h in range(2):
            i = 2 * p + h
            part = stacked[i * rows : (i + 1) * rows]
            pieces.append(part if h == p else pltpu.roll(part, HEAD_DIM, 1))
        result.append(jnp.where(lane(pieces[0].shape) < HEAD_DIM, pieces[0], pieces[1]))
    return result


def attend_body(
    q_ref, pk_ref, pv_ref, ok_ref, ov_ref, bias_ref, x_ref, w_ref, gain_ref,
    att_ref, lse_ref, hidden_ref, low_ref, all_ref,
):
    j = pl.program_id(0)
    rows = q_ref.shape[1]
    q = stack_heads(q_ref[0], score_scale)
    k = jnp.concatenate([pk_ref[0], ok_ref[0, PROMPT_DEV:, :]], axis=0)
    v = jnp.concatenate([pv_ref[0], ov_ref[0, PROMPT_DEV:, :]], axis=0)
    scores = mm(k, q, ((1,), (1,))) + bias_ref[...]
    largest = jnp.max(scores, axis=0, keepdims=True)
    raised = jnp.exp(scores - largest)
    total = jnp.sum(raised, axis=0, keepdims=True)
    weights = (raised * (1.0 / total)).astype(bf16)
    lse_ref[0] = largest + jnp.log(total)
    mixed = mm(v, weights, ((0,), (0,))).T
    for p, part in enumerate(unstack_heads(mixed, rows)):
        at = pl.multiple_of(j * 256 + p * 128, 128)
        att_ref[0, :, p * 128 : (p + 1) * 128] = part.astype(bf16)
        all_ref[:, pl.ds(at, 128)] = part.astype(bf16)

    @pl.when(j == pl.num_programs(0) - 1)
    def _():
        branch = mm(all_ref[...], w_ref[...], ((1,), (0,)))
        hidden = x_ref[0].astype(f32) + branch_scale * branch
        hidden_ref[0] = hidden
        scale = lax.rsqrt(jnp.mean(hidden * hidden, axis=1, keepdims=True) + epsilon)
        low_ref[0] = (hidden * scale * gain_ref[...]).astype(bf16)


def attend(micro, q, kv, prompt, bias, tokens, w_out, gain):
    rows, prompt_rows = q.shape[1], prompt.shape[1]
    steps = KV_HEADS // 2
    full = pl.BlockSpec((1, rows, D), lambda j: (micro, 0, 0))
    one = pl.BlockSpec((1, rows, D), lambda j: (0, 0, 0))
    return pl.pallas_call(
        attend_body,
        grid=(steps,),
        in_specs=[
            pl.BlockSpec((1, rows, 256), lambda j: (micro, 0, j)),
            pl.BlockSpec((1, prompt_rows, 128), lambda j: (micro, 0, j)),
            pl.BlockSpec((1, prompt_rows, 128), lambda j: (micro, 0, j + steps)),
            pl.BlockSpec((1, rows, 128), lambda j: (micro, 0, j)),
            pl.BlockSpec((1, rows, 128), lambda j: (micro, 0, j + steps)),
            pl.BlockSpec(bias.shape, lambda j: (0, 0)),
            full,
            pl.BlockSpec(w_out.shape, lambda j: (0, 0)),
            pl.BlockSpec((1, D), lambda j: (0, 0)),
        ],
        out_specs=[
            pl.BlockSpec((1, rows, 256), lambda j: (0, 0, j)),
            pl.BlockSpec((1, 1, 4 * rows), lambda j: (j, 0, 0)),
            one,
            one,
        ],
        out_shape=[
            jax.ShapeDtypeStruct((1, rows, D), bf16),
            jax.ShapeDtypeStruct((steps, 1, 4 * rows), f32),
            jax.ShapeDtypeStruct((1, rows, D), f32),
            jax.ShapeDtypeStruct((1, rows, D), bf16),
        ],
        scratch_shapes=[pltpu.VMEM((rows, D), bf16)],
        cost_estimate=cost(12),
        compiler_params=params(),
    )(q, prompt, prompt, kv, kv, bias, tokens, w_out, gain)


def norm_back(value, gain, grad):
    scale = lax.rsqrt(jnp.mean(value * value, axis=1, keepdims=True) + epsilon)
    scaled = grad * gain
    inner = jnp.mean(scaled * value, axis=1, keepdims=True)
    back = scale * scaled - value * (scale * scale * scale * inner)
    return back, jnp.sum(grad * value * scale, axis=0, keepdims=True)


def middle_body(*refs, terms):
    term_refs = refs[:terms]
    (logit_ref, router_ref, hidden_ref, gain_ref, cot_ref, w_ref) = refs[terms : terms + 6]
    grad_hidden_ref, branch_ref, att_ref, gain_out_ref = refs[terms + 6 :]
    total = mm(logit_ref[0], router_ref[...], ((0,), (1,)))
    for ref in term_refs:
        total = total + ref[0].astype(f32)
    back, gain_grad = norm_back(hidden_ref[0], gain_ref[...], total)
    grad_hidden = cot_ref[0].astype(f32) + back
    grad_hidden_ref[0] = grad_hidden
    branch = (branch_scale * grad_hidden).astype(bf16)
    branch_ref[0] = branch
    att_ref[0] = mm(branch, w_ref[...], ((1,), (1,))).astype(bf16)

    @pl.when(pl.program_id(0) == 0)
    def _():
        gain_out_ref[...] = gain_grad

    @pl.when(pl.program_id(0) != 0)
    def _():
        gain_out_ref[...] += gain_grad


def middle_back(terms, grad_logits, w_router, hidden, gain, cotangent, w_out):
    micro, rows, _ = hidden.shape
    block = pl.BlockSpec((1, rows, D), lambda m: (m, 0, 0))
    row = pl.BlockSpec((1, D), lambda m: (0, 0))
    return pl.pallas_call(
        functools.partial(middle_body, terms=len(terms)),
        grid=(micro,),
        in_specs=[block] * len(terms)
        + [
            pl.BlockSpec((1, EXPERTS, rows), lambda m: (m, 0, 0)),
            pl.BlockSpec(w_router.shape, lambda m: (0, 0)),
            block,
            row,
            block,
            pl.BlockSpec(w_out.shape, lambda m: (0, 0)),
        ],
        out_specs=[block, block, block, row],
        out_shape=[
            jax.ShapeDtypeStruct((micro, rows, D), f32),
            jax.ShapeDtypeStruct((micro, rows, D), bf16),
            jax.ShapeDtypeStruct((micro, rows, D), bf16),
            jax.ShapeDtypeStruct((1, D), f32),
        ],
        cost_estimate=cost(8),
        compiler_params=params(),
    )(*terms, grad_logits, w_router, hidden, gain, cotangent, w_out)


def attend_back_body(
    q_ref, pk_ref, pv_ref, ok_ref, ov_ref, bias_ref, lse_ref, grad_ref, cos_ref, sin_ref,
    gq_ref, gpk_ref, gpv_ref, gok_ref, gov_ref,
):
    rows, prompt_rows = q_ref.shape[1], pk_ref.shape[1]
    q = stack_heads(q_ref[0], score_scale)
    grad = stack_heads(grad_ref[0], 1.0)
    k = jnp.concatenate([pk_ref[0], ok_ref[0, PROMPT_DEV:, :]], axis=0)
    v = jnp.concatenate([pv_ref[0], ov_ref[0, PROMPT_DEV:, :]], axis=0)
    probs = jnp.exp(mm(k, q, ((1,), (1,))) + bias_ref[...] - lse_ref[0, 0])
    grad_probs = mm(v, grad, ((1,), (1,)))
    centre = jnp.sum(probs * grad_probs, axis=0, keepdims=True)
    grad_scores = (probs * (grad_probs - centre)).astype(bf16)
    grad_v = mm(probs.astype(bf16), grad, ((1,), (0,)))
    grad_k = mm(grad_scores, q, ((1,), (0,)))
    grad_q = mm(k, grad_scores, ((0,), (0,))).T * score_scale
    cosine, sine = cos_ref[...], sin_ref[...]
    for p, part in enumerate(unstack_heads(grad_q, rows)):
        gq_ref[0, :, p * 128 : (p + 1) * 128] = turn(part, cosine, sine, -1.0).astype(bf16)
    gpk_ref[0] = grad_k[:prompt_rows].astype(bf16)
    gpv_ref[0] = grad_v[:prompt_rows].astype(bf16)
    gok_ref[0] = turn(
        grad_k[prompt_rows:], cosine[PROMPT_DEV:], sine[PROMPT_DEV:], -1.0
    ).astype(bf16)
    gov_ref[0] = grad_v[prompt_rows:].astype(bf16)


def attend_back(q, kv, prompt, bias, lse, grad, cosine, sine):
    micro, rows, _ = q.shape
    prompt_rows = prompt.shape[1]
    own_rows = rows - PROMPT_DEV
    steps = KV_HEADS // 2
    wide = pl.BlockSpec((1, rows, 256), lambda m, j: (m, 0, j))
    table = pl.BlockSpec((rows, 128), lambda m, j: (0, 0))
    prompt_spec = pl.BlockSpec((1, prompt_rows, 128), lambda m, j: (m, 0, j))
    own_spec = pl.BlockSpec((1, own_rows, 128), lambda m, j: (m, 0, j))
    k_width = KV_HEADS * HEAD_DIM
    return pl.pallas_call(
        attend_back_body,
        grid=(micro, steps),
        in_specs=[
            wide,
            prompt_spec,
            pl.BlockSpec((1, prompt_rows, 128), lambda m, j: (m, 0, j + steps)),
            pl.BlockSpec((1, rows, 128), lambda m, j: (m, 0, j)),
            pl.BlockSpec((1, rows, 128), lambda m, j: (m, 0, j + steps)),
            pl.BlockSpec(bias.shape, lambda m, j: (0, 0)),
            pl.BlockSpec((1, 1, 1, 4 * rows), lambda m, j: (m, j, 0, 0)),
            wide,
            table,
            table,
        ],
        out_specs=[wide, prompt_spec, prompt_spec, own_spec, own_spec],
        out_shape=[
            jax.ShapeDtypeStruct((micro, rows, D), bf16),
            jax.ShapeDtypeStruct((micro, prompt_rows, k_width), bf16),
            jax.ShapeDtypeStruct((micro, prompt_rows, k_width), bf16),
            jax.ShapeDtypeStruct((micro, own_rows, k_width), bf16),
            jax.ShapeDtypeStruct((micro, own_rows, k_width), bf16),
        ],
        cost_estimate=cost(23),
        compiler_params=pltpu.CompilerParams(
            vmem_limit_bytes=vmem_limit, dimension_semantics=("arbitrary", "arbitrary")
        ),
    )(q, prompt, prompt, kv, kv, bias, lse, grad, cosine, sine)


def weight_body(*refs, terms):
    normed_ref, gq_ref, gok_ref, gov_ref = refs[:4]
    k_terms, v_terms = refs[4 : 4 + terms], refs[4 + terms : 4 + 2 * terms]
    cos_ref, sin_ref, gp_ref, out_ref, acc_ref = refs[4 + 2 * terms :]
    q_width, k_width = HEADS * HEAD_DIM, KV_HEADS * HEAD_DIM
    gp_ref[0, :, :q_width] = gq_ref[0]
    gp_ref[0, PROMPT_DEV:, q_width : q_width + k_width] = gok_ref[0]
    gp_ref[0, PROMPT_DEV:, q_width + k_width :] = gov_ref[0]
    prompt_k, prompt_v = [sum(ref[0].astype(f32) for ref in group) for group in (k_terms, v_terms)]
    cosine, sine = cos_ref[:PROMPT_DEV, :], sin_ref[:PROMPT_DEV, :]
    for at in range(0, k_width, 128):
        turned = turn(prompt_k[:, at : at + 128], cosine, sine, -1.0)
        gp_ref[0, :PROMPT_DEV, q_width + at : q_width + at + 128] = turned.astype(bf16)
    gp_ref[0, :PROMPT_DEV, q_width + k_width :] = prompt_v.astype(bf16)
    part = mm(normed_ref[0], gp_ref[0], ((0,), (0,)))
    m = pl.program_id(0)

    @pl.when(m == 0)
    def _():
        acc_ref[...] = part

    @pl.when(m != 0)
    def _():
        acc_ref[...] += part

    @pl.when(m == pl.num_programs(0) - 1)
    def _():
        out_ref[...] = acc_ref[...].astype(bf16)


def weight_back(normed, gq, gok, gov, k_terms, v_terms, cosine, sine):
    micro, rows, _ = normed.shape
    k_width = KV_HEADS * HEAD_DIM
    wide = pl.BlockSpec((1, rows, D), lambda m: (m, 0, 0))
    own = pl.BlockSpec((1, rows - PROMPT_DEV, k_width), lambda m: (m, 0, 0))
    term = pl.BlockSpec((1, PROMPT_DEV, k_width), lambda m: (m, 0, 0))
    table = pl.BlockSpec((rows, 128), lambda m: (0, 0))
    return pl.pallas_call(
        functools.partial(weight_body, terms=len(k_terms)),
        grid=(micro,),
        in_specs=[wide, wide, own, own] + [term] * (2 * len(k_terms)) + [table, table],
        out_specs=[
            pl.BlockSpec((1, rows, 2 * D), lambda m: (m, 0, 0)),
            pl.BlockSpec((D, 2 * D), lambda m: (0, 0)),
        ],
        out_shape=[
            jax.ShapeDtypeStruct((micro, rows, 2 * D), bf16),
            jax.ShapeDtypeStruct((D, 2 * D), bf16),
        ],
        scratch_shapes=[pltpu.VMEM((D, 2 * D), f32)],
        cost_estimate=cost(11),
        compiler_params=params(),
    )(normed, gq, gok, gov, *k_terms, *v_terms, cosine, sine)


def token_body(gp_ref, w_ref, x_ref, gain_ref, hidden_ref, out_ref, gain_out_ref):
    grad = mm(gp_ref[0], w_ref[...], ((1,), (1,)))
    back, gain_grad = norm_back(x_ref[0].astype(f32), gain_ref[...], grad)
    out_ref[0] = (hidden_ref[0] + back).astype(bf16)

    @pl.when(pl.program_id(0) == 0)
    def _():
        gain_out_ref[...] = gain_grad

    @pl.when(pl.program_id(0) != 0)
    def _():
        gain_out_ref[...] += gain_grad


def token_back(gp, w_qkv, tokens, gain, grad_hidden):
    micro, rows, _ = tokens.shape
    block = pl.BlockSpec((1, rows, D), lambda m: (m, 0, 0))
    row = pl.BlockSpec((1, D), lambda m: (0, 0))
    return pl.pallas_call(
        token_body,
        grid=(micro,),
        in_specs=[
            pl.BlockSpec((1, rows, 2 * D), lambda m: (m, 0, 0)),
            pl.BlockSpec(w_qkv.shape, lambda m: (0, 0)),
            block,
            row,
            block,
        ],
        out_specs=[block, row],
        out_shape=[
            jax.ShapeDtypeStruct((micro, rows, D), bf16),
            jax.ShapeDtypeStruct((1, D), f32),
        ],
        cost_estimate=cost(8),
        compiler_params=params(),
    )(gp, w_qkv, tokens, gain, grad_hidden)


def halve(value, axis, swap, bit):
    rows = value.shape[0] // 2
    keep = lax.dynamic_slice_in_dim(value, bit * rows, rows, 0)
    send = lax.dynamic_slice_in_dim(value, (1 - bit) * rows, rows, 0)
    got = lax.ppermute(send, axis, swap)
    return (keep.astype(f32) + got.astype(f32)).astype(bf16)


def finish_dense_body(table_ref, *refs, pieces):
    first_refs, second_refs = refs[:pieces], refs[pieces : 2 * pieces]
    qkv_ref, out_ref = refs[2 * pieces :]
    width = first_refs[0].shape[1]
    rest = qkv_ref.shape[1] - width
    for i in range(pieces):

        @pl.when(pl.program_id(0) == i)
        def _(i=i):
            qkv_ref[:, :width] = first_refs[i][...].astype(f32)
            qkv_ref[:, width:] = second_refs[i][:, :rest].astype(f32)
            out_ref[...] = second_refs[i][:, rest:].astype(f32)


def finish_dense(table, first, second):
    pieces = len(first)
    height = first[0].shape[0]
    grid_spec = pltpu.PrefetchScalarGridSpec(
        num_scalar_prefetch=1,
        grid=(pieces,),
        in_specs=[full_spec(piece) for piece in first + second],
        out_specs=[
            pl.BlockSpec((height, 2 * D), lambda i, t: (t[i], 0)),
            pl.BlockSpec((height, D), lambda i, t: (t[i], 0)),
        ],
    )
    return pl.pallas_call(
        functools.partial(finish_dense_body, pieces=pieces),
        grid_spec=grid_spec,
        out_shape=[
            jax.ShapeDtypeStruct((pieces * height, 2 * D), f32),
            jax.ShapeDtypeStruct((pieces * height, D), f32),
        ],
        cost_estimate=cost(9),
        compiler_params=params(),
    )(table, *first, *second)


def local(
    tokens, cotangent, expert_ids, norm_attn, w_qkv, w_out, norm_moe, w_router, w_gate_up, w_down
):
    groups = lax.axis_size("expert")
    dp_size = lax.axis_size("dp")
    member = lax.axis_index("expert")
    dp_index = lax.axis_index("dp")
    rows_all = tokens.shape[0]
    tok_rows = rows_all // MICRO
    local_experts = w_gate_up.shape[0]
    prompt_len = PROMPT_DEV * groups
    k_width = KV_HEADS * HEAD_DIM
    pairs = dp_size // 2
    blocks = groups * MICRO
    attn_gain = norm_attn.reshape(1, D)
    moe_gain = norm_moe.reshape(1, D)
    token_rows = tokens.reshape(MICRO, tok_rows, D)
    cot_rows = cotangent.reshape(MICRO, tok_rows, D)

    local_index = jnp.arange(tok_rows, dtype=jnp.int32)
    positions = jnp.where(
        local_index < PROMPT_DEV,
        member * PROMPT_DEV + local_index,
        prompt_len + local_index - PROMPT_DEV,
    )
    half_dim = HEAD_DIM // 2
    inverse = 10000.0 ** (-2.0 * jnp.arange(half_dim, dtype=f32) / HEAD_DIM)
    angles = positions.astype(f32)[:, None] * inverse[None, :]
    cosine = jnp.tile(jnp.cos(angles), (1, 128 // half_dim))
    sine = jnp.tile(jnp.sin(angles), (1, 128 // half_dim))
    sine = jnp.where(jnp.arange(128)[None, :] % HEAD_DIM < half_dim, -sine, sine)
    rows_of = []
    for s in range(groups // 2):
        for c in range(2):
            place = lax.rem(member // 2 + s, groups // 2) * 2 + lax.rem(member + c, 2)
            rows_of.append(place * PROMPT_DEV + jnp.arange(PROMPT_DEV, dtype=jnp.int32))
    key_positions = jnp.concatenate(
        rows_of + [prompt_len + jnp.arange(tok_rows - PROMPT_DEV, dtype=jnp.int32)]
    )
    bias = jnp.where(
        key_positions[:, None] <= jnp.tile(positions, HEADS // (KV_HEADS // 2))[None, :],
        0.0,
        masked_score,
    )

    first_expert = member * local_experts
    ids_t = gather_members(expert_ids.reshape(MICRO, tok_rows, TOP).transpose(0, 2, 1), groups)
    ids_all = lax.rem(jnp.concatenate(ids_t, axis=0) + (EXPERTS - first_expert), EXPERTS)
    cot_pieces = [gather_members(cot_rows[:1], groups)]
    normed, queries, key_value = project(token_rows, attn_gain, w_qkv, cosine, sine)
    prompt_pieces = gather_members(
        after(key_value[:, :PROMPT_DEV], cot_pieces[0][2]), groups
    )
    prompt = jnp.concatenate(prompt_pieces, axis=1)
    cot_pieces += [
        gather_members(after(cot_rows[m : m + 1], prompt_pieces[2]), groups)
        for m in range(1, MICRO)
    ]
    router = lax.dynamic_slice_in_dim(
        jnp.concatenate([w_router, w_router], axis=1), first_expert, EXPERTS, 1
    )

    attended, lse, hidden, moe_pieces, moe_low = [], [], [], [], []
    for m in range(MICRO):
        mask = bias if m == 0 else after(bias, moe_low[-1])
        att, log_total, hid, low = attend(
            m, queries, key_value, prompt, mask, token_rows, w_out, moe_gain
        )
        attended.append(att)
        lse.append(log_total[None])
        hidden.append(hid)
        moe_low.append(low)
        moe_pieces.append(gather_column(low, groups))

    def by_block(pieces):
        return [pieces[m][g] for g in range(groups) for m in range(MICRO)]

    d_rows, slots = pick_grads(after(ids_all, moe_low[-1]), by_block(cot_pieces), local_experts)
    moe_pieces = [gather_cores(column, groups, slots) for column in moe_pieces]
    attended = jnp.concatenate(attended, axis=0)
    lse = jnp.concatenate(lse, axis=0)
    hidden = jnp.concatenate(hidden, axis=0)
    moe_low = jnp.concatenate(moe_low, axis=0)

    x_rows, slot_gate, gates = pick_tokens(ids_all, slots, router, by_block(moe_pieces))
    slot_rows = blocks * SLOTS
    x_rows = x_rows.reshape(local_experts, slot_rows, D)
    d_rows = d_rows.reshape(local_experts, slot_rows, D)
    slot_gate = slot_gate.reshape(local_experts, slot_rows, 128)
    parity = lax.rem(dp_index, 2).astype(jnp.int32)
    swap_x = [(d, d ^ 1) for d in range(dp_size)]
    swap_y = [(m, m ^ 2) for m in range(groups)]
    swap_core = [(m, m ^ 1) for m in range(groups)]
    z_groups = [[d for d in range(dp_size) if d % 2 == r] for r in range(2)]
    piece = (D + FF) // (2 * pairs)

    def sum_z(value):
        count, _, height, _ = value.shape
        return lax.psum_scatter(
            value.reshape(count, pairs * height, D),
            "dp",
            scatter_dimension=1,
            axis_index_groups=z_groups,
            tiled=True,
        )

    plan = CHUNKS
    if sum(count for count, _ in plan) != local_experts:
        plan = tuple((1, e == 0) for e in range(local_experts))
    outs, backs, dots, halves, parts = [], [], [], {}, {}

    held = {}

    def add_x(i, *before, hold=False):
        keep, got = halves.pop(i)
        got = after(got, *before)
        half = (keep.astype(f32) + got.astype(f32)).astype(bf16)
        if hold:
            held[i] = half
        else:
            parts[i] = sum_z(half)
        return half

    first = 0
    order = parity.reshape(1)
    for i, (count, whole) in enumerate(plan):
        if i:
            order = after(order, outs[-1])
        if i == 3:
            order = after(order, add_x(1, outs[-1]))
        if i == 4:
            order = after(order, parts[0])
        out, back, dot, *sums = expert_chunk(
            order, first, count, pairs, not whole, x_rows, d_rows, slot_gate, w_gate_up, w_down
        )
        shape = (count, blocks, SLOTS)
        outs.append(out.reshape(shape + (D,)))
        backs.append(back.reshape(shape + (D,)))
        dots.append(dot.reshape(shape + (128,)))
        if whole:
            parts[i] = sum_z(sums[0])
        else:
            halves[i] = (sums[0], lax.ppermute(sums[1], "dp", swap_x))
        first += count

    def left(i, *before, hold=False):
        return [add_x(i, *before, hold=hold)] if i in halves else []

    def sent(i):
        return [parts[i]] if i in parts else []

    *back_sum, back_dots = sum_rows(slots, backs, dots)

    def pieces_of(value):
        return [value[j * MICRO : (j + 1) * MICRO] for j in range(groups)]

    dot_pieces = exchange_members(pieces_of(back_dots), groups)
    back_terms, back_sent = return_members(back_sum, groups, *dot_pieces)
    token_dots = jnp.zeros((MICRO, EXPERTS, tok_rows), f32)
    for s in range(groups // 2):
        for c in range(2):
            place = lax.rem(member // 2 + groups // 2 - s, groups // 2) * 2 + lax.rem(
                member + c, 2
            )
            label = lax.rem(place + groups - member, groups) * local_experts
            token_dots = lax.dynamic_update_slice_in_dim(
                token_dots, dot_pieces[2 * s + c], label, 1
            )
    own_gates = gates[:MICRO]
    centre = jnp.sum(own_gates * token_dots, axis=1, keepdims=True)
    grad_logits = (own_gates * (token_dots - centre)).astype(bf16)
    mixed = sum_rows(
        after(slots, *back_sent, *sent(1), *left(2, back_sum[0], hold=True)), outs
    )
    mix_terms, _ = return_members(mixed, groups)

    grad_hidden, grad_branch, grad_attended, grad_norm_moe = middle_back(
        back_terms, grad_logits, router, hidden, moe_gain, after(cot_rows, *mixed, *sent(4)), w_out
    )
    grad_router = jnp.einsum("bet,btd->ed", grad_logits, moe_low, preferred_element_type=f32)
    grad_out = jnp.einsum(
        "brd,bre->de", attended, grad_branch, preferred_element_type=f32
    ).astype(bf16)
    core_bit, row_bit = lax.rem(member, 2), lax.rem(member // 2, 2)
    grad_out = halve(grad_out, "expert", swap_core, core_bit)
    gq, gpk, gpv, gok, gov = attend_back(
        queries,
        key_value,
        prompt,
        after(bias, grad_out, *left(3, grad_branch)),
        lse,
        grad_attended,
        cosine,
        sine,
    )

    def prompt_terms(value):
        return return_members(
            [value[:, j * PROMPT_DEV : (j + 1) * PROMPT_DEV] for j in range(groups)], groups
        )[0]

    mixture = sum(after(term, gq).astype(f32) for term in mix_terms)
    output = (hidden + branch_scale * mixture).astype(bf16)
    grad_out = halve(grad_out, "expert", swap_y, row_bit)
    gp, grad_qkv = weight_back(
        after(normed, grad_out, *mix_terms[2:], *left(5, gq)),
        gq,
        gok,
        gov,
        prompt_terms(gpk),
        prompt_terms(gpv),
        cosine,
        sine,
    )
    grad_tokens, grad_norm_attn = token_back(
        after(gp, grad_qkv, output), w_qkv, token_rows, attn_gain, grad_hidden
    )
    last = [add_x(i, grad_norm_attn) for i in list(halves)] + sent(2) + sent(3)
    grad_qkv = halve(grad_qkv, "expert", swap_core, core_bit)
    grad_qkv = halve(grad_qkv, "expert", swap_y, row_bit)

    whole_sums = [parts[i] for i, (_, whole) in enumerate(plan) if whole]
    whole_sums = jnp.concatenate(whole_sums, axis=0)
    swapped = lax.ppermute(after(whole_sums[:, piece:], *last), "dp", swap_x)
    whole_sums = (whole_sums[:, :piece].astype(f32) + swapped.astype(f32)).astype(bf16)
    pieces, at = [], 0
    for i, (count, whole) in enumerate(plan):
        pieces.append(whole_sums[at : at + count] if whole else parts.get(i))
        at += count if whole else 0

    small = jnp.concatenate(
        [
            lax.dynamic_slice_in_dim(
                jnp.concatenate([grad_router, grad_router], axis=0),
                EXPERTS - first_expert,
                EXPERTS,
                0,
            ),
            grad_norm_attn,
            grad_norm_moe,
            jnp.zeros((14, D), f32),
        ],
        axis=0,
    )
    small = after(small, *last)
    for axis, swap in (("expert", swap_core), ("dp", swap_x), ("expert", swap_y)):
        small = small + lax.ppermute(small, axis, swap)
    dense = jnp.concatenate([grad_qkv, grad_out], axis=1)
    dense = after(halve(dense, "dp", swap_x, parity), *sent(5))
    for i in list(held):
        parts[i] = sum_z(after(held.pop(i), dense))
        pieces[i] = parts[i]
    dense_rows = dense.shape[0]
    dense = jnp.concatenate([dense, small.reshape(-1, 3 * D).astype(bf16)], axis=0)
    dense = lax.psum(dense, "dp", axis_index_groups=z_groups)
    if groups > 4:
        rest = [[m for m in range(groups) if m % 4 == r] for r in range(4)]
        dense = lax.psum(dense, "expert", axis_index_groups=rest)
    small = dense[dense_rows:].reshape(-1, D).astype(f32)
    dense = dense[:dense_rows]
    width = dense.shape[1] // 2
    left_own, right_own = dense[:, :width], dense[:, width:]
    left_x = lax.ppermute(left_own, "dp", swap_x)
    right_y = lax.ppermute(right_own, "expert", swap_y)
    left_four = [left_own, left_x] + [
        lax.ppermute(value, "expert", swap_y) for value in (left_own, left_x)
    ]
    right_x = [lax.ppermute(value, "dp", swap_x) for value in (right_own, right_y)]
    right_four = [right_own, right_x[0], right_y, right_x[1]]
    pieces[2] = after(pieces[2], left_four[3], right_four[3])
    left_all = left_four + [core_swap(value, groups) for value in left_four]
    right_all = right_four + [core_swap(value, groups) for value in right_four]
    base = core_bit * 4 + row_bit * 2 + parity
    table = jnp.bitwise_xor(base, jnp.arange(8, dtype=jnp.int32)).astype(jnp.int32)
    full_qkv, full_out = finish_dense(table, left_all, right_all)

    experts_sum = jnp.concatenate(pieces, axis=0).astype(f32)
    gu_piece = D // (2 * pairs)
    return (
        output.reshape(rows_all, D),
        grad_tokens.reshape(rows_all, D),
        small[EXPERTS],
        full_qkv,
        full_out,
        small[EXPERTS + 1],
        small[:EXPERTS].T,
        experts_sum[:, :gu_piece],
        experts_sum[:, gu_piece:],
    )


def solution(mesh):
    in_specs = (
        P(("dp", "expert"), None),
        P(("dp", "expert"), None),
        P(("dp", "expert"), None),
        P(),
        P(),
        P(),
        P(),
        P(),
        P("expert", None, None),
        P("expert", None, None),
    )
    out_specs = (
        P(("dp", "expert"), None),
        P(("dp", "expert"), None),
        P(),
        P(),
        P(),
        P(),
        P(),
        P("expert", "dp", None),
        P("expert", "dp", None),
    )
    return jax.shard_map(local, mesh=mesh, in_specs=in_specs, out_specs=out_specs, check_vma=False)
```

```python
import functools

import jax
import jax.numpy as jnp
from jax import lax
from jax.experimental import pallas as pl
from jax.experimental.pallas import tpu as pltpu
from jax.sharding import PartitionSpec as P

D = 1024
HEADS = 16
KV_HEADS = 8
HEAD_DIM = 64
FF = 512
EXPERTS = 32
TOP = 8
PROMPT_DEV = 64
MICRO = 2
CAP = 100
SLOTS = 112
CHUNKS = ((1, True), (1, False), (2, False), (2, False), (1, True), (1, False))


epsilon = 1e-06
score_scale = 1.0 / 64.0
branch_scale = 0.22
masked_score = -1e30

f32 = jnp.float32
bf16 = jnp.bfloat16
vmem_limit = 60 * 1024 * 1024


def params():
    return pltpu.CompilerParams(
        vmem_limit_bytes=vmem_limit, dimension_semantics=("arbitrary",)
    )


def cost(micros):
    return pl.CostEstimate(flops=int(micros * 1.15e9), bytes_accessed=0, transcendentals=0)


def mm(left, right, dims):
    return lax.dot_general(left, right, (dims, ((), ())), preferred_element_type=f32)


def fill_one_hot(slot_rows, onehot_ref):
    experts, rows = slot_rows.shape
    place = lax.broadcasted_iota(jnp.int32, (SLOTS, rows), 0)
    for e in range(experts):
        hit = place == slot_rows[e : e + 1, :]
        onehot_ref[e * SLOTS : (e + 1) * SLOTS, :] = jnp.where(hit, 1.0, 0.0).astype(bf16)


def chosen_of(ids, count):
    rows = ids.shape[1]
    label = lax.broadcasted_iota(jnp.int32, (count, rows), 0)
    hit = ids[0:1, :] == label
    for k in range(1, ids.shape[0]):
        hit = hit | (ids[k : k + 1, :] == label)
    return hit


def select_block(row_refs, rows_ref):
    b = pl.program_id(0)
    at = 0
    for ref in row_refs:
        for i in range(ref.shape[0]):

            @pl.when(b == at)
            def _(ref=ref, i=i):
                rows_ref[...] = ref[i]

            at += 1


def store_picked(onehot_ref, rows_ref, out_ref):
    picked = mm(onehot_ref[...], rows_ref[...], ((1,), (0,))).astype(bf16)
    for e in range(out_ref.shape[0]):
        out_ref[e, 0] = picked[e * SLOTS : (e + 1) * SLOTS]


def pick_grad_body(*refs, pieces):
    ids_ref = refs[0]
    row_refs = refs[1 : 1 + pieces]
    out_ref, slot_ref, onehot_ref, rows_ref, earlier_ref = refs[1 + pieces :]
    experts, rows = slot_ref.shape[1], slot_ref.shape[2]

    @pl.when(pl.program_id(0) == 0)
    def _():
        first = lax.broadcasted_iota(jnp.int32, (rows, rows), 0)
        second = lax.broadcasted_iota(jnp.int32, (rows, rows), 1)
        earlier_ref[...] = jnp.where(first < second, 1.0, 0.0).astype(bf16)

    select_block(row_refs, rows_ref)
    hit = chosen_of(ids_ref[0], 8)
    rank = mm(jnp.where(hit, 1.0, 0.0).astype(bf16), earlier_ref[...], ((1,), (0,)))
    slots = jnp.where(hit, rank, -1.0).astype(jnp.int32)[:experts]
    slot_ref[0] = slots
    fill_one_hot(slots, onehot_ref)
    store_picked(onehot_ref, rows_ref, out_ref)


def full_spec(array):
    zeros = (0,) * array.ndim
    return pl.BlockSpec(array.shape, lambda *_: zeros)


def pick_grads(ids, pieces, experts):
    blocks, top, tok = ids.shape
    return pl.pallas_call(
        functools.partial(pick_grad_body, pieces=len(pieces)),
        grid=(blocks,),
        in_specs=[pl.BlockSpec((1, top, tok), lambda b: (b, 0, 0))]
        + [full_spec(piece) for piece in pieces],
        out_specs=[
            pl.BlockSpec((experts, 1, SLOTS, D), lambda b: (0, b, 0, 0)),
            pl.BlockSpec((1, experts, tok), lambda b: (b, 0, 0)),
        ],
        out_shape=[
            jax.ShapeDtypeStruct((experts, blocks, SLOTS, D), bf16),
            jax.ShapeDtypeStruct((blocks, experts, tok), jnp.int32),
        ],
        scratch_shapes=[
            pltpu.VMEM((experts * SLOTS, tok), bf16),
            pltpu.VMEM((tok, D), bf16),
            pltpu.VMEM((tok, tok), bf16),
        ],
        cost_estimate=cost(15),
        compiler_params=params(),
    )(ids, *pieces)


def pick_token_body(*refs, pieces):
    ids_ref, slot_ref, router_ref = refs[:3]
    row_refs = refs[3 : 3 + pieces]
    out_ref, slot_gate_ref, gate_ref, onehot_ref, rows_ref = refs[3 + pieces :]
    experts, rows = slot_ref.shape[1], slot_ref.shape[2]
    select_block(row_refs, rows_ref)
    logits = mm(router_ref[...], rows_ref[...], ((0,), (1,)))
    hit = chosen_of(ids_ref[0], EXPERTS)
    masked = jnp.where(hit, logits, masked_score)
    raised = jnp.where(hit, jnp.exp(masked - jnp.max(masked, axis=0, keepdims=True)), 0.0)
    gates = raised / jnp.sum(raised, axis=0, keepdims=True)
    gate_ref[0] = gates
    fill_one_hot(slot_ref[0], onehot_ref)
    store_picked(onehot_ref, rows_ref, out_ref)
    place = lax.broadcasted_iota(jnp.int32, (SLOTS, rows), 0)
    for e in range(experts):
        here = place == slot_ref[0, e : e + 1, :]
        gate = jnp.sum(jnp.where(here, gates[e : e + 1, :], 0.0), axis=1, keepdims=True)
        slot_gate_ref[e, 0] = jnp.broadcast_to(gate, (SLOTS, 128))


def pick_tokens(ids, slots, w_router, pieces):
    blocks, experts, tok = slots.shape
    return pl.pallas_call(
        functools.partial(pick_token_body, pieces=len(pieces)),
        grid=(blocks,),
        in_specs=[
            pl.BlockSpec((1, ids.shape[1], tok), lambda b: (b, 0, 0)),
            pl.BlockSpec((1, experts, tok), lambda b: (b, 0, 0)),
            full_spec(w_router),
        ]
        + [full_spec(piece) for piece in pieces],
        out_specs=[
            pl.BlockSpec((experts, 1, SLOTS, D), lambda b: (0, b, 0, 0)),
            pl.BlockSpec((experts, 1, SLOTS, 128), lambda b: (0, b, 0, 0)),
            pl.BlockSpec((1, EXPERTS, tok), lambda b: (b, 0, 0)),
        ],
        out_shape=[
            jax.ShapeDtypeStruct((experts, blocks, SLOTS, D), bf16),
            jax.ShapeDtypeStruct((experts, blocks, SLOTS, 128), f32),
            jax.ShapeDtypeStruct((blocks, EXPERTS, tok), f32),
        ],
        scratch_shapes=[pltpu.VMEM((experts * SLOTS, tok), bf16), pltpu.VMEM((tok, D), bf16)],
        cost_estimate=cost(17),
        compiler_params=params(),
    )(ids, slots, w_router, *pieces)


def sum_rows_body(*refs, chunks, with_dots):
    slot_ref = refs[0]
    row_refs = refs[1 : 1 + chunks]
    refs = refs[1 + chunks :]
    if with_dots:
        dot_refs, refs = refs[:chunks], refs[chunks:]
        back_ref, onehot_ref, flat_ref = refs[-3:]
        out_refs = refs[:-3]
    else:
        onehot_ref, flat_ref = refs[-2:]
        out_refs = refs[:-2]
    fill_one_hot(slot_ref[0], onehot_ref)
    e = 0
    for ref in row_refs:
        for i in range(ref.shape[0]):
            flat_ref[e * SLOTS : (e + 1) * SLOTS, :] = ref[i, 0]
            e += 1
    total = mm(onehot_ref[...], flat_ref[...], ((0,), (0,))).astype(bf16)
    for j, out_ref in enumerate(out_refs):

        @pl.when(pl.program_id(0) // MICRO == j)
        def _(out_ref=out_ref):
            out_ref[0] = total

    if with_dots:
        place = lax.broadcasted_iota(jnp.int32, (SLOTS, slot_ref.shape[2]), 0)
        e = 0
        for ref in dot_refs:
            for i in range(ref.shape[0]):
                hit = place == slot_ref[0, e : e + 1, :]
                back_ref[0, e : e + 1, :] = jnp.sum(
                    jnp.where(hit, ref[i, 0, :, 0:1], 0.0), axis=0, keepdims=True
                )
                e += 1


def sum_rows(slots, rows, dots=None):
    blocks, experts, tok = slots.shape

    def chunk_spec(chunk):
        return pl.BlockSpec((chunk.shape[0], 1) + chunk.shape[2:], lambda b: (0, b, 0, 0))

    in_specs = [pl.BlockSpec((1, experts, tok), lambda b: (b, 0, 0))]
    in_specs += [chunk_spec(chunk) for chunk in rows]
    args = [slots] + rows
    members = blocks // MICRO

    def member_spec(j):
        return pl.BlockSpec(
            (1, tok, D), lambda b: (jnp.clip(b - j * MICRO, 0, MICRO - 1), 0, 0)
        )

    out_shape = [jax.ShapeDtypeStruct((MICRO, tok, D), bf16)] * members
    out_specs = [member_spec(j) for j in range(members)]
    if dots is not None:
        in_specs += [chunk_spec(chunk) for chunk in dots]
        args += dots
        out_shape.append(jax.ShapeDtypeStruct((blocks, experts, tok), f32))
        out_specs.append(pl.BlockSpec((1, experts, tok), lambda b: (b, 0, 0)))
    return pl.pallas_call(
        functools.partial(sum_rows_body, chunks=len(rows), with_dots=dots is not None),
        grid=(blocks,),
        in_specs=in_specs,
        out_specs=out_specs,
        out_shape=out_shape,
        scratch_shapes=[
            pltpu.VMEM((experts * SLOTS, tok), bf16),
            pltpu.VMEM((experts * SLOTS, D), bf16),
        ],
        cost_estimate=cost(15),
        compiler_params=params(),
    )(*args)


def expert_body(
    parity_ref,
    x_ref,
    d_ref,
    gate_ref,
    wgu_ref,
    wd_ref,
    out_ref,
    back_ref,
    dots_ref,
    *part_refs,
    tile,
):
    mid_ref, grad_ref, act_ref, gu_ref, down_ref = part_refs[-5:]
    part_refs = part_refs[:-5]
    rows = x_ref.shape[1]

    def step(i, carry):
        span = pl.ds(pl.multiple_of(i * tile, tile), tile)
        hidden = mm(x_ref[0, span, :], wgu_ref[0], ((1,), (0,)))
        gate, up = hidden[:, :FF], hidden[:, FF:]
        sig = 1.0 / (1.0 + jnp.exp(-gate))
        silu = gate * sig
        middle = (silu * up).astype(bf16)
        mid_ref[span, :] = middle
        out = mm(middle, wd_ref[0], ((1,), (0,))).astype(bf16).astype(f32)
        weight = gate_ref[0, span, 0:1]
        scaled = branch_scale * d_ref[0, span, :].astype(f32)
        dots_ref[0, span, :] = jnp.broadcast_to(
            jnp.sum(scaled * out, axis=1, keepdims=True), (tile, 128)
        )
        out_ref[0, span, :] = (weight * out).astype(bf16)
        grad = (weight * scaled).astype(bf16)
        grad_ref[span, :] = grad
        grad_mid = mm(grad, wd_ref[0], ((1,), (1,)))
        act_ref[span, :FF] = (grad_mid * up * sig * (1.0 + gate * (1.0 - sig))).astype(bf16)
        act_ref[span, FF:] = (grad_mid * silu).astype(bf16)
        back_ref[0, span, :] = mm(act_ref[span, :], wgu_ref[0], ((1,), (1,))).astype(bf16)
        return carry

    lax.fori_loop(0, rows // tile, step, 0)
    gu_ref[...] = mm(x_ref[0], act_ref[...], ((0,), (0,))).astype(bf16)
    down_ref[...] = mm(mid_ref[...], grad_ref[...], ((0,), (0,))).astype(bf16)
    parity = parity_ref[0]
    pairs = part_refs[0].shape[1]
    half = (gu_ref.shape[0] + down_ref.shape[0]) // (2 * pairs)
    keep_ref, send_ref = part_refs[0], part_refs[-1]
    shift = half if len(part_refs) == 1 else 0
    start = 0
    for full in (gu_ref, down_ref):
        piece = full.shape[0] // (2 * pairs)
        for j in range(pairs):
            mine = pl.multiple_of((2 * j + parity) * piece, piece)
            other = pl.multiple_of((2 * j + 1 - parity) * piece, piece)
            keep_ref[0, j, start : start + piece, :] = full[pl.ds(mine, piece), :]
            send_ref[0, j, shift + start : shift + start + piece, :] = full[pl.ds(other, piece), :]
        start += piece


def expert_chunk(parity, first, count, pairs, split, x_rows, d_rows, slot_gate, w_gate_up, w_down):
    rows = x_rows.shape[1]
    tile = 2 * SLOTS
    mode = pl.Buffered(1 if rows > 1024 else 2)
    row_spec = pl.BlockSpec((1, rows, D), lambda e, p: (e + first, 0, 0), pipeline_mode=mode)
    col_spec = pl.BlockSpec((1, rows, 128), lambda e, p: (e + first, 0, 0))
    parts = 2 if split else 1
    piece = (D + FF) // (parts * pairs)
    part_spec = pl.BlockSpec((1, pairs, piece, D), lambda e, p: (e, 0, 0, 0))
    part_shape = jax.ShapeDtypeStruct((count, pairs, piece, D), bf16)
    out_row = pl.BlockSpec((1, rows, D), lambda e, p: (e, 0, 0))
    grid_spec = pltpu.PrefetchScalarGridSpec(
        num_scalar_prefetch=1,
        grid=(count,),
        in_specs=[
            row_spec,
            row_spec,
            col_spec,
            pl.BlockSpec((1, D, 2 * FF), lambda e, p: (e + first, 0, 0)),
            pl.BlockSpec((1, FF, D), lambda e, p: (e + first, 0, 0)),
        ],
        out_specs=[
            out_row,
            out_row,
            pl.BlockSpec((1, rows, 128), lambda e, p: (e, 0, 0)),
        ]
        + [part_spec] * parts,
        scratch_shapes=[
            pltpu.VMEM((rows, FF), bf16),
            pltpu.VMEM((rows, D), bf16),
            pltpu.VMEM((rows, 2 * FF), bf16),
            pltpu.VMEM((D, 2 * FF), bf16),
            pltpu.VMEM((FF, D), bf16),
        ],
    )
    return pl.pallas_call(
        functools.partial(expert_body, tile=tile),
        grid_spec=grid_spec,
        out_shape=[
            jax.ShapeDtypeStruct((count, rows, D), bf16),
            jax.ShapeDtypeStruct((count, rows, D), bf16),
            jax.ShapeDtypeStruct((count, rows, 128), f32),
        ]
        + [part_shape] * parts,
        cost_estimate=cost(15 * count),
        compiler_params=params(),
    )(parity, x_rows, d_rows, slot_gate, w_gate_up, w_down)


def core_swap(value, groups):
    return lax.ppermute(value, "expert", [(m, m ^ 1) for m in range(groups)])


def from_row(value, groups, shift):
    count = groups // 2
    pairs = [((((y + shift) % count) * 2 + c), y * 2 + c) for y in range(count) for c in range(2)]
    return lax.ppermute(value, "expert", pairs)


def to_row(value, groups, shift):
    count = groups // 2
    pairs = [(y * 2 + c, ((y + shift) % count) * 2 + c) for y in range(count) for c in range(2)]
    return lax.ppermute(value, "expert", pairs)


def after(value, *others):
    return lax.optimization_barrier((value,) + others)[0]


def gather_column(value, groups):
    return [value] + [from_row(value, groups, s) for s in range(1, groups // 2)]


def gather_cores(column, groups, *before):
    result = [column[0], core_swap(column[0], groups)]
    for piece in column[1:]:
        piece = after(piece, *before)
        result += [piece, core_swap(piece, groups)]
    return result


def gather_members(value, groups):
    return gather_cores(gather_column(value, groups), groups)


def return_members(pieces, groups, *before):
    swapped = [core_swap(pieces[2 * s + 1], groups) for s in range(groups // 2)]
    terms, sent = [pieces[0], swapped[0]], []
    for s in range(1, groups // 2):
        mine = after(pieces[2 * s], *before)
        both = (mine.astype(f32) + swapped[s].astype(f32)).astype(bf16)
        sent.append(both)
        terms.append(to_row(both, groups, s))
    return terms, sent


def exchange_members(pieces, groups):
    count = groups // 2
    result = []
    for s in range(count):
        for c in range(2):
            if s == 0 and c == 0:
                result.append(pieces[0])
                continue
            pairs = [
                (((y - s) % count) * 2 + (core ^ c), y * 2 + core)
                for y in range(count)
                for core in range(2)
            ]
            result.append(lax.ppermute(pieces[2 * s + c], "expert", pairs))
    return result


def lane(shape):
    return lax.broadcasted_iota(jnp.int32, shape, len(shape) - 1)


def turn(value, cosine, sine, sign):
    first = lax.rem(lane(value.shape), HEAD_DIM) < HEAD_DIM // 2
    other = jnp.where(
        first, pltpu.roll(value, 128 - HEAD_DIM // 2, 1), pltpu.roll(value, HEAD_DIM // 2, 1)
    )
    return value * cosine + sign * other * sine


def project_body(x_ref, gain_ref, w_ref, cos_ref, sin_ref, normed_ref, q_ref, kv_ref):
    x = x_ref[0].astype(f32)
    scale = lax.rsqrt(jnp.mean(x * x, axis=1, keepdims=True) + epsilon)
    normed = (x * scale * gain_ref[...]).astype(bf16)
    normed_ref[0] = normed
    cosine, sine = cos_ref[...], sin_ref[...]
    q_width, k_width = HEADS * HEAD_DIM, KV_HEADS * HEAD_DIM
    for start in range(0, q_width + 2 * k_width, 512):
        part = mm(normed, w_ref[:, start : start + 512], ((1,), (0,)))
        for inner in range(0, 512, 128):
            at = start + inner
            value = part[:, inner : inner + 128]
            if at < q_width:
                q_ref[0, :, at : at + 128] = turn(value, cosine, sine, 1.0).astype(bf16)
            elif at < q_width + k_width:
                at -= q_width
                kv_ref[0, :, at : at + 128] = turn(value, cosine, sine, 1.0).astype(bf16)
            else:
                at -= q_width
                kv_ref[0, :, at : at + 128] = value.astype(bf16)


def project(tokens, gain, w_qkv, cosine, sine):
    micro, rows, _ = tokens.shape
    block = pl.BlockSpec((1, rows, D), lambda m: (m, 0, 0))
    table = pl.BlockSpec((rows, 128), lambda m: (0, 0))
    shape = jax.ShapeDtypeStruct((micro, rows, D), bf16)
    return pl.pallas_call(
        project_body,
        grid=(micro,),
        in_specs=[
            block,
            pl.BlockSpec((1, D), lambda m: (0, 0)),
            pl.BlockSpec(w_qkv.shape, lambda m: (0, 0)),
            table,
            table,
        ],
        out_specs=[block, block, block],
        out_shape=[shape, shape, shape],
        cost_estimate=cost(7),
        compiler_params=params(),
    )(tokens, gain, w_qkv, cosine, sine)


def stack_heads(block, scale):
    wide = block.astype(f32) * scale
    result = []
    for p in range(2):
        part = wide[:, p * 128 : (p + 1) * 128]
        half = (lane(part.shape) >= HEAD_DIM) == (p == 1)
        for h in range(2):
            moved = part if h == p else pltpu.roll(part, HEAD_DIM, 1)
            result.append(jnp.where(half, moved, 0.0).astype(bf16))
    return jnp.concatenate(result, axis=0)


def unstack_heads(stacked, rows):
    result = []
    for p in range(2):
        pieces = []
        for h in range(2):
            i = 2 * p + h
            part = stacked[i * rows : (i + 1) * rows]
            pieces.append(part if h == p else pltpu.roll(part, HEAD_DIM, 1))
        result.append(jnp.where(lane(pieces[0].shape) < HEAD_DIM, pieces[0], pieces[1]))
    return result


def attend_body(
    q_ref, pk_ref, pv_ref, ok_ref, ov_ref, bias_ref, x_ref, w_ref, gain_ref,
    att_ref, lse_ref, hidden_ref, low_ref, all_ref,
):
    j = pl.program_id(0)
    rows = q_ref.shape[1]
    q = stack_heads(q_ref[0], score_scale)
    k = jnp.concatenate([pk_ref[0], ok_ref[0, PROMPT_DEV:, :]], axis=0)
    v = jnp.concatenate([pv_ref[0], ov_ref[0, PROMPT_DEV:, :]], axis=0)
    scores = mm(k, q, ((1,), (1,))) + bias_ref[...]
    largest = jnp.max(scores, axis=0, keepdims=True)
    raised = jnp.exp(scores - largest)
    total = jnp.sum(raised, axis=0, keepdims=True)
    weights = (raised * (1.0 / total)).astype(bf16)
    lse_ref[0] = largest + jnp.log(total)
    mixed = mm(v, weights, ((0,), (0,))).T
    for p, part in enumerate(unstack_heads(mixed, rows)):
        at = pl.multiple_of(j * 256 + p * 128, 128)
        att_ref[0, :, p * 128 : (p + 1) * 128] = part.astype(bf16)
        all_ref[:, pl.ds(at, 128)] = part.astype(bf16)

    @pl.when(j == pl.num_programs(0) - 1)
    def _():
        branch = mm(all_ref[...], w_ref[...], ((1,), (0,)))
        hidden = x_ref[0].astype(f32) + branch_scale * branch
        hidden_ref[0] = hidden
        scale = lax.rsqrt(jnp.mean(hidden * hidden, axis=1, keepdims=True) + epsilon)
        low_ref[0] = (hidden * scale * gain_ref[...]).astype(bf16)


def attend(micro, q, kv, prompt, bias, tokens, w_out, gain):
    rows, prompt_rows = q.shape[1], prompt.shape[1]
    steps = KV_HEADS // 2
    full = pl.BlockSpec((1, rows, D), lambda j: (micro, 0, 0))
    one = pl.BlockSpec((1, rows, D), lambda j: (0, 0, 0))
    return pl.pallas_call(
        attend_body,
        grid=(steps,),
        in_specs=[
            pl.BlockSpec((1, rows, 256), lambda j: (micro, 0, j)),
            pl.BlockSpec((1, prompt_rows, 128), lambda j: (micro, 0, j)),
            pl.BlockSpec((1, prompt_rows, 128), lambda j: (micro, 0, j + steps)),
            pl.BlockSpec((1, rows, 128), lambda j: (micro, 0, j)),
            pl.BlockSpec((1, rows, 128), lambda j: (micro, 0, j + steps)),
            pl.BlockSpec(bias.shape, lambda j: (0, 0)),
            full,
            pl.BlockSpec(w_out.shape, lambda j: (0, 0)),
            pl.BlockSpec((1, D), lambda j: (0, 0)),
        ],
        out_specs=[
            pl.BlockSpec((1, rows, 256), lambda j: (0, 0, j)),
            pl.BlockSpec((1, 1, 4 * rows), lambda j: (j, 0, 0)),
            one,
            one,
        ],
        out_shape=[
            jax.ShapeDtypeStruct((1, rows, D), bf16),
            jax.ShapeDtypeStruct((steps, 1, 4 * rows), f32),
            jax.ShapeDtypeStruct((1, rows, D), f32),
            jax.ShapeDtypeStruct((1, rows, D), bf16),
        ],
        scratch_shapes=[pltpu.VMEM((rows, D), bf16)],
        cost_estimate=cost(12),
        compiler_params=params(),
    )(q, prompt, prompt, kv, kv, bias, tokens, w_out, gain)


def norm_back(value, gain, grad):
    scale = lax.rsqrt(jnp.mean(value * value, axis=1, keepdims=True) + epsilon)
    scaled = grad * gain
    inner = jnp.mean(scaled * value, axis=1, keepdims=True)
    back = scale * scaled - value * (scale * scale * scale * inner)
    return back, jnp.sum(grad * value * scale, axis=0, keepdims=True)


def middle_body(*refs, terms):
    term_refs = refs[:terms]
    (logit_ref, router_ref, hidden_ref, gain_ref, cot_ref, w_ref) = refs[terms : terms + 6]
    grad_hidden_ref, branch_ref, att_ref, gain_out_ref = refs[terms + 6 :]
    total = mm(logit_ref[0], router_ref[...], ((0,), (1,)))
    for ref in term_refs:
        total = total + ref[0].astype(f32)
    back, gain_grad = norm_back(hidden_ref[0], gain_ref[...], total)
    grad_hidden = cot_ref[0].astype(f32) + back
    grad_hidden_ref[0] = grad_hidden
    branch = (branch_scale * grad_hidden).astype(bf16)
    branch_ref[0] = branch
    att_ref[0] = mm(branch, w_ref[...], ((1,), (1,))).astype(bf16)

    @pl.when(pl.program_id(0) == 0)
    def _():
        gain_out_ref[...] = gain_grad

    @pl.when(pl.program_id(0) != 0)
    def _():
        gain_out_ref[...] += gain_grad


def middle_back(terms, grad_logits, w_router, hidden, gain, cotangent, w_out):
    micro, rows, _ = hidden.shape
    block = pl.BlockSpec((1, rows, D), lambda m: (m, 0, 0))
    row = pl.BlockSpec((1, D), lambda m: (0, 0))
    return pl.pallas_call(
        functools.partial(middle_body, terms=len(terms)),
        grid=(micro,),
        in_specs=[block] * len(terms)
        + [
            pl.BlockSpec((1, EXPERTS, rows), lambda m: (m, 0, 0)),
            pl.BlockSpec(w_router.shape, lambda m: (0, 0)),
            block,
            row,
            block,
            pl.BlockSpec(w_out.shape, lambda m: (0, 0)),
        ],
        out_specs=[block, block, block, row],
        out_shape=[
            jax.ShapeDtypeStruct((micro, rows, D), f32),
            jax.ShapeDtypeStruct((micro, rows, D), bf16),
            jax.ShapeDtypeStruct((micro, rows, D), bf16),
            jax.ShapeDtypeStruct((1, D), f32),
        ],
        cost_estimate=cost(8),
        compiler_params=params(),
    )(*terms, grad_logits, w_router, hidden, gain, cotangent, w_out)


def attend_back_body(
    q_ref, pk_ref, pv_ref, ok_ref, ov_ref, bias_ref, lse_ref, grad_ref, cos_ref, sin_ref,
    gq_ref, gpk_ref, gpv_ref, gok_ref, gov_ref,
):
    rows, prompt_rows = q_ref.shape[1], pk_ref.shape[1]
    q = stack_heads(q_ref[0], score_scale)
    grad = stack_heads(grad_ref[0], 1.0)
    k = jnp.concatenate([pk_ref[0], ok_ref[0, PROMPT_DEV:, :]], axis=0)
    v = jnp.concatenate([pv_ref[0], ov_ref[0, PROMPT_DEV:, :]], axis=0)
    probs = jnp.exp(mm(k, q, ((1,), (1,))) + bias_ref[...] - lse_ref[0, 0])
    grad_probs = mm(v, grad, ((1,), (1,)))
    centre = jnp.sum(probs * grad_probs, axis=0, keepdims=True)
    grad_scores = (probs * (grad_probs - centre)).astype(bf16)
    grad_v = mm(probs.astype(bf16), grad, ((1,), (0,)))
    grad_k = mm(grad_scores, q, ((1,), (0,)))
    grad_q = mm(k, grad_scores, ((0,), (0,))).T * score_scale
    cosine, sine = cos_ref[...], sin_ref[...]
    for p, part in enumerate(unstack_heads(grad_q, rows)):
        gq_ref[0, :, p * 128 : (p + 1) * 128] = turn(part, cosine, sine, -1.0).astype(bf16)
    gpk_ref[0] = grad_k[:prompt_rows].astype(bf16)
    gpv_ref[0] = grad_v[:prompt_rows].astype(bf16)
    gok_ref[0] = turn(
        grad_k[prompt_rows:], cosine[PROMPT_DEV:], sine[PROMPT_DEV:], -1.0
    ).astype(bf16)
    gov_ref[0] = grad_v[prompt_rows:].astype(bf16)


def attend_back(q, kv, prompt, bias, lse, grad, cosine, sine):
    micro, rows, _ = q.shape
    prompt_rows = prompt.shape[1]
    own_rows = rows - PROMPT_DEV
    steps = KV_HEADS // 2
    wide = pl.BlockSpec((1, rows, 256), lambda m, j: (m, 0, j))
    table = pl.BlockSpec((rows, 128), lambda m, j: (0, 0))
    prompt_spec = pl.BlockSpec((1, prompt_rows, 128), lambda m, j: (m, 0, j))
    own_spec = pl.BlockSpec((1, own_rows, 128), lambda m, j: (m, 0, j))
    k_width = KV_HEADS * HEAD_DIM
    return pl.pallas_call(
        attend_back_body,
        grid=(micro, steps),
        in_specs=[
            wide,
            prompt_spec,
            pl.BlockSpec((1, prompt_rows, 128), lambda m, j: (m, 0, j + steps)),
            pl.BlockSpec((1, rows, 128), lambda m, j: (m, 0, j)),
            pl.BlockSpec((1, rows, 128), lambda m, j: (m, 0, j + steps)),
            pl.BlockSpec(bias.shape, lambda m, j: (0, 0)),
            pl.BlockSpec((1, 1, 1, 4 * rows), lambda m, j: (m, j, 0, 0)),
            wide,
            table,
            table,
        ],
        out_specs=[wide, prompt_spec, prompt_spec, own_spec, own_spec],
        out_shape=[
            jax.ShapeDtypeStruct((micro, rows, D), bf16),
            jax.ShapeDtypeStruct((micro, prompt_rows, k_width), bf16),
            jax.ShapeDtypeStruct((micro, prompt_rows, k_width), bf16),
            jax.ShapeDtypeStruct((micro, own_rows, k_width), bf16),
            jax.ShapeDtypeStruct((micro, own_rows, k_width), bf16),
        ],
        cost_estimate=cost(23),
        compiler_params=pltpu.CompilerParams(
            vmem_limit_bytes=vmem_limit, dimension_semantics=("arbitrary", "arbitrary")
        ),
    )(q, prompt, prompt, kv, kv, bias, lse, grad, cosine, sine)


def weight_body(*refs, terms):
    normed_ref, gq_ref, gok_ref, gov_ref = refs[:4]
    k_terms, v_terms = refs[4 : 4 + terms], refs[4 + terms : 4 + 2 * terms]
    cos_ref, sin_ref, gp_ref, out_ref, acc_ref = refs[4 + 2 * terms :]
    q_width, k_width = HEADS * HEAD_DIM, KV_HEADS * HEAD_DIM
    gp_ref[0, :, :q_width] = gq_ref[0]
    gp_ref[0, PROMPT_DEV:, q_width : q_width + k_width] = gok_ref[0]
    gp_ref[0, PROMPT_DEV:, q_width + k_width :] = gov_ref[0]
    prompt_k, prompt_v = [sum(ref[0].astype(f32) for ref in group) for group in (k_terms, v_terms)]
    cosine, sine = cos_ref[:PROMPT_DEV, :], sin_ref[:PROMPT_DEV, :]
    for at in range(0, k_width, 128):
        turned = turn(prompt_k[:, at : at + 128], cosine, sine, -1.0)
        gp_ref[0, :PROMPT_DEV, q_width + at : q_width + at + 128] = turned.astype(bf16)
    gp_ref[0, :PROMPT_DEV, q_width + k_width :] = prompt_v.astype(bf16)
    part = mm(normed_ref[0], gp_ref[0], ((0,), (0,)))
    m = pl.program_id(0)

    @pl.when(m == 0)
    def _():
        acc_ref[...] = part

    @pl.when(m != 0)
    def _():
        acc_ref[...] += part

    @pl.when(m == pl.num_programs(0) - 1)
    def _():
        out_ref[...] = acc_ref[...].astype(bf16)


def weight_back(normed, gq, gok, gov, k_terms, v_terms, cosine, sine):
    micro, rows, _ = normed.shape
    k_width = KV_HEADS * HEAD_DIM
    wide = pl.BlockSpec((1, rows, D), lambda m: (m, 0, 0))
    own = pl.BlockSpec((1, rows - PROMPT_DEV, k_width), lambda m: (m, 0, 0))
    term = pl.BlockSpec((1, PROMPT_DEV, k_width), lambda m: (m, 0, 0))
    table = pl.BlockSpec((rows, 128), lambda m: (0, 0))
    return pl.pallas_call(
        functools.partial(weight_body, terms=len(k_terms)),
        grid=(micro,),
        in_specs=[wide, wide, own, own] + [term] * (2 * len(k_terms)) + [table, table],
        out_specs=[
            pl.BlockSpec((1, rows, 2 * D), lambda m: (m, 0, 0)),
            pl.BlockSpec((D, 2 * D), lambda m: (0, 0)),
        ],
        out_shape=[
            jax.ShapeDtypeStruct((micro, rows, 2 * D), bf16),
            jax.ShapeDtypeStruct((D, 2 * D), bf16),
        ],
        scratch_shapes=[pltpu.VMEM((D, 2 * D), f32)],
        cost_estimate=cost(11),
        compiler_params=params(),
    )(normed, gq, gok, gov, *k_terms, *v_terms, cosine, sine)


def token_body(gp_ref, w_ref, x_ref, gain_ref, hidden_ref, out_ref, gain_out_ref):
    grad = mm(gp_ref[0], w_ref[...], ((1,), (1,)))
    back, gain_grad = norm_back(x_ref[0].astype(f32), gain_ref[...], grad)
    out_ref[0] = (hidden_ref[0] + back).astype(bf16)

    @pl.when(pl.program_id(0) == 0)
    def _():
        gain_out_ref[...] = gain_grad

    @pl.when(pl.program_id(0) != 0)
    def _():
        gain_out_ref[...] += gain_grad


def token_back(gp, w_qkv, tokens, gain, grad_hidden):
    micro, rows, _ = tokens.shape
    block = pl.BlockSpec((1, rows, D), lambda m: (m, 0, 0))
    row = pl.BlockSpec((1, D), lambda m: (0, 0))
    return pl.pallas_call(
        token_body,
        grid=(micro,),
        in_specs=[
            pl.BlockSpec((1, rows, 2 * D), lambda m: (m, 0, 0)),
            pl.BlockSpec(w_qkv.shape, lambda m: (0, 0)),
            block,
            row,
            block,
        ],
        out_specs=[block, row],
        out_shape=[
            jax.ShapeDtypeStruct((micro, rows, D), bf16),
            jax.ShapeDtypeStruct((1, D), f32),
        ],
        cost_estimate=cost(8),
        compiler_params=params(),
    )(gp, w_qkv, tokens, gain, grad_hidden)


def halve(value, axis, swap, bit, *before):
    rows = value.shape[0] // 2
    keep = lax.dynamic_slice_in_dim(value, bit * rows, rows, 0)
    send = lax.dynamic_slice_in_dim(value, (1 - bit) * rows, rows, 0)
    got = after(lax.ppermute(send, axis, swap), *before)
    return (keep.astype(f32) + got.astype(f32)).astype(bf16)


def finish_dense_body(table_ref, *refs, pieces):
    first_refs, second_refs = refs[:pieces], refs[pieces : 2 * pieces]
    qkv_ref, out_ref = refs[2 * pieces :]
    width = first_refs[0].shape[1]
    rest = qkv_ref.shape[1] - width
    for i in range(pieces):

        @pl.when(pl.program_id(0) == i)
        def _(i=i):
            qkv_ref[:, :width] = first_refs[i][...].astype(f32)
            qkv_ref[:, width:] = second_refs[i][:, :rest].astype(f32)
            out_ref[...] = second_refs[i][:, rest:].astype(f32)


def finish_dense(table, first, second):
    pieces = len(first)
    height = first[0].shape[0]
    grid_spec = pltpu.PrefetchScalarGridSpec(
        num_scalar_prefetch=1,
        grid=(pieces,),
        in_specs=[full_spec(piece) for piece in first + second],
        out_specs=[
            pl.BlockSpec((height, 2 * D), lambda i, t: (t[i], 0)),
            pl.BlockSpec((height, D), lambda i, t: (t[i], 0)),
        ],
    )
    return pl.pallas_call(
        functools.partial(finish_dense_body, pieces=pieces),
        grid_spec=grid_spec,
        out_shape=[
            jax.ShapeDtypeStruct((pieces * height, 2 * D), f32),
            jax.ShapeDtypeStruct((pieces * height, D), f32),
        ],
        cost_estimate=cost(9),
        compiler_params=params(),
    )(table, *first, *second)


def local(
    tokens, cotangent, expert_ids, norm_attn, w_qkv, w_out, norm_moe, w_router, w_gate_up, w_down
):
    groups = lax.axis_size("expert")
    dp_size = lax.axis_size("dp")
    member = lax.axis_index("expert")
    dp_index = lax.axis_index("dp")
    rows_all = tokens.shape[0]
    tok_rows = rows_all // MICRO
    local_experts = w_gate_up.shape[0]
    prompt_len = PROMPT_DEV * groups
    k_width = KV_HEADS * HEAD_DIM
    pairs = dp_size // 2
    blocks = groups * MICRO
    attn_gain = norm_attn.reshape(1, D)
    moe_gain = norm_moe.reshape(1, D)
    token_rows = tokens.reshape(MICRO, tok_rows, D)
    cot_rows = cotangent.reshape(MICRO, tok_rows, D)

    local_index = jnp.arange(tok_rows, dtype=jnp.int32)
    positions = jnp.where(
        local_index < PROMPT_DEV,
        member * PROMPT_DEV + local_index,
        prompt_len + local_index - PROMPT_DEV,
    )
    half_dim = HEAD_DIM // 2
    inverse = 10000.0 ** (-2.0 * jnp.arange(half_dim, dtype=f32) / HEAD_DIM)
    angles = positions.astype(f32)[:, None] * inverse[None, :]
    cosine = jnp.tile(jnp.cos(angles), (1, 128 // half_dim))
    sine = jnp.tile(jnp.sin(angles), (1, 128 // half_dim))
    sine = jnp.where(jnp.arange(128)[None, :] % HEAD_DIM < half_dim, -sine, sine)
    rows_of = []
    for s in range(groups // 2):
        for c in range(2):
            place = lax.rem(member // 2 + s, groups // 2) * 2 + lax.rem(member + c, 2)
            rows_of.append(place * PROMPT_DEV + jnp.arange(PROMPT_DEV, dtype=jnp.int32))
    key_positions = jnp.concatenate(
        rows_of + [prompt_len + jnp.arange(tok_rows - PROMPT_DEV, dtype=jnp.int32)]
    )
    bias = jnp.where(
        key_positions[:, None] <= jnp.tile(positions, HEADS // (KV_HEADS // 2))[None, :],
        0.0,
        masked_score,
    )

    first_expert = member * local_experts
    ids_t = gather_members(expert_ids.reshape(MICRO, tok_rows, TOP).transpose(0, 2, 1), groups)
    ids_all = lax.rem(jnp.concatenate(ids_t, axis=0) + (EXPERTS - first_expert), EXPERTS)
    cot_pieces = [gather_members(cot_rows[:1], groups)]
    normed, queries, key_value = project(token_rows, attn_gain, w_qkv, cosine, sine)
    prompt_pieces = gather_members(
        after(key_value[:, :PROMPT_DEV], cot_pieces[0][2]), groups
    )
    prompt = jnp.concatenate(prompt_pieces, axis=1)
    cot_pieces += [
        gather_members(after(cot_rows[m : m + 1], prompt_pieces[2]), groups)
        for m in range(1, MICRO)
    ]
    router = lax.dynamic_slice_in_dim(
        jnp.concatenate([w_router, w_router], axis=1), first_expert, EXPERTS, 1
    )

    attended, lse, hidden, moe_pieces, moe_low = [], [], [], [], []
    for m in range(MICRO):
        mask = bias if m == 0 else after(bias, moe_low[-1])
        att, log_total, hid, low = attend(
            m, queries, key_value, prompt, mask, token_rows, w_out, moe_gain
        )
        attended.append(att)
        lse.append(log_total[None])
        hidden.append(hid)
        moe_low.append(low)
        moe_pieces.append(gather_column(low, groups))

    def by_block(pieces):
        return [pieces[m][g] for g in range(groups) for m in range(MICRO)]

    d_rows, slots = pick_grads(after(ids_all, moe_low[-1]), by_block(cot_pieces), local_experts)
    moe_pieces = [gather_cores(column, groups, slots) for column in moe_pieces]
    attended = jnp.concatenate(attended, axis=0)
    lse = jnp.concatenate(lse, axis=0)
    hidden = jnp.concatenate(hidden, axis=0)
    moe_low = jnp.concatenate(moe_low, axis=0)

    x_rows, slot_gate, gates = pick_tokens(ids_all, slots, router, by_block(moe_pieces))
    slot_rows = blocks * SLOTS
    x_rows = x_rows.reshape(local_experts, slot_rows, D)
    d_rows = d_rows.reshape(local_experts, slot_rows, D)
    slot_gate = slot_gate.reshape(local_experts, slot_rows, 128)
    parity = lax.rem(dp_index, 2).astype(jnp.int32)
    swap_x = [(d, d ^ 1) for d in range(dp_size)]
    swap_y = [(m, m ^ 2) for m in range(groups)]
    swap_core = [(m, m ^ 1) for m in range(groups)]
    z_groups = [[d for d in range(dp_size) if d % 2 == r] for r in range(2)]
    piece = (D + FF) // (2 * pairs)

    def sum_z(value):
        count, _, height, _ = value.shape
        return lax.psum_scatter(
            value.reshape(count, pairs * height, D),
            "dp",
            scatter_dimension=1,
            axis_index_groups=z_groups,
            tiled=True,
        )

    plan = CHUNKS
    if sum(count for count, _ in plan) != local_experts:
        plan = tuple((1, e == 0) for e in range(local_experts))
    outs, backs, dots, halves, parts = [], [], [], {}, {}

    held = {}

    def add_x(i, *before, hold=False):
        keep, got = halves.pop(i)
        got = after(got, *before)
        half = (keep.astype(f32) + got.astype(f32)).astype(bf16)
        if hold:
            held[i] = half
        else:
            parts[i] = sum_z(half)
        return half

    first = 0
    order = parity.reshape(1)
    for i, (count, whole) in enumerate(plan):
        if i:
            order = after(order, outs[-1])
        if i == 3:
            order = after(order, add_x(1, outs[-1]))
        if i == 4:
            order = after(order, parts[0])
        out, back, dot, *sums = expert_chunk(
            order, first, count, pairs, not whole, x_rows, d_rows, slot_gate, w_gate_up, w_down
        )
        shape = (count, blocks, SLOTS)
        outs.append(out.reshape(shape + (D,)))
        backs.append(back.reshape(shape + (D,)))
        dots.append(dot.reshape(shape + (128,)))
        if whole:
            parts[i] = sum_z(sums[0])
        else:
            halves[i] = (sums[0], lax.ppermute(sums[1], "dp", swap_x))
        first += count

    def left(i, *before, hold=False):
        return [add_x(i, *before, hold=hold)] if i in halves else []

    def sent(i):
        return [parts[i]] if i in parts else []

    *back_sum, back_dots = sum_rows(slots, backs, dots)

    def pieces_of(value):
        return [value[j * MICRO : (j + 1) * MICRO] for j in range(groups)]

    dot_pieces = exchange_members(pieces_of(back_dots), groups)
    back_terms, back_sent = return_members(back_sum, groups, *dot_pieces)
    token_dots = jnp.zeros((MICRO, EXPERTS, tok_rows), f32)
    for s in range(groups // 2):
        for c in range(2):
            place = lax.rem(member // 2 + groups // 2 - s, groups // 2) * 2 + lax.rem(
                member + c, 2
            )
            label = lax.rem(place + groups - member, groups) * local_experts
            token_dots = lax.dynamic_update_slice_in_dim(
                token_dots, dot_pieces[2 * s + c], label, 1
            )
    own_gates = gates[:MICRO]
    centre = jnp.sum(own_gates * token_dots, axis=1, keepdims=True)
    grad_logits = (own_gates * (token_dots - centre)).astype(bf16)
    mixed = sum_rows(
        after(slots, *back_sent, *sent(1), *left(2, back_sum[0], hold=True)), outs
    )
    mix_terms, _ = return_members(mixed, groups)

    grad_hidden, grad_branch, grad_attended, grad_norm_moe = middle_back(
        back_terms, grad_logits, router, hidden, moe_gain, after(cot_rows, *mixed, *sent(4)), w_out
    )
    grad_router = jnp.einsum("bet,btd->ed", grad_logits, moe_low, preferred_element_type=f32)
    grad_out = jnp.einsum(
        "brd,bre->de", attended, grad_branch, preferred_element_type=f32
    ).astype(bf16)
    core_bit, row_bit = lax.rem(member, 2), lax.rem(member // 2, 2)
    grad_out = halve(grad_out, "expert", swap_core, core_bit)
    gq, gpk, gpv, gok, gov = attend_back(
        queries,
        key_value,
        prompt,
        after(bias, grad_out, *left(3, grad_branch)),
        lse,
        grad_attended,
        cosine,
        sine,
    )

    for i in list(held):
        parts[i] = sum_z(after(held.pop(i), gq))

    def prompt_terms(value):
        return return_members(
            [value[:, j * PROMPT_DEV : (j + 1) * PROMPT_DEV] for j in range(groups)], groups
        )[0]

    mixture = sum(after(term, gq).astype(f32) for term in mix_terms)
    output = (hidden + branch_scale * mixture).astype(bf16)
    k_terms, v_terms = prompt_terms(gpk), prompt_terms(gpv)
    grad_out = halve(after(grad_out, k_terms[2], v_terms[2]), "expert", swap_y, row_bit)
    gp, grad_qkv = weight_back(
        after(normed, *mix_terms[2:], *left(5, gq, hold=True)),
        gq,
        gok,
        gov,
        k_terms,
        v_terms,
        cosine,
        sine,
    )
    grad_tokens, grad_norm_attn = token_back(
        after(gp, grad_qkv, output), w_qkv, token_rows, attn_gain, grad_hidden
    )
    last = [add_x(i, grad_norm_attn) for i in list(halves)]
    grad_qkv = after(halve(grad_qkv, "expert", swap_core, core_bit), grad_out)
    grad_qkv = halve(grad_qkv, "expert", swap_y, row_bit, grad_norm_attn)

    whole_sums = [parts[i] for i, (_, whole) in enumerate(plan) if whole]
    whole_sums = jnp.concatenate(whole_sums, axis=0)
    swapped = lax.ppermute(after(whole_sums[:, piece:], *last), "dp", swap_x)
    whole_sums = (whole_sums[:, :piece].astype(f32) + swapped.astype(f32)).astype(bf16)
    pieces, at = [], 0
    for i, (count, whole) in enumerate(plan):
        pieces.append(whole_sums[at : at + count] if whole else parts.get(i))
        at += count if whole else 0

    small = jnp.concatenate(
        [
            lax.dynamic_slice_in_dim(
                jnp.concatenate([grad_router, grad_router], axis=0),
                EXPERTS - first_expert,
                EXPERTS,
                0,
            ),
            grad_norm_attn,
            grad_norm_moe,
            jnp.zeros((14, D), f32),
        ],
        axis=0,
    )
    small = after(small, *last)
    for axis, swap in (("expert", swap_core), ("dp", swap_x), ("expert", swap_y)):
        small = small + lax.ppermute(small, axis, swap)
    dense = jnp.concatenate([grad_qkv, grad_out], axis=1)
    dense = after(halve(dense, "dp", swap_x, parity), *sent(2), *sent(3))
    for i in list(held):
        parts[i] = sum_z(after(held.pop(i), dense))
        pieces[i] = parts[i]
    dense_rows = dense.shape[0]
    dense = jnp.concatenate([dense, small.reshape(-1, 3 * D).astype(bf16)], axis=0)
    dense = lax.psum(dense, "dp", axis_index_groups=z_groups)
    if groups > 4:
        rest = [[m for m in range(groups) if m % 4 == r] for r in range(4)]
        dense = lax.psum(dense, "expert", axis_index_groups=rest)
    small = dense[dense_rows:].reshape(-1, D).astype(f32)
    dense = dense[:dense_rows]
    width = dense.shape[1] // 2
    left_own, right_own = dense[:, :width], dense[:, width:]
    left_x = lax.ppermute(left_own, "dp", swap_x)
    right_y = lax.ppermute(right_own, "expert", swap_y)
    left_four = [left_own, left_x] + [
        lax.ppermute(value, "expert", swap_y) for value in (left_own, left_x)
    ]
    right_x = [lax.ppermute(value, "dp", swap_x) for value in (right_own, right_y)]
    right_four = [right_own, right_x[0], right_y, right_x[1]]
    if 5 in parts:
        pieces[5] = after(pieces[5], left_four[3], right_four[3])
    left_all = left_four + [core_swap(value, groups) for value in left_four]
    right_all = right_four + [core_swap(value, groups) for value in right_four]
    base = core_bit * 4 + row_bit * 2 + parity
    table = jnp.bitwise_xor(base, jnp.arange(8, dtype=jnp.int32)).astype(jnp.int32)
    full_qkv, full_out = finish_dense(table, left_all, right_all)

    experts_sum = jnp.concatenate(pieces, axis=0).astype(f32)
    gu_piece = D // (2 * pairs)
    return (
        output.reshape(rows_all, D),
        grad_tokens.reshape(rows_all, D),
        small[EXPERTS],
        full_qkv,
        full_out,
        small[EXPERTS + 1],
        small[:EXPERTS].T,
        experts_sum[:, :gu_piece],
        experts_sum[:, gu_piece:],
    )


def solution(mesh):
    in_specs = (
        P(("dp", "expert"), None),
        P(("dp", "expert"), None),
        P(("dp", "expert"), None),
        P(),
        P(),
        P(),
        P(),
        P(),
        P("expert", None, None),
        P("expert", None, None),
    )
    out_specs = (
        P(("dp", "expert"), None),
        P(("dp", "expert"), None),
        P(),
        P(),
        P(),
        P(),
        P(),
        P("expert", "dp", None),
        P("expert", "dp", None),
    )
    return jax.shard_map(local, mesh=mesh, in_specs=in_specs, out_specs=out_specs, check_vma=False)
```

```python
import functools

import jax
import jax.numpy as jnp
from jax import lax
from jax.experimental import pallas as pl
from jax.experimental.pallas import tpu as pltpu
from jax.sharding import PartitionSpec as P

D = 1024
HEADS = 16
KV_HEADS = 8
HEAD_DIM = 64
FF = 512
EXPERTS = 32
TOP = 8
PROMPT_DEV = 64
MICRO = 2
CAP = 100
SLOTS = 112
CHUNKS = ((1, True), (1, False), (2, False), (2, False), (1, True), (1, False))


epsilon = 1e-06
score_scale = 1.0 / 64.0
branch_scale = 0.22
masked_score = -1e30

f32 = jnp.float32
bf16 = jnp.bfloat16
vmem_limit = 60 * 1024 * 1024


def params():
    return pltpu.CompilerParams(
        vmem_limit_bytes=vmem_limit, dimension_semantics=("arbitrary",)
    )


def cost(micros):
    return pl.CostEstimate(flops=int(micros * 1.15e9), bytes_accessed=0, transcendentals=0)


def mm(left, right, dims):
    return lax.dot_general(left, right, (dims, ((), ())), preferred_element_type=f32)


def fill_one_hot(slot_rows, onehot_ref):
    experts, rows = slot_rows.shape
    place = lax.broadcasted_iota(jnp.int32, (SLOTS, rows), 0)
    for e in range(experts):
        hit = place == slot_rows[e : e + 1, :]
        onehot_ref[e * SLOTS : (e + 1) * SLOTS, :] = jnp.where(hit, 1.0, 0.0).astype(bf16)


def chosen_of(ids, count):
    rows = ids.shape[1]
    label = lax.broadcasted_iota(jnp.int32, (count, rows), 0)
    hit = ids[0:1, :] == label
    for k in range(1, ids.shape[0]):
        hit = hit | (ids[k : k + 1, :] == label)
    return hit


def select_block(row_refs, rows_ref):
    b = pl.program_id(0)
    at = 0
    for ref in row_refs:
        for i in range(ref.shape[0]):

            @pl.when(b == at)
            def _(ref=ref, i=i):
                rows_ref[...] = ref[i]

            at += 1


def store_picked(onehot_ref, rows_ref, out_ref):
    picked = mm(onehot_ref[...], rows_ref[...], ((1,), (0,))).astype(bf16)
    for e in range(out_ref.shape[0]):
        out_ref[e, 0] = picked[e * SLOTS : (e + 1) * SLOTS]


def pick_grad_body(*refs, pieces):
    ids_ref = refs[0]
    row_refs = refs[1 : 1 + pieces]
    out_ref, slot_ref, onehot_ref, rows_ref, earlier_ref = refs[1 + pieces :]
    experts, rows = slot_ref.shape[1], slot_ref.shape[2]

    @pl.when(pl.program_id(0) == 0)
    def _():
        first = lax.broadcasted_iota(jnp.int32, (rows, rows), 0)
        second = lax.broadcasted_iota(jnp.int32, (rows, rows), 1)
        earlier_ref[...] = jnp.where(first < second, 1.0, 0.0).astype(bf16)

    select_block(row_refs, rows_ref)
    hit = chosen_of(ids_ref[0], 8)
    rank = mm(jnp.where(hit, 1.0, 0.0).astype(bf16), earlier_ref[...], ((1,), (0,)))
    slots = jnp.where(hit, rank, -1.0).astype(jnp.int32)[:experts]
    slot_ref[0] = slots
    fill_one_hot(slots, onehot_ref)
    store_picked(onehot_ref, rows_ref, out_ref)


def full_spec(array):
    zeros = (0,) * array.ndim
    return pl.BlockSpec(array.shape, lambda *_: zeros)


def pick_grads(ids, pieces, experts):
    blocks, top, tok = ids.shape
    return pl.pallas_call(
        functools.partial(pick_grad_body, pieces=len(pieces)),
        grid=(blocks,),
        in_specs=[pl.BlockSpec((1, top, tok), lambda b: (b, 0, 0))]
        + [full_spec(piece) for piece in pieces],
        out_specs=[
            pl.BlockSpec((experts, 1, SLOTS, D), lambda b: (0, b, 0, 0)),
            pl.BlockSpec((1, experts, tok), lambda b: (b, 0, 0)),
        ],
        out_shape=[
            jax.ShapeDtypeStruct((experts, blocks, SLOTS, D), bf16),
            jax.ShapeDtypeStruct((blocks, experts, tok), jnp.int32),
        ],
        scratch_shapes=[
            pltpu.VMEM((experts * SLOTS, tok), bf16),
            pltpu.VMEM((tok, D), bf16),
            pltpu.VMEM((tok, tok), bf16),
        ],
        cost_estimate=cost(15),
        compiler_params=params(),
    )(ids, *pieces)


def pick_token_body(*refs, pieces):
    ids_ref, slot_ref, router_ref = refs[:3]
    row_refs = refs[3 : 3 + pieces]
    out_ref, slot_gate_ref, gate_ref, onehot_ref, rows_ref = refs[3 + pieces :]
    experts, rows = slot_ref.shape[1], slot_ref.shape[2]
    select_block(row_refs, rows_ref)
    logits = mm(router_ref[...], rows_ref[...], ((0,), (1,)))
    hit = chosen_of(ids_ref[0], EXPERTS)
    masked = jnp.where(hit, logits, masked_score)
    raised = jnp.where(hit, jnp.exp(masked - jnp.max(masked, axis=0, keepdims=True)), 0.0)
    gates = raised / jnp.sum(raised, axis=0, keepdims=True)
    gate_ref[0] = gates
    fill_one_hot(slot_ref[0], onehot_ref)
    store_picked(onehot_ref, rows_ref, out_ref)
    place = lax.broadcasted_iota(jnp.int32, (SLOTS, rows), 0)
    for e in range(experts):
        here = place == slot_ref[0, e : e + 1, :]
        gate = jnp.sum(jnp.where(here, gates[e : e + 1, :], 0.0), axis=1, keepdims=True)
        slot_gate_ref[e, 0] = jnp.broadcast_to(gate, (SLOTS, 128))


def pick_tokens(ids, slots, w_router, pieces):
    blocks, experts, tok = slots.shape
    return pl.pallas_call(
        functools.partial(pick_token_body, pieces=len(pieces)),
        grid=(blocks,),
        in_specs=[
            pl.BlockSpec((1, ids.shape[1], tok), lambda b: (b, 0, 0)),
            pl.BlockSpec((1, experts, tok), lambda b: (b, 0, 0)),
            full_spec(w_router),
        ]
        + [full_spec(piece) for piece in pieces],
        out_specs=[
            pl.BlockSpec((experts, 1, SLOTS, D), lambda b: (0, b, 0, 0)),
            pl.BlockSpec((experts, 1, SLOTS, 128), lambda b: (0, b, 0, 0)),
            pl.BlockSpec((1, EXPERTS, tok), lambda b: (b, 0, 0)),
        ],
        out_shape=[
            jax.ShapeDtypeStruct((experts, blocks, SLOTS, D), bf16),
            jax.ShapeDtypeStruct((experts, blocks, SLOTS, 128), f32),
            jax.ShapeDtypeStruct((blocks, EXPERTS, tok), f32),
        ],
        scratch_shapes=[pltpu.VMEM((experts * SLOTS, tok), bf16), pltpu.VMEM((tok, D), bf16)],
        cost_estimate=cost(17),
        compiler_params=params(),
    )(ids, slots, w_router, *pieces)


def sum_rows_body(*refs, chunks, with_dots):
    slot_ref = refs[0]
    row_refs = refs[1 : 1 + chunks]
    refs = refs[1 + chunks :]
    if with_dots:
        dot_refs, refs = refs[:chunks], refs[chunks:]
        back_ref, onehot_ref, flat_ref = refs[-3:]
        out_refs = refs[:-3]
    else:
        onehot_ref, flat_ref = refs[-2:]
        out_refs = refs[:-2]
    fill_one_hot(slot_ref[0], onehot_ref)
    e = 0
    for ref in row_refs:
        for i in range(ref.shape[0]):
            flat_ref[e * SLOTS : (e + 1) * SLOTS, :] = ref[i, 0]
            e += 1
    total = mm(onehot_ref[...], flat_ref[...], ((0,), (0,))).astype(bf16)
    for j, out_ref in enumerate(out_refs):

        @pl.when(pl.program_id(0) // MICRO == j)
        def _(out_ref=out_ref):
            out_ref[0] = total

    if with_dots:
        place = lax.broadcasted_iota(jnp.int32, (SLOTS, slot_ref.shape[2]), 0)
        e = 0
        for ref in dot_refs:
            for i in range(ref.shape[0]):
                hit = place == slot_ref[0, e : e + 1, :]
                back_ref[0, e : e + 1, :] = jnp.sum(
                    jnp.where(hit, ref[i, 0, :, 0:1], 0.0), axis=0, keepdims=True
                )
                e += 1


def sum_rows(slots, rows, dots=None):
    blocks, experts, tok = slots.shape

    def chunk_spec(chunk):
        return pl.BlockSpec((chunk.shape[0], 1) + chunk.shape[2:], lambda b: (0, b, 0, 0))

    in_specs = [pl.BlockSpec((1, experts, tok), lambda b: (b, 0, 0))]
    in_specs += [chunk_spec(chunk) for chunk in rows]
    args = [slots] + rows
    members = blocks // MICRO

    def member_spec(j):
        return pl.BlockSpec(
            (1, tok, D), lambda b: (jnp.clip(b - j * MICRO, 0, MICRO - 1), 0, 0)
        )

    out_shape = [jax.ShapeDtypeStruct((MICRO, tok, D), bf16)] * members
    out_specs = [member_spec(j) for j in range(members)]
    if dots is not None:
        in_specs += [chunk_spec(chunk) for chunk in dots]
        args += dots
        out_shape.append(jax.ShapeDtypeStruct((blocks, experts, tok), f32))
        out_specs.append(pl.BlockSpec((1, experts, tok), lambda b: (b, 0, 0)))
    return pl.pallas_call(
        functools.partial(sum_rows_body, chunks=len(rows), with_dots=dots is not None),
        grid=(blocks,),
        in_specs=in_specs,
        out_specs=out_specs,
        out_shape=out_shape,
        scratch_shapes=[
            pltpu.VMEM((experts * SLOTS, tok), bf16),
            pltpu.VMEM((experts * SLOTS, D), bf16),
        ],
        cost_estimate=cost(15),
        compiler_params=params(),
    )(*args)


def expert_body(
    parity_ref,
    x_ref,
    d_ref,
    gate_ref,
    wgu_ref,
    wd_ref,
    out_ref,
    back_ref,
    dots_ref,
    *part_refs,
    tile,
):
    mid_ref, grad_ref, act_ref, gu_ref, down_ref = part_refs[-5:]
    part_refs = part_refs[:-5]
    rows = x_ref.shape[1]

    def step(i, carry):
        span = pl.ds(pl.multiple_of(i * tile, tile), tile)
        hidden = mm(x_ref[0, span, :], wgu_ref[0], ((1,), (0,)))
        gate, up = hidden[:, :FF], hidden[:, FF:]
        sig = 1.0 / (1.0 + jnp.exp(-gate))
        silu = gate * sig
        middle = (silu * up).astype(bf16)
        mid_ref[span, :] = middle
        out = mm(middle, wd_ref[0], ((1,), (0,))).astype(bf16).astype(f32)
        weight = gate_ref[0, span, 0:1]
        scaled = branch_scale * d_ref[0, span, :].astype(f32)
        dots_ref[0, span, :] = jnp.broadcast_to(
            jnp.sum(scaled * out, axis=1, keepdims=True), (tile, 128)
        )
        out_ref[0, span, :] = (weight * out).astype(bf16)
        grad = (weight * scaled).astype(bf16)
        grad_ref[span, :] = grad
        grad_mid = mm(grad, wd_ref[0], ((1,), (1,)))
        act_ref[span, :FF] = (grad_mid * up * sig * (1.0 + gate * (1.0 - sig))).astype(bf16)
        act_ref[span, FF:] = (grad_mid * silu).astype(bf16)
        back_ref[0, span, :] = mm(act_ref[span, :], wgu_ref[0], ((1,), (1,))).astype(bf16)
        return carry

    lax.fori_loop(0, rows // tile, step, 0)
    gu_ref[...] = mm(x_ref[0], act_ref[...], ((0,), (0,))).astype(bf16)
    down_ref[...] = mm(mid_ref[...], grad_ref[...], ((0,), (0,))).astype(bf16)
    parity = parity_ref[0]
    pairs = part_refs[0].shape[1]
    half = (gu_ref.shape[0] + down_ref.shape[0]) // (2 * pairs)
    keep_ref, send_ref = part_refs[0], part_refs[-1]
    shift = half if len(part_refs) == 1 else 0
    start = 0
    for full in (gu_ref, down_ref):
        piece = full.shape[0] // (2 * pairs)
        for j in range(pairs):
            mine = pl.multiple_of((2 * j + parity) * piece, piece)
            other = pl.multiple_of((2 * j + 1 - parity) * piece, piece)
            keep_ref[0, j, start : start + piece, :] = full[pl.ds(mine, piece), :]
            send_ref[0, j, shift + start : shift + start + piece, :] = full[pl.ds(other, piece), :]
        start += piece


def expert_chunk(parity, first, count, pairs, split, x_rows, d_rows, slot_gate, w_gate_up, w_down):
    rows = x_rows.shape[1]
    tile = 2 * SLOTS
    mode = pl.Buffered(1 if rows > 1024 else 2)
    row_spec = pl.BlockSpec((1, rows, D), lambda e, p: (e + first, 0, 0), pipeline_mode=mode)
    col_spec = pl.BlockSpec((1, rows, 128), lambda e, p: (e + first, 0, 0))
    parts = 2 if split else 1
    piece = (D + FF) // (parts * pairs)
    part_spec = pl.BlockSpec((1, pairs, piece, D), lambda e, p: (e, 0, 0, 0))
    part_shape = jax.ShapeDtypeStruct((count, pairs, piece, D), bf16)
    out_row = pl.BlockSpec((1, rows, D), lambda e, p: (e, 0, 0))
    grid_spec = pltpu.PrefetchScalarGridSpec(
        num_scalar_prefetch=1,
        grid=(count,),
        in_specs=[
            row_spec,
            row_spec,
            col_spec,
            pl.BlockSpec((1, D, 2 * FF), lambda e, p: (e + first, 0, 0)),
            pl.BlockSpec((1, FF, D), lambda e, p: (e + first, 0, 0)),
        ],
        out_specs=[
            out_row,
            out_row,
            pl.BlockSpec((1, rows, 128), lambda e, p: (e, 0, 0)),
        ]
        + [part_spec] * parts,
        scratch_shapes=[
            pltpu.VMEM((rows, FF), bf16),
            pltpu.VMEM((rows, D), bf16),
            pltpu.VMEM((rows, 2 * FF), bf16),
            pltpu.VMEM((D, 2 * FF), bf16),
            pltpu.VMEM((FF, D), bf16),
        ],
    )
    return pl.pallas_call(
        functools.partial(expert_body, tile=tile),
        grid_spec=grid_spec,
        out_shape=[
            jax.ShapeDtypeStruct((count, rows, D), bf16),
            jax.ShapeDtypeStruct((count, rows, D), bf16),
            jax.ShapeDtypeStruct((count, rows, 128), f32),
        ]
        + [part_shape] * parts,
        cost_estimate=cost(15 * count),
        compiler_params=params(),
    )(parity, x_rows, d_rows, slot_gate, w_gate_up, w_down)


def core_swap(value, groups):
    return lax.ppermute(value, "expert", [(m, m ^ 1) for m in range(groups)])


def from_row(value, groups, shift):
    count = groups // 2
    pairs = [((((y + shift) % count) * 2 + c), y * 2 + c) for y in range(count) for c in range(2)]
    return lax.ppermute(value, "expert", pairs)


def to_row(value, groups, shift):
    count = groups // 2
    pairs = [(y * 2 + c, ((y + shift) % count) * 2 + c) for y in range(count) for c in range(2)]
    return lax.ppermute(value, "expert", pairs)


def after(value, *others):
    return lax.optimization_barrier((value,) + others)[0]


def gather_column(value, groups):
    return [value] + [from_row(value, groups, s) for s in range(1, groups // 2)]


def gather_cores(column, groups, *before):
    result = [column[0], core_swap(column[0], groups)]
    for piece in column[1:]:
        piece = after(piece, *before)
        result += [piece, core_swap(piece, groups)]
    return result


def gather_members(value, groups):
    return gather_cores(gather_column(value, groups), groups)


def return_members(pieces, groups, *before):
    swapped = [core_swap(pieces[2 * s + 1], groups) for s in range(groups // 2)]
    terms, sent = [pieces[0], swapped[0]], []
    for s in range(1, groups // 2):
        mine = after(pieces[2 * s], *before)
        both = (mine.astype(f32) + swapped[s].astype(f32)).astype(bf16)
        sent.append(both)
        terms.append(to_row(both, groups, s))
    return terms, sent


def exchange_members(pieces, groups):
    count = groups // 2
    result = []
    for s in range(count):
        for c in range(2):
            if s == 0 and c == 0:
                result.append(pieces[0])
                continue
            pairs = [
                (((y - s) % count) * 2 + (core ^ c), y * 2 + core)
                for y in range(count)
                for core in range(2)
            ]
            result.append(lax.ppermute(pieces[2 * s + c], "expert", pairs))
    return result


def lane(shape):
    return lax.broadcasted_iota(jnp.int32, shape, len(shape) - 1)


def turn(value, cosine, sine, sign):
    first = lax.rem(lane(value.shape), HEAD_DIM) < HEAD_DIM // 2
    other = jnp.where(
        first, pltpu.roll(value, 128 - HEAD_DIM // 2, 1), pltpu.roll(value, HEAD_DIM // 2, 1)
    )
    return value * cosine + sign * other * sine


def project_body(x_ref, gain_ref, w_ref, cos_ref, sin_ref, normed_ref, q_ref, kv_ref):
    x = x_ref[0].astype(f32)
    scale = lax.rsqrt(jnp.mean(x * x, axis=1, keepdims=True) + epsilon)
    normed = (x * scale * gain_ref[...]).astype(bf16)
    normed_ref[0] = normed
    cosine, sine = cos_ref[...], sin_ref[...]
    q_width, k_width = HEADS * HEAD_DIM, KV_HEADS * HEAD_DIM
    for start in range(0, q_width + 2 * k_width, 512):
        part = mm(normed, w_ref[:, start : start + 512], ((1,), (0,)))
        for inner in range(0, 512, 128):
            at = start + inner
            value = part[:, inner : inner + 128]
            if at < q_width:
                q_ref[0, :, at : at + 128] = turn(value, cosine, sine, 1.0).astype(bf16)
            elif at < q_width + k_width:
                at -= q_width
                kv_ref[0, :, at : at + 128] = turn(value, cosine, sine, 1.0).astype(bf16)
            else:
                at -= q_width
                kv_ref[0, :, at : at + 128] = value.astype(bf16)


def project(tokens, gain, w_qkv, cosine, sine):
    micro, rows, _ = tokens.shape
    block = pl.BlockSpec((1, rows, D), lambda m: (m, 0, 0))
    table = pl.BlockSpec((rows, 128), lambda m: (0, 0))
    shape = jax.ShapeDtypeStruct((micro, rows, D), bf16)
    return pl.pallas_call(
        project_body,
        grid=(micro,),
        in_specs=[
            block,
            pl.BlockSpec((1, D), lambda m: (0, 0)),
            pl.BlockSpec(w_qkv.shape, lambda m: (0, 0)),
            table,
            table,
        ],
        out_specs=[block, block, block],
        out_shape=[shape, shape, shape],
        cost_estimate=cost(7),
        compiler_params=params(),
    )(tokens, gain, w_qkv, cosine, sine)


def stack_heads(block, scale):
    wide = block.astype(f32) * scale
    result = []
    for p in range(2):
        part = wide[:, p * 128 : (p + 1) * 128]
        half = (lane(part.shape) >= HEAD_DIM) == (p == 1)
        for h in range(2):
            moved = part if h == p else pltpu.roll(part, HEAD_DIM, 1)
            result.append(jnp.where(half, moved, 0.0).astype(bf16))
    return jnp.concatenate(result, axis=0)


def unstack_heads(stacked, rows):
    result = []
    for p in range(2):
        pieces = []
        for h in range(2):
            i = 2 * p + h
            part = stacked[i * rows : (i + 1) * rows]
            pieces.append(part if h == p else pltpu.roll(part, HEAD_DIM, 1))
        result.append(jnp.where(lane(pieces[0].shape) < HEAD_DIM, pieces[0], pieces[1]))
    return result


def attend_body(
    q_ref, pk_ref, pv_ref, ok_ref, ov_ref, bias_ref, x_ref, w_ref, gain_ref,
    att_ref, lse_ref, hidden_ref, low_ref, all_ref,
):
    j = pl.program_id(0)
    rows = q_ref.shape[1]
    q = stack_heads(q_ref[0], score_scale)
    k = jnp.concatenate([pk_ref[0], ok_ref[0, PROMPT_DEV:, :]], axis=0)
    v = jnp.concatenate([pv_ref[0], ov_ref[0, PROMPT_DEV:, :]], axis=0)
    scores = mm(k, q, ((1,), (1,))) + bias_ref[...]
    largest = jnp.max(scores, axis=0, keepdims=True)
    raised = jnp.exp(scores - largest)
    total = jnp.sum(raised, axis=0, keepdims=True)
    weights = (raised * (1.0 / total)).astype(bf16)
    lse_ref[0] = largest + jnp.log(total)
    mixed = mm(v, weights, ((0,), (0,))).T
    for p, part in enumerate(unstack_heads(mixed, rows)):
        at = pl.multiple_of(j * 256 + p * 128, 128)
        att_ref[0, :, p * 128 : (p + 1) * 128] = part.astype(bf16)
        all_ref[:, pl.ds(at, 128)] = part.astype(bf16)

    @pl.when(j == pl.num_programs(0) - 1)
    def _():
        branch = mm(all_ref[...], w_ref[...], ((1,), (0,)))
        hidden = x_ref[0].astype(f32) + branch_scale * branch
        hidden_ref[0] = hidden
        scale = lax.rsqrt(jnp.mean(hidden * hidden, axis=1, keepdims=True) + epsilon)
        low_ref[0] = (hidden * scale * gain_ref[...]).astype(bf16)


def attend(micro, q, kv, prompt, bias, tokens, w_out, gain):
    rows, prompt_rows = q.shape[1], prompt.shape[1]
    steps = KV_HEADS // 2
    full = pl.BlockSpec((1, rows, D), lambda j: (micro, 0, 0))
    one = pl.BlockSpec((1, rows, D), lambda j: (0, 0, 0))
    return pl.pallas_call(
        attend_body,
        grid=(steps,),
        in_specs=[
            pl.BlockSpec((1, rows, 256), lambda j: (micro, 0, j)),
            pl.BlockSpec((1, prompt_rows, 128), lambda j: (micro, 0, j)),
            pl.BlockSpec((1, prompt_rows, 128), lambda j: (micro, 0, j + steps)),
            pl.BlockSpec((1, rows, 128), lambda j: (micro, 0, j)),
            pl.BlockSpec((1, rows, 128), lambda j: (micro, 0, j + steps)),
            pl.BlockSpec(bias.shape, lambda j: (0, 0)),
            full,
            pl.BlockSpec(w_out.shape, lambda j: (0, 0)),
            pl.BlockSpec((1, D), lambda j: (0, 0)),
        ],
        out_specs=[
            pl.BlockSpec((1, rows, 256), lambda j: (0, 0, j)),
            pl.BlockSpec((1, 1, 4 * rows), lambda j: (j, 0, 0)),
            one,
            one,
        ],
        out_shape=[
            jax.ShapeDtypeStruct((1, rows, D), bf16),
            jax.ShapeDtypeStruct((steps, 1, 4 * rows), f32),
            jax.ShapeDtypeStruct((1, rows, D), f32),
            jax.ShapeDtypeStruct((1, rows, D), bf16),
        ],
        scratch_shapes=[pltpu.VMEM((rows, D), bf16)],
        cost_estimate=cost(12),
        compiler_params=params(),
    )(q, prompt, prompt, kv, kv, bias, tokens, w_out, gain)


def norm_back(value, gain, grad):
    scale = lax.rsqrt(jnp.mean(value * value, axis=1, keepdims=True) + epsilon)
    scaled = grad * gain
    inner = jnp.mean(scaled * value, axis=1, keepdims=True)
    back = scale * scaled - value * (scale * scale * scale * inner)
    return back, jnp.sum(grad * value * scale, axis=0, keepdims=True)


def middle_body(*refs, terms):
    term_refs = refs[:terms]
    (logit_ref, router_ref, hidden_ref, gain_ref, cot_ref, w_ref) = refs[terms : terms + 6]
    grad_hidden_ref, branch_ref, att_ref, gain_out_ref = refs[terms + 6 :]
    total = mm(logit_ref[0], router_ref[...], ((0,), (1,)))
    for ref in term_refs:
        total = total + ref[0].astype(f32)
    back, gain_grad = norm_back(hidden_ref[0], gain_ref[...], total)
    grad_hidden = cot_ref[0].astype(f32) + back
    grad_hidden_ref[0] = grad_hidden
    branch = (branch_scale * grad_hidden).astype(bf16)
    branch_ref[0] = branch
    att_ref[0] = mm(branch, w_ref[...], ((1,), (1,))).astype(bf16)

    @pl.when(pl.program_id(0) == 0)
    def _():
        gain_out_ref[...] = gain_grad

    @pl.when(pl.program_id(0) != 0)
    def _():
        gain_out_ref[...] += gain_grad


def middle_back(terms, grad_logits, w_router, hidden, gain, cotangent, w_out):
    micro, rows, _ = hidden.shape
    block = pl.BlockSpec((1, rows, D), lambda m: (m, 0, 0))
    row = pl.BlockSpec((1, D), lambda m: (0, 0))
    return pl.pallas_call(
        functools.partial(middle_body, terms=len(terms)),
        grid=(micro,),
        in_specs=[block] * len(terms)
        + [
            pl.BlockSpec((1, EXPERTS, rows), lambda m: (m, 0, 0)),
            pl.BlockSpec(w_router.shape, lambda m: (0, 0)),
            block,
            row,
            block,
            pl.BlockSpec(w_out.shape, lambda m: (0, 0)),
        ],
        out_specs=[block, block, block, row],
        out_shape=[
            jax.ShapeDtypeStruct((micro, rows, D), f32),
            jax.ShapeDtypeStruct((micro, rows, D), bf16),
            jax.ShapeDtypeStruct((micro, rows, D), bf16),
            jax.ShapeDtypeStruct((1, D), f32),
        ],
        cost_estimate=cost(8),
        compiler_params=params(),
    )(*terms, grad_logits, w_router, hidden, gain, cotangent, w_out)


def attend_back_body(
    q_ref, pk_ref, pv_ref, ok_ref, ov_ref, bias_ref, lse_ref, grad_ref, cos_ref, sin_ref,
    gq_ref, gpk_ref, gpv_ref, gok_ref, gov_ref,
):
    rows, prompt_rows = q_ref.shape[1], pk_ref.shape[1]
    q = stack_heads(q_ref[0], score_scale)
    grad = stack_heads(grad_ref[0], 1.0)
    k = jnp.concatenate([pk_ref[0], ok_ref[0, PROMPT_DEV:, :]], axis=0)
    v = jnp.concatenate([pv_ref[0], ov_ref[0, PROMPT_DEV:, :]], axis=0)
    probs = jnp.exp(mm(k, q, ((1,), (1,))) + bias_ref[...] - lse_ref[0, 0])
    grad_probs = mm(v, grad, ((1,), (1,)))
    centre = jnp.sum(probs * grad_probs, axis=0, keepdims=True)
    grad_scores = (probs * (grad_probs - centre)).astype(bf16)
    grad_v = mm(probs.astype(bf16), grad, ((1,), (0,)))
    grad_k = mm(grad_scores, q, ((1,), (0,)))
    grad_q = mm(k, grad_scores, ((0,), (0,))).T * score_scale
    cosine, sine = cos_ref[...], sin_ref[...]
    for p, part in enumerate(unstack_heads(grad_q, rows)):
        gq_ref[0, :, p * 128 : (p + 1) * 128] = turn(part, cosine, sine, -1.0).astype(bf16)
    gpk_ref[0] = grad_k[:prompt_rows].astype(bf16)
    gpv_ref[0] = grad_v[:prompt_rows].astype(bf16)
    gok_ref[0] = turn(
        grad_k[prompt_rows:], cosine[PROMPT_DEV:], sine[PROMPT_DEV:], -1.0
    ).astype(bf16)
    gov_ref[0] = grad_v[prompt_rows:].astype(bf16)


def attend_back(q, kv, prompt, bias, lse, grad, cosine, sine):
    micro, rows, _ = q.shape
    prompt_rows = prompt.shape[1]
    own_rows = rows - PROMPT_DEV
    steps = KV_HEADS // 2
    wide = pl.BlockSpec((1, rows, 256), lambda m, j: (m, 0, j))
    table = pl.BlockSpec((rows, 128), lambda m, j: (0, 0))
    prompt_spec = pl.BlockSpec((1, prompt_rows, 128), lambda m, j: (m, 0, j))
    own_spec = pl.BlockSpec((1, own_rows, 128), lambda m, j: (m, 0, j))
    k_width = KV_HEADS * HEAD_DIM
    return pl.pallas_call(
        attend_back_body,
        grid=(micro, steps),
        in_specs=[
            wide,
            prompt_spec,
            pl.BlockSpec((1, prompt_rows, 128), lambda m, j: (m, 0, j + steps)),
            pl.BlockSpec((1, rows, 128), lambda m, j: (m, 0, j)),
            pl.BlockSpec((1, rows, 128), lambda m, j: (m, 0, j + steps)),
            pl.BlockSpec(bias.shape, lambda m, j: (0, 0)),
            pl.BlockSpec((1, 1, 1, 4 * rows), lambda m, j: (m, j, 0, 0)),
            wide,
            table,
            table,
        ],
        out_specs=[wide, prompt_spec, prompt_spec, own_spec, own_spec],
        out_shape=[
            jax.ShapeDtypeStruct((micro, rows, D), bf16),
            jax.ShapeDtypeStruct((micro, prompt_rows, k_width), bf16),
            jax.ShapeDtypeStruct((micro, prompt_rows, k_width), bf16),
            jax.ShapeDtypeStruct((micro, own_rows, k_width), bf16),
            jax.ShapeDtypeStruct((micro, own_rows, k_width), bf16),
        ],
        cost_estimate=cost(23),
        compiler_params=pltpu.CompilerParams(
            vmem_limit_bytes=vmem_limit, dimension_semantics=("arbitrary", "arbitrary")
        ),
    )(q, prompt, prompt, kv, kv, bias, lse, grad, cosine, sine)


def weight_body(*refs, terms):
    normed_ref, gq_ref, gok_ref, gov_ref = refs[:4]
    k_terms, v_terms = refs[4 : 4 + terms], refs[4 + terms : 4 + 2 * terms]
    cos_ref, sin_ref, gp_ref, out_ref, acc_ref = refs[4 + 2 * terms :]
    q_width, k_width = HEADS * HEAD_DIM, KV_HEADS * HEAD_DIM
    gp_ref[0, :, :q_width] = gq_ref[0]
    gp_ref[0, PROMPT_DEV:, q_width : q_width + k_width] = gok_ref[0]
    gp_ref[0, PROMPT_DEV:, q_width + k_width :] = gov_ref[0]
    prompt_k, prompt_v = [sum(ref[0].astype(f32) for ref in group) for group in (k_terms, v_terms)]
    cosine, sine = cos_ref[:PROMPT_DEV, :], sin_ref[:PROMPT_DEV, :]
    for at in range(0, k_width, 128):
        turned = turn(prompt_k[:, at : at + 128], cosine, sine, -1.0)
        gp_ref[0, :PROMPT_DEV, q_width + at : q_width + at + 128] = turned.astype(bf16)
    gp_ref[0, :PROMPT_DEV, q_width + k_width :] = prompt_v.astype(bf16)
    part = mm(normed_ref[0], gp_ref[0], ((0,), (0,)))
    m = pl.program_id(0)

    @pl.when(m == 0)
    def _():
        acc_ref[...] = part

    @pl.when(m != 0)
    def _():
        acc_ref[...] += part

    @pl.when(m == pl.num_programs(0) - 1)
    def _():
        out_ref[...] = acc_ref[...].astype(bf16)


def weight_back(normed, gq, gok, gov, k_terms, v_terms, cosine, sine):
    micro, rows, _ = normed.shape
    k_width = KV_HEADS * HEAD_DIM
    wide = pl.BlockSpec((1, rows, D), lambda m: (m, 0, 0))
    own = pl.BlockSpec((1, rows - PROMPT_DEV, k_width), lambda m: (m, 0, 0))
    term = pl.BlockSpec((1, PROMPT_DEV, k_width), lambda m: (m, 0, 0))
    table = pl.BlockSpec((rows, 128), lambda m: (0, 0))
    return pl.pallas_call(
        functools.partial(weight_body, terms=len(k_terms)),
        grid=(micro,),
        in_specs=[wide, wide, own, own] + [term] * (2 * len(k_terms)) + [table, table],
        out_specs=[
            pl.BlockSpec((1, rows, 2 * D), lambda m: (m, 0, 0)),
            pl.BlockSpec((D, 2 * D), lambda m: (0, 0)),
        ],
        out_shape=[
            jax.ShapeDtypeStruct((micro, rows, 2 * D), bf16),
            jax.ShapeDtypeStruct((D, 2 * D), bf16),
        ],
        scratch_shapes=[pltpu.VMEM((D, 2 * D), f32)],
        cost_estimate=cost(11),
        compiler_params=params(),
    )(normed, gq, gok, gov, *k_terms, *v_terms, cosine, sine)


def token_body(gp_ref, w_ref, x_ref, gain_ref, hidden_ref, out_ref, gain_out_ref):
    grad = mm(gp_ref[0], w_ref[...], ((1,), (1,)))
    back, gain_grad = norm_back(x_ref[0].astype(f32), gain_ref[...], grad)
    out_ref[0] = (hidden_ref[0] + back).astype(bf16)

    @pl.when(pl.program_id(0) == 0)
    def _():
        gain_out_ref[...] = gain_grad

    @pl.when(pl.program_id(0) != 0)
    def _():
        gain_out_ref[...] += gain_grad


def token_back(gp, w_qkv, tokens, gain, grad_hidden):
    micro, rows, _ = tokens.shape
    block = pl.BlockSpec((1, rows, D), lambda m: (m, 0, 0))
    row = pl.BlockSpec((1, D), lambda m: (0, 0))
    return pl.pallas_call(
        token_body,
        grid=(micro,),
        in_specs=[
            pl.BlockSpec((1, rows, 2 * D), lambda m: (m, 0, 0)),
            pl.BlockSpec(w_qkv.shape, lambda m: (0, 0)),
            block,
            row,
            block,
        ],
        out_specs=[block, row],
        out_shape=[
            jax.ShapeDtypeStruct((micro, rows, D), bf16),
            jax.ShapeDtypeStruct((1, D), f32),
        ],
        cost_estimate=cost(8),
        compiler_params=params(),
    )(gp, w_qkv, tokens, gain, grad_hidden)


def halve(value, axis, swap, bit, *before):
    rows = value.shape[0] // 2
    keep = lax.dynamic_slice_in_dim(value, bit * rows, rows, 0)
    send = lax.dynamic_slice_in_dim(value, (1 - bit) * rows, rows, 0)
    got = after(lax.ppermute(send, axis, swap), *before)
    return (keep.astype(f32) + got.astype(f32)).astype(bf16)


def finish_dense_body(table_ref, *refs, pieces):
    first_refs, second_refs = refs[:pieces], refs[pieces : 2 * pieces]
    qkv_ref, out_ref = refs[2 * pieces :]
    width = first_refs[0].shape[1]
    rest = qkv_ref.shape[1] - width
    for i in range(pieces):

        @pl.when(pl.program_id(0) == i)
        def _(i=i):
            qkv_ref[:, :width] = first_refs[i][...].astype(f32)
            qkv_ref[:, width:] = second_refs[i][:, :rest].astype(f32)
            out_ref[...] = second_refs[i][:, rest:].astype(f32)


def finish_dense(table, first, second):
    pieces = len(first)
    height = first[0].shape[0]
    grid_spec = pltpu.PrefetchScalarGridSpec(
        num_scalar_prefetch=1,
        grid=(pieces,),
        in_specs=[full_spec(piece) for piece in first + second],
        out_specs=[
            pl.BlockSpec((height, 2 * D), lambda i, t: (t[i], 0)),
            pl.BlockSpec((height, D), lambda i, t: (t[i], 0)),
        ],
    )
    return pl.pallas_call(
        functools.partial(finish_dense_body, pieces=pieces),
        grid_spec=grid_spec,
        out_shape=[
            jax.ShapeDtypeStruct((pieces * height, 2 * D), f32),
            jax.ShapeDtypeStruct((pieces * height, D), f32),
        ],
        cost_estimate=cost(9),
        compiler_params=params(),
    )(table, *first, *second)


def local(
    tokens, cotangent, expert_ids, norm_attn, w_qkv, w_out, norm_moe, w_router, w_gate_up, w_down
):
    groups = lax.axis_size("expert")
    dp_size = lax.axis_size("dp")
    member = lax.axis_index("expert")
    dp_index = lax.axis_index("dp")
    rows_all = tokens.shape[0]
    tok_rows = rows_all // MICRO
    local_experts = w_gate_up.shape[0]
    prompt_len = PROMPT_DEV * groups
    k_width = KV_HEADS * HEAD_DIM
    pairs = dp_size // 2
    blocks = groups * MICRO
    attn_gain = norm_attn.reshape(1, D)
    moe_gain = norm_moe.reshape(1, D)
    token_rows = tokens.reshape(MICRO, tok_rows, D)
    cot_rows = cotangent.reshape(MICRO, tok_rows, D)

    local_index = jnp.arange(tok_rows, dtype=jnp.int32)
    positions = jnp.where(
        local_index < PROMPT_DEV,
        member * PROMPT_DEV + local_index,
        prompt_len + local_index - PROMPT_DEV,
    )
    half_dim = HEAD_DIM // 2
    inverse = 10000.0 ** (-2.0 * jnp.arange(half_dim, dtype=f32) / HEAD_DIM)
    angles = positions.astype(f32)[:, None] * inverse[None, :]
    cosine = jnp.tile(jnp.cos(angles), (1, 128 // half_dim))
    sine = jnp.tile(jnp.sin(angles), (1, 128 // half_dim))
    sine = jnp.where(jnp.arange(128)[None, :] % HEAD_DIM < half_dim, -sine, sine)
    rows_of = []
    for s in range(groups // 2):
        for c in range(2):
            place = lax.rem(member // 2 + s, groups // 2) * 2 + lax.rem(member + c, 2)
            rows_of.append(place * PROMPT_DEV + jnp.arange(PROMPT_DEV, dtype=jnp.int32))
    key_positions = jnp.concatenate(
        rows_of + [prompt_len + jnp.arange(tok_rows - PROMPT_DEV, dtype=jnp.int32)]
    )
    bias = jnp.where(
        key_positions[:, None] <= jnp.tile(positions, HEADS // (KV_HEADS // 2))[None, :],
        0.0,
        masked_score,
    )

    first_expert = member * local_experts
    ids_t = gather_members(expert_ids.reshape(MICRO, tok_rows, TOP).transpose(0, 2, 1), groups)
    ids_all = lax.rem(jnp.concatenate(ids_t, axis=0) + (EXPERTS - first_expert), EXPERTS)
    cot_pieces = [gather_members(cot_rows[:1], groups)]
    normed, queries, key_value = project(token_rows, attn_gain, w_qkv, cosine, sine)
    prompt_pieces = gather_members(
        after(key_value[:, :PROMPT_DEV], cot_pieces[0][2]), groups
    )
    prompt = jnp.concatenate(prompt_pieces, axis=1)
    cot_pieces += [
        gather_members(after(cot_rows[m : m + 1], prompt_pieces[2]), groups)
        for m in range(1, MICRO)
    ]
    router = lax.dynamic_slice_in_dim(
        jnp.concatenate([w_router, w_router], axis=1), first_expert, EXPERTS, 1
    )

    attended, lse, hidden, moe_pieces, moe_low = [], [], [], [], []
    for m in range(MICRO):
        mask = bias if m == 0 else after(bias, moe_low[-1])
        att, log_total, hid, low = attend(
            m, queries, key_value, prompt, mask, token_rows, w_out, moe_gain
        )
        attended.append(att)
        lse.append(log_total[None])
        hidden.append(hid)
        moe_low.append(low)
        moe_pieces.append(gather_column(low, groups))

    def by_block(pieces):
        return [pieces[m][g] for g in range(groups) for m in range(MICRO)]

    d_rows, slots = pick_grads(after(ids_all, moe_low[-1]), by_block(cot_pieces), local_experts)
    moe_pieces = [gather_cores(column, groups, slots) for column in moe_pieces]
    attended = jnp.concatenate(attended, axis=0)
    lse = jnp.concatenate(lse, axis=0)
    hidden = jnp.concatenate(hidden, axis=0)
    moe_low = jnp.concatenate(moe_low, axis=0)

    x_rows, slot_gate, gates = pick_tokens(ids_all, slots, router, by_block(moe_pieces))
    slot_rows = blocks * SLOTS
    x_rows = x_rows.reshape(local_experts, slot_rows, D)
    d_rows = d_rows.reshape(local_experts, slot_rows, D)
    slot_gate = slot_gate.reshape(local_experts, slot_rows, 128)
    parity = lax.rem(dp_index, 2).astype(jnp.int32)
    swap_x = [(d, d ^ 1) for d in range(dp_size)]
    swap_y = [(m, m ^ 2) for m in range(groups)]
    swap_core = [(m, m ^ 1) for m in range(groups)]
    z_groups = [[d for d in range(dp_size) if d % 2 == r] for r in range(2)]
    piece = (D + FF) // (2 * pairs)

    def sum_z(value):
        count, _, height, _ = value.shape
        return lax.psum_scatter(
            value.reshape(count, pairs * height, D),
            "dp",
            scatter_dimension=1,
            axis_index_groups=z_groups,
            tiled=True,
        )

    plan = CHUNKS
    if sum(count for count, _ in plan) != local_experts:
        plan = tuple((1, e == 0) for e in range(local_experts))
    outs, backs, dots, halves, parts = [], [], [], {}, {}

    held = {}

    def add_x(i, *before, hold=False):
        keep, got = halves.pop(i)
        got = after(got, *before)
        half = (keep.astype(f32) + got.astype(f32)).astype(bf16)
        if hold:
            held[i] = half
        else:
            parts[i] = sum_z(half)
        return half

    first = 0
    order = parity.reshape(1)
    for i, (count, whole) in enumerate(plan):
        if i:
            order = after(order, outs[-1])
        if i == 3:
            order = after(order, add_x(1, outs[-1]))
        if i == 4:
            order = after(order, parts[0])
        out, back, dot, *sums = expert_chunk(
            order, first, count, pairs, not whole, x_rows, d_rows, slot_gate, w_gate_up, w_down
        )
        shape = (count, blocks, SLOTS)
        outs.append(out.reshape(shape + (D,)))
        backs.append(back.reshape(shape + (D,)))
        dots.append(dot.reshape(shape + (128,)))
        if whole:
            parts[i] = sum_z(sums[0])
        else:
            halves[i] = (sums[0], lax.ppermute(sums[1], "dp", swap_x))
        first += count

    def left(i, *before, hold=False):
        return [add_x(i, *before, hold=hold)] if i in halves else []

    def sent(i):
        return [parts[i]] if i in parts else []

    *back_sum, back_dots = sum_rows(slots, backs, dots)

    def pieces_of(value):
        return [value[j * MICRO : (j + 1) * MICRO] for j in range(groups)]

    dot_pieces = exchange_members(pieces_of(back_dots), groups)
    back_terms, back_sent = return_members(back_sum, groups, *dot_pieces)
    token_dots = jnp.zeros((MICRO, EXPERTS, tok_rows), f32)
    for s in range(groups // 2):
        for c in range(2):
            place = lax.rem(member // 2 + groups // 2 - s, groups // 2) * 2 + lax.rem(
                member + c, 2
            )
            label = lax.rem(place + groups - member, groups) * local_experts
            token_dots = lax.dynamic_update_slice_in_dim(
                token_dots, dot_pieces[2 * s + c], label, 1
            )
    own_gates = gates[:MICRO]
    centre = jnp.sum(own_gates * token_dots, axis=1, keepdims=True)
    grad_logits = (own_gates * (token_dots - centre)).astype(bf16)
    mixed = sum_rows(
        after(slots, *back_sent, *sent(1), *left(2, back_sum[0], hold=True)), outs
    )
    mix_terms, _ = return_members(mixed, groups)

    grad_hidden, grad_branch, grad_attended, grad_norm_moe = middle_back(
        back_terms, grad_logits, router, hidden, moe_gain, after(cot_rows, *mixed, *sent(4)), w_out
    )
    grad_router = jnp.einsum("bet,btd->ed", grad_logits, moe_low, preferred_element_type=f32)
    grad_out = jnp.einsum(
        "brd,bre->de", attended, grad_branch, preferred_element_type=f32
    ).astype(bf16)
    core_bit, row_bit = lax.rem(member, 2), lax.rem(member // 2, 2)
    grad_out = halve(grad_out, "expert", swap_core, core_bit)
    gq, gpk, gpv, gok, gov = attend_back(
        queries,
        key_value,
        prompt,
        after(bias, grad_out, *left(3, grad_branch)),
        lse,
        grad_attended,
        cosine,
        sine,
    )

    for i in list(held):
        parts[i] = sum_z(after(held.pop(i), gq))

    def prompt_terms(value):
        return return_members(
            [value[:, j * PROMPT_DEV : (j + 1) * PROMPT_DEV] for j in range(groups)], groups
        )[0]

    mixture = sum(after(term, gq).astype(f32) for term in mix_terms)
    output = (hidden + branch_scale * mixture).astype(bf16)
    k_terms, v_terms = prompt_terms(gpk), prompt_terms(gpv)
    grad_out = halve(after(grad_out, k_terms[2], v_terms[2]), "expert", swap_y, row_bit)
    gp, grad_qkv = weight_back(
        after(normed, *mix_terms[2:], *left(5, gq, hold=True)),
        gq,
        gok,
        gov,
        k_terms,
        v_terms,
        cosine,
        sine,
    )
    grad_tokens, grad_norm_attn = token_back(
        after(gp, grad_qkv, output), w_qkv, token_rows, attn_gain, grad_hidden
    )
    last = [add_x(i, grad_norm_attn) for i in list(halves)]
    grad_qkv = halve(after(grad_qkv, grad_out), "expert", swap_core, core_bit)

    whole_sums = [parts[i] for i, (_, whole) in enumerate(plan) if whole]
    whole_sums = jnp.concatenate(whole_sums, axis=0)
    swapped = lax.ppermute(after(whole_sums[:, piece:], *last), "dp", swap_x)
    whole_sums = (whole_sums[:, :piece].astype(f32) + swapped.astype(f32)).astype(bf16)
    pieces, at = [], 0
    for i, (count, whole) in enumerate(plan):
        pieces.append(whole_sums[at : at + count] if whole else parts.get(i))
        at += count if whole else 0

    small = jnp.concatenate(
        [
            lax.dynamic_slice_in_dim(
                jnp.concatenate([grad_router, grad_router], axis=0),
                EXPERTS - first_expert,
                EXPERTS,
                0,
            ),
            grad_norm_attn,
            grad_norm_moe,
            jnp.zeros((14, D), f32),
        ],
        axis=0,
    )
    small = after(small, *last)
    for axis, swap in (("expert", swap_core), ("dp", swap_x)):
        small = small + lax.ppermute(small, axis, swap)
    grad_qkv = halve(grad_qkv, "expert", swap_y, row_bit, small)
    small = small + lax.ppermute(small, "expert", swap_y)
    dense = jnp.concatenate([grad_qkv, grad_out], axis=1)
    dense = after(halve(dense, "dp", swap_x, parity), *sent(2), *sent(3))
    for i in list(held):
        parts[i] = sum_z(after(held.pop(i), dense))
        pieces[i] = parts[i]
    dense_rows = dense.shape[0]
    dense = jnp.concatenate([dense, small.reshape(-1, 3 * D).astype(bf16)], axis=0)
    dense = lax.psum(dense, "dp", axis_index_groups=z_groups)
    if groups > 4:
        rest = [[m for m in range(groups) if m % 4 == r] for r in range(4)]
        dense = lax.psum(dense, "expert", axis_index_groups=rest)
    small = dense[dense_rows:].reshape(-1, D).astype(f32)
    dense = dense[:dense_rows]
    width = dense.shape[1] // 2
    left_own, right_own = dense[:, :width], dense[:, width:]
    left_x = lax.ppermute(left_own, "dp", swap_x)
    right_y = lax.ppermute(right_own, "expert", swap_y)
    left_four = [left_own, left_x] + [
        lax.ppermute(value, "expert", swap_y) for value in (left_own, left_x)
    ]
    right_x = [lax.ppermute(value, "dp", swap_x) for value in (right_own, right_y)]
    right_four = [right_own, right_x[0], right_y, right_x[1]]
    if 5 in parts:
        pieces[5] = after(pieces[5], left_four[3], right_four[3])
    left_all = left_four + [core_swap(value, groups) for value in left_four]
    right_all = right_four + [core_swap(value, groups) for value in right_four]
    base = core_bit * 4 + row_bit * 2 + parity
    table = jnp.bitwise_xor(base, jnp.arange(8, dtype=jnp.int32)).astype(jnp.int32)
    full_qkv, full_out = finish_dense(table, left_all, right_all)

    experts_sum = jnp.concatenate(pieces, axis=0).astype(f32)
    gu_piece = D // (2 * pairs)
    return (
        output.reshape(rows_all, D),
        grad_tokens.reshape(rows_all, D),
        small[EXPERTS],
        full_qkv,
        full_out,
        small[EXPERTS + 1],
        small[:EXPERTS].T,
        experts_sum[:, :gu_piece],
        experts_sum[:, gu_piece:],
    )


def solution(mesh):
    in_specs = (
        P(("dp", "expert"), None),
        P(("dp", "expert"), None),
        P(("dp", "expert"), None),
        P(),
        P(),
        P(),
        P(),
        P(),
        P("expert", None, None),
        P("expert", None, None),
    )
    out_specs = (
        P(("dp", "expert"), None),
        P(("dp", "expert"), None),
        P(),
        P(),
        P(),
        P(),
        P(),
        P("expert", "dp", None),
        P("expert", "dp", None),
    )
    return jax.shard_map(local, mesh=mesh, in_specs=in_specs, out_specs=out_specs, check_vma=False)
```
